32 devices in a mesh: ctx: 8 (over z, y), head: 4 (over x, core).
Axes of the slice: x: 2, y: 2, z: 4, core: 2. Of those that a mesh axis runs over, the one named last changes fastest.
Arguments:
- query: bfloat16 [2048, 4096], P('ctx', 'head'), may hold values from -6 to 6
- key: bfloat16 [2048, 4096], P('ctx', 'head'), may hold values from -6 to 6
- value: bfloat16 [2048, 4096], P('ctx', 'head'), may hold values from -6 to 6
- episode_lengths: int32 [8], replicated, may hold values from 1 to 1024, 2048 in all
- attn_gain: float32 [4096], P('head'), may hold values from 0.1 to 1.9
- out_weight: bfloat16 [4096, 3072], P('head', 'ctx'), may hold values from -0.09375 to 0.09375
- residual: bfloat16 [2048, 3072], P('ctx', 'head'), may hold values from -36 to 36
- norm_gain: float32 [3072], P('head'), may hold values from 0.1 to 1.9
- expert_ids: int32 [2048, 2], P('ctx'), may hold values from 0 to 7, all different within a row; in each aligned block of 256 rows (0 to 255, 256 to 511, ...) at most 96 rows name the same one
- route_weights: int32 [2048, 2], P('ctx'), may hold values from 4096 to 65535
- gate_weight: bfloat16 [8, 3072, 5120], P('ctx', None, 'head'), may hold values from -0.109375 to 0.109375
- up_weight: bfloat16 [8, 3072, 5120], P('ctx', None, 'head'), may hold values from -0.109375 to 0.109375
- down_weight: bfloat16 [8, 5120, 3072], P('ctx', 'head'), may hold values from -0.125 to 0.125
Outputs:
- layer_out: bfloat16 [2048, 3072], P('ctx', 'head')
The draws below stay inside these ranges and needn't reach their ends.
Inputs may be any that keep to these rules, and one draw needn't show every extreme that they name: `expert_ids`: in the rows of one device (256 tokens) no expert is named by more than 96 rows, a bound that some block reaches; a row names two different experts.
All inputs are finite; a program needn't handle non-finite values.
Results may differ from the reference program's by a relative error of at most 0.012.
Values may be sent and summed in bfloat16 or wider, within the bound.
A program may use at most 128 MiB of HBM per device.

```python
import math
import jax
import jax.numpy as jnp
import numpy as np
from jax import lax

D = 3072
HEADS = 32
HEAD_DIM = 128
FF = 5120
TOK_DEV = 256
EPISODES = 8
HQ = 4096
EXPERTS = 8
TOKENS = 2048
CAP = 96
N_HEAD = 4


def draw_residual(key, part):
    first, second, third = jax.random.split(key, 3)
    base = jnp.clip(jax.random.normal(first, (TOKENS, D), jnp.float32), -4.0, 4.0)
    rows = jnp.exp(jax.random.uniform(second, (TOKENS, 1), jnp.float32, math.log(0.3), math.log(3.0)))
    columns = jnp.exp(jax.random.uniform(third, (1, D), jnp.float32, math.log(0.3), math.log(3.0)))
    return (base * rows * columns).astype(jnp.bfloat16)


def set_ends(entries, own_key, least, top_value):
    index_at = [jax.random.randint(jax.random.fold_in(own_key, axis), (), 0, length) for axis, length in enumerate(entries.shape)]
    main_axis = entries.shape.index(max(entries.shape))
    neighbour = index_at[:main_axis] + [(index_at[main_axis] + 1) % entries.shape[main_axis]] + index_at[main_axis + 1:]
    return entries.at[tuple(index_at)].set(least).at[tuple(neighbour)].set(top_value)


def with_spikes(result, key, source, target, parts, factor):
    owner, partner = [(jnp.arange(result.shape[axis_at]) // (result.shape[axis_at] // parts)).reshape([-1 if axis == axis_at else 1 for axis in range(result.ndim)]) for axis_at in (source, target)]
    chosen = jax.random.permutation(key, parts)[partner]
    strong = (owner == chosen) | (owner == (partner + parts // 2) % parts)
    return jnp.where(strong, factor * result, result)


def shard_levels(own_key, dims, pieces, low, high):
    level, own = 1.0, jax.random.fold_in(own_key, 6)
    for position, blocks in pieces:
        draws = jnp.exp(jax.random.uniform(jax.random.fold_in(own, position), (blocks,), jnp.float32, low / len(pieces), high / len(pieces)))
        level = level * jnp.repeat(draws, dims[position] // blocks).reshape([-1 if axis == position else 1 for axis in range(len(dims))])
    return level


def length_profile(amount, total, bound, skew):
    portions = [(1 << 20) // math.isqrt(rank ** skew) + 1 for rank in range(2, amount + 1)]
    rest, counts = total - bound - (amount - 1), [1] * (amount - 1)
    while rest > 0:
        candidates = [i for i in range(amount - 1) if counts[i] < bound]
        pool, remaining = sum([portions[i] for i in candidates]), rest
        for i in candidates:
            extra = min(bound - counts[i], max(1, remaining * portions[i] // pool), rest)
            counts[i] = counts[i] + extra
            rest = rest - extra
    return np.array([bound] + counts)


def uneven_parts(key, amount, total, most, lean):
    if amount == 2:
        one = jax.random.randint(key, (), max(1, total - most), min(most, total - 1) + 1)
        return jnp.stack([one, total - one])
    sizes = jnp.asarray(length_profile(amount, total, most, lean), jnp.int32)
    pairs = (amount - 1) // 2
    giver, taker = sizes[1:1 + 2 * pairs:2], sizes[2:2 + 2 * pairs:2]
    slack = jnp.minimum(giver - 1, most - taker)
    passed = jax.random.randint(jax.random.fold_in(key, 1), (pairs,), 0, 1 << 20) % (slack + 1)
    sizes = sizes.at[1:1 + 2 * pairs:2].set(giver - passed).at[2:2 + 2 * pairs:2].set(taker + passed)
    return sizes[jax.random.permutation(jax.random.fold_in(key, 2), amount)]


def routed_block(own_key, own, number, rows, number_of, top, limit, slope):
    sequence = jax.random.permutation(own_key, number_of)
    packed, ordinary = load_shares(number_of, rows * top, limit, slope, True), load_shares(number_of, rows * top, limit, slope, False)
    places = jnp.arange(number_of)

    def named(sizes, turn):
        used = int((sizes > 0).sum())
        fixed = max(1, used // 4)
        moved = fixed + (places - fixed + turn * (used - fixed)) % max(1, number_of - fixed)
        return jnp.zeros((number_of,), jnp.int32).at[sequence[jnp.where(places < fixed, places, moved)]].set(jnp.asarray(sizes, jnp.int32))

    sizes = jnp.where(number % 4 == 0, named(packed, number // 4), named(ordinary, number - number // 4 - 1))
    mixed = jax.random.permutation(jax.random.fold_in(own, 3), number_of)
    donor, taker = mixed[0:number_of // 2 * 2:2], mixed[1:number_of // 2 * 2:2]
    slack = jnp.minimum(sizes[donor] - 1, limit - sizes[taker]) // 2
    slack = jnp.where((donor == sequence[0]) | (taker == sequence[0]) | (sizes[taker] == 0), 0, jnp.maximum(slack, 0))
    moved = jax.random.randint(jax.random.fold_in(own, 4), (number_of // 2,), 0, 1 << 20) % (slack + 1)
    sizes = sizes.at[donor].add(-moved).at[taker].add(moved)
    labels = jnp.searchsorted(jnp.cumsum(sizes), jnp.arange(rows * top), side="right").astype(jnp.int32)
    listing = labels.reshape(top, rows).T
    listing = listing[jax.random.permutation(jax.random.fold_in(own, 1), rows)]
    turn = jax.random.randint(jax.random.fold_in(own, 2), (rows, 1), 0, top)
    return jnp.take_along_axis(listing, (jnp.arange(top)[None, :] + turn) % top, axis=1)


def load_shares(count, total, bound, slope, full):
    loads = [(1 << 20) // math.isqrt(rank ** slope) + 1 for rank in range(1, count + 1)]
    largest = bound if full else min(bound, max(-(-total // count), total * loads[0] // sum(loads)))
    least = 1 if total - largest >= count - 1 else 0
    holding, spare = [largest] + [least] * (count - 1), total - largest - least * (count - 1)
    while spare > 0:
        candidates = [i for i in range(1, count) if holding[i] < largest] or [i for i in range(1, count) if holding[i] < bound]
        pool, budget = sum([loads[i] for i in candidates]), spare
        for i in candidates:
            extra = min(bound - holding[i], max(1, budget * loads[i] // pool), spare)
            holding[i] = holding[i] + extra
            spare = spare - extra
    return np.array(holding)


def normal_values(rng, dims, spread, limit, pieces=(), held_as=jnp.bfloat16):
    entries = jax.random.normal(rng, dims, jnp.float32) * spread
    if len(pieces) > 0:
        entries = shard_levels(rng, dims, pieces, -0.22, 0.18) * entries
    return jnp.clip(entries, min=-limit, max=limit).astype(held_as)


def noise_with(rng, dims, spread, limit, pieces, heavy, kind=jnp.bfloat16):
    values = spread * jax.random.normal(rng, dims, jnp.float32)
    if pieces:
        values = values * shard_levels(rng, dims, pieces, -0.22, 0.18)
    return jnp.clip(with_spikes(values, jax.random.fold_in(rng, 3), *heavy), -limit, limit).astype(kind)


def setup_inputs(seed: int = 0) -> dict:
    splits = jax.random.split(jax.random.key(seed), 14)
    query = normal_values(splits[0], (TOKENS, HQ), 1.0, 6.0, ((0, 8), (1, 4)))
    key = normal_values(splits[1], (TOKENS, HQ), 1.0, 6.0, ((0, 8), (1, 4)))
    value = normal_values(splits[2], (TOKENS, HQ), 1.0, 6.0, ((0, 8), (1, 4)))
    episode_lengths = uneven_parts(splits[3], EPISODES, TOKENS, TOKENS // 2, 2).astype(jnp.int32)
    attn_gain = jnp.clip(1.0 + 0.18 * jax.random.normal(splits[4], (HQ,), jnp.float32), 0.1, 1.9)
    out_weight = normal_values(splits[5], (HQ, D), HQ ** -0.5, 0.09375, ((0, 4), (1, 8)))
    residual = draw_residual(jax.random.fold_in(splits[13], 71), 0)
    norm_gain = jnp.clip(1.0 + 0.18 * jax.random.normal(splits[7], (D,), jnp.float32), 0.1, 1.9)
    expert_ids_keys = jax.random.split(jax.random.fold_in(splits[8], 1), TOKENS // TOK_DEV)
    expert_ids_turns = jax.random.permutation(jax.random.fold_in(splits[8], 3), TOKENS // TOK_DEV)
    expert_ids = jax.vmap(lambda own, number: routed_block(jax.random.fold_in(splits[8], 2), own, number, TOK_DEV, EXPERTS, 2, CAP, 2))(expert_ids_keys, expert_ids_turns).reshape((TOKENS, 2))
    route_weights = set_ends(jax.random.randint(splits[9], (TOKENS, 2), 4096, 65536), jax.random.fold_in(splits[9], 1), 4096, 65535).astype(jnp.int32)
    gate_weight = normal_values(splits[10], (EXPERTS, D, FF), D ** -0.5, 0.109375, ((0, 8), (2, 4)))
    up_weight = normal_values(splits[11], (EXPERTS, D, FF), D ** -0.5, 0.109375, ((0, 8), (2, 4)))
    down_weight = noise_with(splits[12], (EXPERTS, FF, D), FF ** -0.5, 0.125, ((0, 8), (1, 4)), (1, 2, 4, 2.0))
    return dict(query=query, key=key, value=value, episode_lengths=episode_lengths, attn_gain=attn_gain, out_weight=out_weight, residual=residual, norm_gain=norm_gain, expert_ids=expert_ids, route_weights=route_weights, gate_weight=gate_weight, up_weight=up_weight, down_weight=down_weight)


def episode_of(positions, lengths):
    starts = (jnp.cumsum(lengths) - lengths).astype(jnp.int32)
    return (lax.optimization_barrier(jnp.sum((starts[None, :] <= positions[:, None]).astype(jnp.int32), axis=1)) - 1).astype(jnp.int32)

def attention(query, key, value, episode_lengths, attn_gain):
    total = query.shape[0]
    blocks = total // TOK_DEV
    positions = jnp.arange(total, dtype=jnp.int32)
    episode = episode_of(positions, episode_lengths)
    lifted_query = jax.nn.silu(query.astype(jnp.float32)).reshape(blocks, TOK_DEV, HEADS, HEAD_DIM)
    lifted_key = jax.nn.silu(key.astype(jnp.float32)).reshape(blocks, TOK_DEV, HEADS, HEAD_DIM)
    value_rows = value.astype(jnp.float32).reshape(blocks, TOK_DEV, HEADS, HEAD_DIM)
    episode_blocks = episode.reshape(blocks, TOK_DEV)
    order = jnp.arange(TOK_DEV, dtype=jnp.int32)
    causal = order[:, None] >= order[None, :]
    highest = lax.Precision.HIGHEST

    def advance(carry, inputs):
        state, prior = carry
        block_query, block_key, block_value, block_episode = inputs
        allowed = (causal & (block_episode[:, None] == block_episode[None, :])).astype(jnp.float32)
        scores = jnp.einsum('thd,shd->hts', block_query, block_key, precision=highest)
        inside = jnp.einsum('hts,shd->thd', scores * allowed[None], block_value, precision=highest)
        carry_mask = (block_episode == prior).astype(jnp.float32)
        outside = jnp.einsum('thd,hde->the', block_query, state, precision=highest)
        final = block_episode[-1].astype(jnp.int32)
        keep = (block_episode == final).astype(jnp.float32)
        fresh = jnp.einsum('shd,she->hde', block_key * keep[:, None, None], block_value, precision=highest)
        state = jnp.where(final == prior, state + fresh, fresh)
        return ((state, final), inside + outside * carry_mask[:, None, None])
    start_state = (jnp.zeros((HEADS, HEAD_DIM, HEAD_DIM), jnp.float32), jnp.array(-1, jnp.int32))
    _, outputs = lax.scan(advance, start_state, (lifted_query, lifted_key, value_rows, episode_blocks))
    attn = outputs.reshape(total, HEADS, HEAD_DIM)
    mean_square = lax.optimization_barrier(jnp.mean(attn * attn, axis=2, keepdims=True))
    scaled = attn * lax.rsqrt(mean_square + 1e-06) * attn_gain.reshape(HEADS, HEAD_DIM)
    return scaled.reshape(total, HQ).astype(jnp.bfloat16)

def reference(query, key, value, episode_lengths, attn_gain, out_weight, residual, norm_gain, expert_ids, route_weights, gate_weight, up_weight, down_weight):
    headed = attention(query, key, value, episode_lengths, attn_gain)
    mixed = jnp.dot(headed, out_weight, preferred_element_type=jnp.float32)
    hidden_state = residual.astype(jnp.float32) + mixed
    mean_square = lax.optimization_barrier(jnp.mean(hidden_state * hidden_state, axis=1, keepdims=True))
    normed = (hidden_state * lax.rsqrt(mean_square + 1e-06) * norm_gain).astype(jnp.bfloat16)
    raw_weights = route_weights.astype(jnp.float32)
    share = (raw_weights / lax.optimization_barrier(jnp.sum(raw_weights, axis=1, keepdims=True))).reshape(-1)
    flat_ids = expert_ids.reshape(-1)
    pair_rows = jnp.arange(flat_ids.shape[0], dtype=jnp.int32) // 2
    room = EXPERTS * CAP
    slice_width = FF // N_HEAD

    def expert_step(total, inputs):
        expert, gate_one, up_one, down_one = inputs
        matches = flat_ids == expert
        chosen = jnp.nonzero(matches, size=room, fill_value=0)[0].astype(jnp.int32)
        count = jnp.sum(matches.astype(jnp.int32)).astype(jnp.int32)
        valid = (jnp.arange(room, dtype=jnp.int32) < count).astype(jnp.float32)
        rows = normed[pair_rows[chosen]]
        gate = jnp.dot(rows, gate_one, preferred_element_type=jnp.float32)
        up = jnp.dot(rows, up_one, preferred_element_type=jnp.float32)
        gated = (jax.nn.silu(gate) * up).astype(jnp.bfloat16)
        combined = jnp.zeros((room, D), jnp.float32)
        for part_index in range(N_HEAD):
            lower = part_index * slice_width
            upper = lower + slice_width
            partial_value = jnp.dot(gated[:, lower:upper], down_one[lower:upper], preferred_element_type=jnp.float32).astype(jnp.bfloat16)
            combined = combined + partial_value.astype(jnp.float32)
        contribution = combined * (share[chosen] * valid)[:, None]
        total = total.at[pair_rows[chosen]].add(contribution)
        return (total, None)
    experts_list = jnp.arange(EXPERTS, dtype=jnp.int32)
    moe, _ = lax.scan(expert_step, jnp.zeros((TOKENS, D), jnp.float32), (experts_list, gate_weight, up_weight, down_weight))
    return (hidden_state + moe).astype(jnp.bfloat16)
```

```python
import functools

import jax
import jax.numpy as jnp
from jax import lax
from jax.experimental import pallas as pl
from jax.experimental.pallas import tpu as pltpu
from jax.sharding import PartitionSpec as P

HEAD_DIM = 128


highest = lax.Precision.HIGHEST


MESH = pl.DeviceIdType.MESH


def remote(src, dst, send, recv, ctx, head):
    return pltpu.make_async_remote_copy(
        src_ref=src,
        dst_ref=dst,
        send_sem=send,
        recv_sem=recv,
        device_id=(ctx, head),
        device_id_type=MESH,
    )


def seat():
    head = lax.axis_index("head")
    return lax.axis_index("ctx"), lax.div(head, 2), lax.rem(head, 2)


def flip(me, i, n):
    if n & (n - 1):
        return lax.rem(i - me + 2 * n, n)
    other, bit = me, 1
    while bit < n:
        on = lax.rem(lax.div(me, bit), 2)
        other = other + lax.rem(lax.div(i, bit), 2) * bit * (1 - 2 * on)
        bit *= 2
    return other


def moe_kernel(
    n,
    chips,
    hidden_ref,
    normed_ref,
    ids_ref,
    route_ref,
    gate_ref,
    up_ref,
    down_ref,
    layer_ref,
    gate_w,
    up_w,
    down_w,
    outb,
    full,
    gated,
    part,
    pair,
    out_x,
    in_x,
    total,
    ret,
    acc,
    rank_row,
    rank_col,
    weight_col,
    w_s,
    a_s,
    a_r,
    p_s,
    p_r,
    x_s,
    x_r,
    f_s,
    f_r,
    s_s,
    s_r,
    c_s,
    c_r,
    h_s,
    h_r,
):
    me, chip, core = seat()
    f32, bf16 = jnp.float32, jnp.bfloat16
    tokens, width = normed_ref.shape
    cap = full.shape[1]
    batch = n // 4
    mine, partner = chip * 2 + core, chip * 2 + 1 - core

    weights = [
        pltpu.make_async_copy(gate_ref, gate_w, w_s.at[0]),
        pltpu.make_async_copy(up_ref, up_w, w_s.at[1]),
        pltpu.make_async_copy(down_ref, down_w, w_s.at[2]),
    ]
    for copy in weights:
        copy.start()

    barrier = pltpu.get_barrier_semaphore()

    def tell(ctx, head):
        pl.semaphore_signal(barrier, inc=1, device_id=(ctx, head), device_id_type=MESH)

    tell(me, partner)
    for j in range(1, chips):
        tell(me, lax.rem(chip + j, chips) * 2 + core)

    @pl.loop(1, n)
    def _(i):
        tell(lax.rem(me + i, n), mine)

    expert = lax.broadcasted_iota(jnp.int32, (n, tokens), 0)
    first = ids_ref[0:1, :] == expert
    second = ids_ref[1:2, :] == expert
    raw = route_ref[...].astype(f32)
    shares = raw / (raw[0:1, :] + raw[1:2, :])
    weight = jnp.where(first, shares[0:1, :], 0.0) + jnp.where(second, shares[1:2, :], 0.0)
    named = first | second
    before = (
        lax.broadcasted_iota(jnp.int32, (tokens, tokens), 0)
        < lax.broadcasted_iota(jnp.int32, (tokens, tokens), 1)
    ).astype(f32)
    count = jnp.dot(
        jnp.where(named, 1.0, 0.0).astype(bf16), before.astype(bf16), preferred_element_type=f32
    )
    rank = jnp.where(named, count, -1.0)
    rank_t, weight_t = rank.T, weight.T
    for e in range(n):
        rank_row[e] = jnp.broadcast_to(rank[e : e + 1, :], rank_row.shape[1:])
        rank_col[e] = jnp.broadcast_to(rank_t[:, e : e + 1], rank_col.shape[1:])
        weight_col[e] = jnp.broadcast_to(weight_t[:, e : e + 1], weight_col.shape[1:])
    acc[...] = hidden_ref[...]

    def spread_of(i):
        row = rank_row[flip(me, i, n)][0:1, :]
        place = lax.broadcasted_iota(jnp.int32, (cap, tokens), 0).astype(f32)
        chosen = jnp.where(place == row, 1.0, 0.0).astype(bf16)
        return jnp.dot(chosen, normed_ref[...], preferred_element_type=f32).astype(bf16)

    def cell(ref, block, head):
        return ref.at[block, :, pl.ds(pl.multiple_of(head * width, 128), width)]

    full[0, :, pl.ds(pl.multiple_of(mine * width, 128), width)] = spread_of(0)

    pl.semaphore_wait(barrier, chips + n - 1)

    def to_partner(i, head):
        b = cell(full, i, head)
        return remote(b, b, p_s.at[i], p_r.at[i], me, partner)

    def to_chip(i, j):
        b = cell(full, i, mine)
        return remote(b, b, x_s.at[j, i], x_r.at[j, i], me, lax.rem(chip + j, chips) * 2 + core)

    def from_chip(i, j):
        b = cell(full, i, lax.rem(chip - j + chips, chips) * 2 + core)
        return remote(b, b, x_s.at[j, i], x_r.at[j, i], me, partner)

    def forward(i, j, which):
        b = cell(full, i, lax.rem(chip - j + chips, chips) * 2 + which)
        return remote(b, b, f_s.at[j, i], f_r.at[j, i], me, partner)

    def sent(i):
        return remote(
            outb.at[i], cell(full, i, mine), a_s.at[i], a_r.at[i], flip(me, i, n), mine
        )

    def spread(i):
        for j in range(1, chips):
            to_chip(i, j).start()
        to_partner(i, mine).start()

    spread(0)
    half = n // 2

    def issue(i):
        outb[i] = spread_of(i)
        sent(i).start()

    @pl.loop(0, half)
    def _(k):
        @pl.when(k >= 1)
        def _():
            issue(k)

        issue(k + half)

    def each(b, body, skip=0):
        @pl.loop(b * batch + skip, (b + 1) * batch)
        def _(i):
            body(i)

    def arrive(i):
        sent(i).wait_recv()
        spread(i)

    def relay(i):
        for j in range(1, chips):
            from_chip(i, j).wait_recv()
            forward(i, j, core).start()

    def complete(i):
        to_partner(i, partner).wait_recv()
        for j in range(1, chips):
            forward(i, j, 1 - core).wait_recv()

    def expand(b):
        each(b, complete)
        tile = 256 if gate_w.shape[1] % 256 == 0 else gate_w.shape[1]

        @pl.loop(0, gate_w.shape[1] // tile)
        def _(t):
            rows = full[pl.ds(b * batch, batch)].reshape(batch * cap, full.shape[2])
            at = pl.ds(pl.multiple_of(t * tile, 128), tile)
            gate = jnp.dot(rows, gate_w[:, at], preferred_element_type=f32)
            up = jnp.dot(rows, up_w[:, at], preferred_element_type=f32)
            gated[:, at] = (gate / (1.0 + jnp.exp(-gate)) * up).astype(bf16)

    def column(j):
        return lax.rem(chip + j, chips)

    def swap(i, j):
        return remote(
            cell(part, i, column(j) * 2 + 1 - core),
            pair.at[i, j],
            s_s.at[j, i],
            s_r.at[j, i],
            me,
            partner,
        )

    def cross(i, j):
        return remote(
            out_x.at[i, j], in_x.at[i, j], c_s.at[j, i], c_r.at[j, i], me, column(j) * 2 + core
        )

    def home(i):
        return remote(total.at[i], ret.at[i], h_s.at[i], h_r.at[i], flip(me, i, n), mine)

    def contract(b):
        tile = 256

        @pl.loop(0, part.shape[2] // tile)
        def _(t):
            at = pl.ds(pl.multiple_of(t * tile, 128), tile)
            value = jnp.dot(gated[...], down_w[:, at], preferred_element_type=f32)
            part[pl.ds(b * batch, batch), :, at] = value.astype(bf16).reshape(batch, cap, tile)

        def begin(i):
            for j in list(range(1, chips)) + [0]:
                swap(i, j).start()

        each(b, begin)

    def paired(i, j):
        swap(i, j).wait_recv()
        head = pl.multiple_of((column(j) * 2 + core) * width, 128)
        return part[i, :, pl.ds(head, width)].astype(f32) + pair[i, j].astype(f32)

    def pass_on(i):
        for j in range(1, chips):
            out_x[i, j] = paired(i, j).astype(bf16)
            cross(i, j).start()

    def gather(i):
        value = paired(i, 0)
        for j in range(1, chips):
            cross(i, j).wait_recv()
            value = value + in_x[i, j].astype(f32)
        return value.astype(bf16)

    def send_home(i):
        total[i] = gather(i)
        home(i).start()

    def combine(i):
        e = flip(me, i, n)
        place = lax.broadcasted_iota(jnp.int32, (tokens, cap), 1).astype(f32)
        pick = jnp.where(rank_col[e][:, 0:cap] == place, 1.0, 0.0).astype(bf16)
        value = jnp.dot(pick, ret[i], preferred_element_type=f32)
        acc[...] += weight_col[e][:, 0:1] * value

    def receive(i):
        home(i).wait_recv()
        combine(i)

    each(0, arrive, 1)
    each(1, arrive)
    each(0, relay)
    weights[0].wait()
    weights[1].wait()
    expand(0)
    each(1, relay)
    weights[2].wait()
    contract(0)
    each(2, arrive)
    each(0, pass_on)
    expand(1)
    each(2, relay)
    contract(1)
    each(3, arrive)
    each(1, pass_on)
    ret[0] = gather(0)
    each(0, send_home, 1)
    expand(2)
    each(3, relay)
    contract(2)
    each(2, pass_on)
    each(1, send_home)
    combine(0)
    expand(3)
    each(2, send_home)
    contract(3)
    each(3, pass_on)
    each(0, receive, 1)
    each(1, receive)
    each(3, send_home)
    each(2, receive)
    each(3, receive)
    layer_ref[...] = acc[...].astype(bf16)

    @pl.loop(0, n)
    def _(i):
        to_partner(i, mine).wait_send()
        for j in range(1, chips):
            forward(i, j, core).wait_send()
            to_chip(i, j).wait_send()
            cross(i, j).wait_send()
        for j in range(chips):
            swap(i, j).wait_send()

    @pl.loop(1, n)
    def _(i):
        sent(i).wait_send()
        home(i).wait_send()


def experts(hidden, normed, ids, route, gate, up, down, n, heads):
    chips = heads // 2
    tokens, width = normed.shape
    cap = -(-3 * tokens // n // 16) * 16
    dma = pltpu.SemaphoreType.DMA
    bf16, f32 = jnp.bfloat16, jnp.float32
    vmem, hbm = pl.BlockSpec(memory_space=pltpu.VMEM), pl.BlockSpec(memory_space=pl.ANY)
    block = pltpu.VMEM((n, cap, width), bf16)
    piece = pltpu.VMEM((n, chips, cap, width), bf16)
    wide = pltpu.VMEM((n, cap, width * heads), bf16)
    column = pltpu.VMEM((n, tokens, 128), f32)
    return pl.pallas_call(
        functools.partial(moe_kernel, n, chips),
        out_shape=jax.ShapeDtypeStruct((tokens, width), bf16),
        in_specs=[vmem] * 4 + [hbm] * 3,
        out_specs=vmem,
        scratch_shapes=[
            pltpu.VMEM(gate.shape, gate.dtype),
            pltpu.VMEM(up.shape, up.dtype),
            pltpu.VMEM(down.shape, down.dtype),
            block,
            wide,
            pltpu.VMEM((n // 4 * cap, gate.shape[1]), bf16),
            wide,
            piece,
            piece,
            piece,
            block,
            block,
            pltpu.VMEM((tokens, width), f32),
            pltpu.VMEM((n, 8, tokens), f32),
            column,
            column,
        ]
        + [dma((3,))]
        + [dma((n,))] * 4
        + [dma((chips, n))] * 8
        + [dma((n,))] * 2,
        compiler_params=pltpu.CompilerParams(
            collective_id=0, has_side_effects=True, vmem_limit_bytes=60 * 1024 * 1024
        ),
        name="experts",
    )(hidden, normed, ids, route, gate, up, down)


def attend_kernel(
    n,
    heads,
    q_ref,
    k_ref,
    v_ref,
    allowed_ref,
    keep_ref,
    carry_ref,
    earlier_ref,
    gain_ref,
    w_ref,
    res_ref,
    hidden_ref,
    squares_ref,
    wall,
    states,
    attn,
    headed,
    acc,
    mixed,
    pair,
    out_x,
    in_x,
    sq_own,
    sq_all,
    here,
    w_s,
    w_r,
    s_s,
    s_r,
    p_s,
    p_r,
    x_s,
    x_r,
    q_s,
    q_r,
):
    me, chip, core = seat()
    chips = heads // 2
    mine, partner = chip * 2 + core, chip * 2 + 1 - core
    local, size = states.shape[1], HEAD_DIM
    half, piece = w_ref.shape[0] // 2, w_ref.shape[0] // 4
    group = n // heads
    f32 = jnp.float32

    def seat_at(p):
        return 2 * p - lax.div(p, n // 2) * (4 * p - 2 * n + 1)

    low = lax.div(me, 2)
    place = low + lax.rem(me, 2) * (n - lax.div(me + 1, 2) - low)
    ahead = [seat_at(lax.rem(place + 1, n)), seat_at(lax.rem(place + n - 1, n))]

    def origin(way, distance):
        step = n - distance if way == 0 else distance
        return seat_at(lax.rem(place + step, n))

    barrier = pltpu.get_barrier_semaphore()

    def tell(ctx, head):
        pl.semaphore_signal(barrier, inc=1, device_id=(ctx, head), device_id_type=MESH)

    tell(ahead[0], mine)
    tell(ahead[1], mine)
    for j in range(1, heads):
        tell(me, lax.rem(mine + j, heads))
    pl.semaphore_wait(barrier, heads + 1)

    def w_rows(way, part):
        return pl.ds(way * half + part * piece, piece)

    def w_first(way, part):
        rows = w_rows(way, part)
        return remote(
            w_ref.at[rows],
            wall.at[me, rows],
            w_s.at[way, part, 0],
            w_r.at[way, part, 0],
            ahead[way],
            mine,
        )

    def w_step(way, part, held, stage):
        cell = wall.at[origin(way, held), w_rows(way, part)]
        return remote(
            cell, cell, w_s.at[way, part, stage], w_r.at[way, part, stage], ahead[way], mine
        )

    def s_step(way, held, stage):
        cell = states.at[origin(way, held), pl.ds(way * (local // 2), local // 2)]
        return remote(cell, cell, s_s.at[way, stage], s_r.at[way, stage], ahead[way], mine)

    for part in range(2):
        for way in range(2):
            w_first(way, part).start()
    own = pltpu.make_async_copy(w_ref, wall.at[me], here)
    own.start()

    def columns(h):
        return pl.ds(pl.multiple_of(h * size, size), size)

    def lifted(ref, h):
        x = ref[:, columns(h)].astype(f32)
        return x / (1.0 + jnp.exp(-x))

    @pl.loop(0, local)
    def _(h):
        kept = lifted(k_ref, h) * keep_ref[...]
        state = jnp.dot(
            kept.T, v_ref[:, columns(h)].astype(f32), precision=highest, preferred_element_type=f32
        )
        states[me, h] = state.astype(jnp.bfloat16)

    for way in range(2):
        s_step(way, 0, 0).start()

    @pl.loop(0, local)
    def _(h):
        scores = lax.dot_general(
            lifted(q_ref, h),
            lifted(k_ref, h),
            (((1,), (1,)), ((), ())),
            precision=highest,
            preferred_element_type=f32,
        )
        attn[:, columns(h)] = jnp.dot(
            scores * allowed_ref[...],
            v_ref[:, columns(h)].astype(f32),
            precision=highest,
            preferred_element_type=f32,
        )

    acc[...] = jnp.zeros_like(acc)

    def s_stage(stage):
        for way in range(2):
            s_step(way, stage + 1, stage).wait_recv()

            @pl.when(stage < n - 2)
            def _():
                s_step(way, stage + 1, stage + 1).start()

    def w_stage(stage):
        for part in range(2):
            for way in range(2):
                w_step(way, part, stage + 1, stage).wait_recv()

                @pl.when(stage < n - 2)
                def _():
                    w_step(way, part, stage + 1, stage + 1).start()

    early = (n - 2) // 2

    @pl.loop(0, early)
    def _(t):
        s_stage(2 * t)
        s_stage(2 * t + 1)
        w_stage(t)

    s_stage(n - 2)

    @pl.loop(0, local)
    def _(h):
        def add(j, total):
            return total + earlier_ref[j] * states[j, h].astype(f32)

        state = lax.fori_loop(0, n, add, jnp.zeros((size, size), f32))
        outside = jnp.dot(
            lifted(q_ref, h), state, precision=highest, preferred_element_type=f32
        )
        full = attn[:, columns(h)] + outside * carry_ref[...]
        mean_square = jnp.mean(full * full, axis=1, keepdims=True)
        scaled = full * lax.rsqrt(mean_square + 1e-06) * gain_ref[:, columns(h)]
        headed[:, columns(h)] = scaled.astype(jnp.bfloat16)

    def project(way, held):
        src = origin(way, held)
        rows = pl.ds(way * half, half)
        acc[src] += jnp.dot(headed[:, rows], wall[src, rows], preferred_element_type=f32)

    own.wait()

    @pl.loop(0, early + 1)
    def _(held):
        project(0, held)
        project(1, held)

    @pl.loop(early, n - 1)
    def _(stage):
        w_stage(stage)
        project(0, stage + 1)
        project(1, stage + 1)

    mixed[...] = acc[...].astype(jnp.bfloat16)

    def column(j):
        return lax.rem(chip + j, chips)

    def blocks(head):
        return pl.ds(head * group, group)

    def swap(j):
        return remote(
            mixed.at[blocks(column(j) * 2 + 1 - core)],
            pair.at[j],
            p_s.at[j],
            p_r.at[j],
            me,
            partner,
        )

    def cross(j):
        return remote(
            out_x.at[j], in_x.at[j], x_s.at[j], x_r.at[j], me, column(j) * 2 + core
        )

    for j in list(range(1, chips)) + [0]:
        swap(j).start()

    def paired(j):
        swap(j).wait_recv()
        return acc[blocks(column(j) * 2 + core)] + pair[j].astype(f32)

    for j in range(1, chips):
        out_x[j] = paired(j).astype(jnp.bfloat16)
        cross(j).start()
    total = paired(0) + res_ref[...].astype(f32)
    hidden_ref[...] = total
    for j in range(1, chips):
        cross(j).wait_recv()
        hidden_ref[...] += in_x[j].astype(f32)
    ones = jnp.ones((8, hidden_ref.shape[2]), f32)
    squares = jnp.zeros((8, hidden_ref.shape[1]), f32)
    for b in range(group):
        part = hidden_ref[b]
        squares = squares + lax.dot_general(
            ones,
            part * part,
            (((1,), (1,)), ((), ())),
            precision=highest,
            preferred_element_type=f32,
        )
    sq_own[...] = squares

    def share(j, to, slot):
        return remote(sq_own, sq_all.at[slot], q_s.at[j], q_r.at[j], me, to)

    for j in range(1, heads):
        share(j, lax.rem(mine + j, heads), j).start()
    for j in range(1, heads):
        share(j, mine, j).wait_recv()
        squares = squares + sq_all[j]
    squares_ref[...] = squares

    for j in range(1, heads):
        share(j, mine, j).wait_send()
    for j in range(chips):
        swap(j).wait_send()
    for j in range(1, chips):
        cross(j).wait_send()

    for part in range(2):
        for way in range(2):
            w_first(way, part).wait_send()

    @pl.loop(0, n - 1)
    def _(stage):
        for way in range(2):
            s_step(way, stage, stage).wait_send()

    @pl.loop(1, n - 1)
    def _(stage):
        for part in range(2):
            for way in range(2):
                w_step(way, part, stage, stage).wait_send()


def attend(query, key, value, allowed, keep, carry, earlier, gain, weight, residual, n, heads):
    rows, feats = query.shape
    width, group = weight.shape[1], n // heads
    local, chips = feats // HEAD_DIM, heads // 2
    dma = pltpu.SemaphoreType.DMA
    bf16, f32 = jnp.bfloat16, jnp.float32
    vmem = pl.BlockSpec(memory_space=pltpu.VMEM)
    piece = pltpu.VMEM((chips, group, rows, width), bf16)
    return pl.pallas_call(
        functools.partial(attend_kernel, n, heads),
        out_shape=(
            jax.ShapeDtypeStruct((group, rows, width), f32),
            jax.ShapeDtypeStruct((8, rows), f32),
        ),
        in_specs=[vmem] * 8 + [pl.BlockSpec(memory_space=pl.ANY), vmem],
        out_specs=(vmem, vmem),
        scratch_shapes=[
            pltpu.VMEM((n,) + weight.shape, bf16),
            pltpu.VMEM((n, local, HEAD_DIM, HEAD_DIM), bf16),
            pltpu.VMEM((rows, feats), f32),
            pltpu.VMEM((rows, feats), bf16),
            pltpu.VMEM((n, rows, width), f32),
            pltpu.VMEM((n, rows, width), bf16),
            piece,
            piece,
            piece,
            pltpu.VMEM((8, rows), f32),
            pltpu.VMEM((heads, 8, rows), f32),
            dma,
            dma((2, 2, n)),
            dma((2, 2, n)),
            dma((2, n)),
            dma((2, n)),
            dma((chips,)),
            dma((chips,)),
            dma((chips,)),
            dma((chips,)),
            dma((heads,)),
            dma((heads,)),
        ],
        compiler_params=pltpu.CompilerParams(
            collective_id=2, has_side_effects=True, vmem_limit_bytes=60 * 1024 * 1024
        ),
        name="attend",
    )(query, key, value, allowed, keep, carry, earlier, gain, weight, residual)


def episode_of(positions, lengths):
    starts = jnp.cumsum(lengths) - lengths
    return jnp.sum((starts[None, :] <= positions[:, None]).astype(jnp.int32), axis=1) - 1


def on_device(
    query,
    key,
    value,
    episode_lengths,
    attn_gain,
    out_weight,
    residual,
    norm_gain,
    expert_ids,
    route_weights,
    gate_weight,
    up_weight,
    down_weight,
):
    tok_rows = query.shape[0]
    head_size = HEAD_DIM
    own_index = lax.axis_index("ctx")
    ctx_count = lax.axis_size("ctx")
    positions = own_index * tok_rows + jnp.arange(tok_rows, dtype=jnp.int32)
    episode = episode_of(positions, episode_lengths)
    prior = episode_of(positions[:1] - 1, episode_lengths)[0]
    final = episode[-1]
    keep = (episode == final).astype(jnp.float32)
    finals = episode_of(
        (jnp.arange(ctx_count, dtype=jnp.int32) + 1) * tok_rows - 1, episode_lengths
    )
    earlier = (jnp.arange(ctx_count) < own_index) & (finals == prior)
    earlier = jnp.broadcast_to(
        earlier.astype(jnp.float32)[:, None, None], (ctx_count, 1, head_size)
    )
    order = jnp.arange(tok_rows, dtype=jnp.int32)
    allowed = ((order[:, None] >= order[None, :]) & (episode[:, None] == episode[None, :])).astype(
        jnp.float32
    )
    heads = lax.axis_size("head")
    col = out_weight.shape[1]
    width = residual.shape[1] * heads
    hidden_blocks, squares = attend(
        query,
        key,
        value,
        allowed,
        keep[:, None],
        (episode == prior).astype(jnp.float32)[:, None],
        earlier,
        attn_gain[None, :],
        out_weight,
        jnp.swapaxes(residual.reshape(tok_rows, -1, col), 0, 1),
        ctx_count,
        heads,
    )
    hidden_slice = jnp.swapaxes(hidden_blocks, 0, 1).reshape(tok_rows, -1)
    normed = (
        hidden_slice * lax.rsqrt(squares[0] / width + 1e-06)[:, None] * norm_gain
    ).astype(jnp.bfloat16)
    return experts(
        hidden_slice,
        normed,
        expert_ids.T,
        route_weights.T,
        gate_weight[0],
        up_weight[0],
        down_weight[0],
        ctx_count,
        heads,
    )


def solution(mesh):
    placed = (
        P("ctx", "head"),
        P("ctx", "head"),
        P("ctx", "head"),
        P(),
        P("head"),
        P("head", "ctx"),
        P("ctx", "head"),
        P("head"),
        P("ctx", None),
        P("ctx", None),
        P("ctx", None, "head"),
        P("ctx", None, "head"),
        P("ctx", "head", None),
    )
    return jax.shard_map(
        on_device, mesh=mesh, in_specs=placed, out_specs=P("ctx", "head"), check_vma=False
    )
```

```python
import functools

import jax
import jax.numpy as jnp
from jax import lax
from jax.experimental import pallas as pl
from jax.experimental.pallas import tpu as pltpu
from jax.sharding import PartitionSpec as P

HEAD_DIM = 128
WINDOW = 1


highest = lax.Precision.HIGHEST


MESH = pl.DeviceIdType.MESH


def remote(src, dst, send, recv, ctx, head):
    return pltpu.make_async_remote_copy(
        src_ref=src,
        dst_ref=dst,
        send_sem=send,
        recv_sem=recv,
        device_id=(ctx, head),
        device_id_type=MESH,
    )


def seat():
    head = lax.axis_index("head")
    return lax.axis_index("ctx"), lax.div(head, 2), lax.rem(head, 2)


def flip(me, i, n):
    if n & (n - 1):
        return lax.rem(i - me + 2 * n, n)
    other, bit = me, 1
    while bit < n:
        on = lax.rem(lax.div(me, bit), 2)
        other = other + lax.rem(lax.div(i, bit), 2) * bit * (1 - 2 * on)
        bit *= 2
    return other


def moe_kernel(
    n,
    chips,
    hidden_ref,
    normed_ref,
    ids_ref,
    route_ref,
    gate_ref,
    up_ref,
    down_ref,
    layer_ref,
    gate_w,
    up_w,
    down_w,
    outb,
    full,
    gated,
    part,
    pair,
    out_x,
    in_x,
    total,
    ret,
    acc,
    rank_row,
    rank_col,
    weight_col,
    w_s,
    a_s,
    a_r,
    p_s,
    p_r,
    x_s,
    x_r,
    f_s,
    f_r,
    s_s,
    s_r,
    c_s,
    c_r,
    h_s,
    h_r,
):
    me, chip, core = seat()
    f32, bf16 = jnp.float32, jnp.bfloat16
    tokens, width = normed_ref.shape
    cap = full.shape[1]
    mine, partner = chip * 2 + core, chip * 2 + 1 - core

    weights = [
        pltpu.make_async_copy(gate_ref, gate_w, w_s.at[0]),
        pltpu.make_async_copy(up_ref, up_w, w_s.at[1]),
        pltpu.make_async_copy(down_ref, down_w, w_s.at[2]),
    ]
    for copy in weights:
        copy.start()

    barrier = pltpu.get_barrier_semaphore()

    def tell(ctx, head):
        pl.semaphore_signal(barrier, inc=1, device_id=(ctx, head), device_id_type=MESH)

    tell(me, partner)
    for j in range(1, chips):
        tell(me, lax.rem(chip + j, chips) * 2 + core)

    @pl.loop(1, n)
    def _(i):
        tell(lax.rem(me + i, n), mine)

    expert = lax.broadcasted_iota(jnp.int32, (n, tokens), 0)
    first = ids_ref[0:1, :] == expert
    second = ids_ref[1:2, :] == expert
    raw = route_ref[...].astype(f32)
    shares = raw / (raw[0:1, :] + raw[1:2, :])
    weight = jnp.where(first, shares[0:1, :], 0.0) + jnp.where(second, shares[1:2, :], 0.0)
    named = first | second
    before = (
        lax.broadcasted_iota(jnp.int32, (tokens, tokens), 0)
        < lax.broadcasted_iota(jnp.int32, (tokens, tokens), 1)
    ).astype(f32)
    count = jnp.dot(
        jnp.where(named, 1.0, 0.0).astype(bf16), before.astype(bf16), preferred_element_type=f32
    )
    rank = jnp.where(named, count, -1.0)
    rank_t, weight_t = rank.T, weight.T
    for e in range(n):
        rank_row[e] = jnp.broadcast_to(rank[e : e + 1, :], rank_row.shape[1:])
        rank_col[e] = jnp.broadcast_to(rank_t[:, e : e + 1], rank_col.shape[1:])
        weight_col[e] = jnp.broadcast_to(weight_t[:, e : e + 1], weight_col.shape[1:])
    acc[...] = hidden_ref[...]

    def spread_of(i):
        row = rank_row[flip(me, i, n)][0:1, :]
        place = lax.broadcasted_iota(jnp.int32, (cap, tokens), 0).astype(f32)
        chosen = jnp.where(place == row, 1.0, 0.0).astype(bf16)
        return jnp.dot(chosen, normed_ref[...], preferred_element_type=f32).astype(bf16)

    def cell(ref, block, head):
        return ref.at[block, :, pl.ds(pl.multiple_of(head * width, 128), width)]

    full[0, :, pl.ds(pl.multiple_of(mine * width, 128), width)] = spread_of(0)

    pl.semaphore_wait(barrier, chips + n - 1)

    def to_partner(i, head):
        b = cell(full, i, head)
        return remote(b, b, p_s.at[i], p_r.at[i], me, partner)

    def to_chip(i, j):
        b = cell(full, i, mine)
        return remote(b, b, x_s.at[j, i], x_r.at[j, i], me, lax.rem(chip + j, chips) * 2 + core)

    def from_chip(i, j):
        b = cell(full, i, lax.rem(chip - j + chips, chips) * 2 + core)
        return remote(b, b, x_s.at[j, i], x_r.at[j, i], me, partner)

    def forward(i, j, which):
        b = cell(full, i, lax.rem(chip - j + chips, chips) * 2 + which)
        return remote(b, b, f_s.at[j, i], f_r.at[j, i], me, partner)

    def sent(i):
        return remote(
            outb.at[i], cell(full, i, mine), a_s.at[i], a_r.at[i], flip(me, i, n), mine
        )

    def spread(i):
        for j in range(1, chips):
            to_chip(i, j).start()
        to_partner(i, mine).start()

    spread(0)
    half = n // 2
    share = half // 4

    def issue(i):
        outb[i] = spread_of(i)
        sent(i).start()

    def near(b, body, skip=0):
        @pl.loop(b * share + skip, (b + 1) * share)
        def _(i):
            body(i)

    def far(b, body):
        near(b, lambda i: body(half + i))

    def both(b, body, skip=0):
        far(b, body)
        near(b, body, skip)

    far(0, issue)
    near(0, issue, 1)
    for b in range(1, 4):
        if b < WINDOW:
            far(b, issue)
        near(b, issue)

    def arrive(i):
        sent(i).wait_recv()
        spread(i)

    def arrive_far(b):
        far(b, arrive)
        if b + WINDOW < 4:
            far(b + WINDOW, issue)

    def relay(i):
        for j in range(1, chips):
            from_chip(i, j).wait_recv()
            forward(i, j, core).start()

    def complete(i):
        to_partner(i, partner).wait_recv()
        for j in range(1, chips):
            forward(i, j, 1 - core).wait_recv()

    def pick_rows(b):
        rows = [full[pl.ds(at + b * share, share)] for at in (0, half)]
        return jnp.concatenate([r.reshape(share * cap, r.shape[2]) for r in rows], axis=0)

    def expand(b):
        both(b, complete)
        tile = 256 if gate_w.shape[1] % 256 == 0 else gate_w.shape[1]

        @pl.loop(0, gate_w.shape[1] // tile)
        def _(t):
            rows = pick_rows(b)
            at = pl.ds(pl.multiple_of(t * tile, 128), tile)
            gate = jnp.dot(rows, gate_w[:, at], preferred_element_type=f32)
            up = jnp.dot(rows, up_w[:, at], preferred_element_type=f32)
            gated[:, at] = (gate / (1.0 + jnp.exp(-gate)) * up).astype(bf16)

    def column(j):
        return lax.rem(chip + j, chips)

    def swap(i, j):
        return remote(
            cell(part, i, column(j) * 2 + 1 - core),
            pair.at[i, j],
            s_s.at[j, i],
            s_r.at[j, i],
            me,
            partner,
        )

    def cross(i, j):
        return remote(
            out_x.at[i, j], in_x.at[i, j], c_s.at[j, i], c_r.at[j, i], me, column(j) * 2 + core
        )

    def home(i):
        return remote(total.at[i], ret.at[i], h_s.at[i], h_r.at[i], flip(me, i, n), mine)

    def contract(b):
        tile = 256

        @pl.loop(0, part.shape[2] // tile)
        def _(t):
            at = pl.ds(pl.multiple_of(t * tile, 128), tile)
            value = jnp.dot(gated[...], down_w[:, at], preferred_element_type=f32)
            value = value.astype(bf16).reshape(2, share, cap, tile)
            for side in range(2):
                part[pl.ds(side * half + b * share, share), :, at] = value[side]

        def begin(i):
            for j in list(range(1, chips)) + [0]:
                swap(i, j).start()

        both(b, begin)

    def paired(i, j):
        swap(i, j).wait_recv()
        head = pl.multiple_of((column(j) * 2 + core) * width, 128)
        return part[i, :, pl.ds(head, width)].astype(f32) + pair[i, j].astype(f32)

    def pass_on(i):
        for j in range(1, chips):
            out_x[i, j] = paired(i, j).astype(bf16)
            cross(i, j).start()

    def gather(i):
        value = paired(i, 0)
        for j in range(1, chips):
            cross(i, j).wait_recv()
            value = value + in_x[i, j].astype(f32)
        return value.astype(bf16)

    def send_home(i):
        total[i] = gather(i)
        home(i).start()

    def combine(i):
        e = flip(me, i, n)
        place = lax.broadcasted_iota(jnp.int32, (tokens, cap), 1).astype(f32)
        pick = jnp.where(rank_col[e][:, 0:cap] == place, 1.0, 0.0).astype(bf16)
        value = jnp.dot(pick, ret[i], preferred_element_type=f32)
        acc[...] += weight_col[e][:, 0:1] * value

    def receive(i):
        home(i).wait_recv()
        combine(i)

    near(0, arrive, 1)
    near(1, arrive)
    near(0, relay)
    near(2, arrive)
    arrive_far(0)
    near(1, relay)
    near(3, arrive)
    near(2, relay)
    far(0, relay)
    near(3, relay)
    for copy in weights:
        copy.wait()
    for b in range(4):
        expand(b)
        if b < 3:
            arrive_far(b + 1)
        contract(b)
        if b == 1:
            far(0, send_home)
            ret[0] = gather(0)
            near(0, send_home, 1)
        elif b > 1:
            both(b - 1, send_home)
        if b < 3:
            far(b + 1, relay)
        both(b, pass_on)
    combine(0)
    near(0, receive, 1)
    near(1, receive)
    far(0, receive)
    both(3, send_home)
    near(2, receive)
    far(1, receive)
    far(2, receive)
    near(3, receive)
    far(3, receive)
    layer_ref[...] = acc[...].astype(bf16)

    @pl.loop(0, n)
    def _(i):
        to_partner(i, mine).wait_send()
        for j in range(1, chips):
            forward(i, j, core).wait_send()
            to_chip(i, j).wait_send()
            cross(i, j).wait_send()
        for j in range(chips):
            swap(i, j).wait_send()

    @pl.loop(1, n)
    def _(i):
        sent(i).wait_send()
        home(i).wait_send()


def experts(hidden, normed, ids, route, gate, up, down, n, heads):
    chips = heads // 2
    tokens, width = normed.shape
    cap = -(-3 * tokens // n // 16) * 16
    dma = pltpu.SemaphoreType.DMA
    bf16, f32 = jnp.bfloat16, jnp.float32
    vmem, hbm = pl.BlockSpec(memory_space=pltpu.VMEM), pl.BlockSpec(memory_space=pl.ANY)
    block = pltpu.VMEM((n, cap, width), bf16)
    piece = pltpu.VMEM((n, chips, cap, width), bf16)
    wide = pltpu.VMEM((n, cap, width * heads), bf16)
    column = pltpu.VMEM((n, tokens, 128), f32)
    return pl.pallas_call(
        functools.partial(moe_kernel, n, chips),
        out_shape=jax.ShapeDtypeStruct((tokens, width), bf16),
        in_specs=[vmem] * 4 + [hbm] * 3,
        out_specs=vmem,
        scratch_shapes=[
            pltpu.VMEM(gate.shape, gate.dtype),
            pltpu.VMEM(up.shape, up.dtype),
            pltpu.VMEM(down.shape, down.dtype),
            block,
            wide,
            pltpu.VMEM((n // 4 * cap, gate.shape[1]), bf16),
            wide,
            piece,
            piece,
            piece,
            block,
            block,
            pltpu.VMEM((tokens, width), f32),
            pltpu.VMEM((n, 8, tokens), f32),
            column,
            column,
        ]
        + [dma((3,))]
        + [dma((n,))] * 4
        + [dma((chips, n))] * 8
        + [dma((n,))] * 2,
        compiler_params=pltpu.CompilerParams(
            collective_id=0, has_side_effects=True, vmem_limit_bytes=60 * 1024 * 1024
        ),
        name="experts",
    )(hidden, normed, ids, route, gate, up, down)


def attend_kernel(
    n,
    heads,
    flat,
    lengths_ref,
    q_ref,
    k_ref,
    v_ref,
    gain_ref,
    w_ref,
    res_ref,
    norm_ref,
    hidden_ref,
    normed_ref,
    wall,
    allowed,
    keep,
    carry,
    fresh,
    before,
    after,
    attn,
    headed,
    acc,
    mixed,
    parts,
    sum_out,
    sum_in,
    sq_own,
    sq_all,
    here,
    y_s,
    y_r,
    m_s,
    m_r,
    f_s,
    f_r,
    c_s,
    c_r,
    e_s,
    e_r,
    r_s,
    r_r,
    o_s,
    o_r,
    q_s,
    q_r,
):
    me, chip, core = seat()
    mine = chip * 2 + core
    rows, feats = q_ref.shape
    size = HEAD_DIM
    local, slots, group, col = feats // size, n // 2, n // heads, w_ref.shape[1]
    pieces, share = 4, w_ref.shape[0] // 4
    f32, bf16 = jnp.float32, jnp.bfloat16
    beside, across = flip(me, 1, n), flip(me, 2, n)

    barrier = pltpu.get_barrier_semaphore()

    def tell(ctx, head):
        pl.semaphore_signal(barrier, inc=1, device_id=(ctx, head), device_id_type=MESH)

    tell(beside, mine)
    tell(across, mine)
    for q in range(1, slots // 2):
        tell(flip(me, 4 * q, n), mine)
    tell(lax.rem(me + 1, n), mine)
    tell(lax.rem(me + n - 1, n), mine)
    for j in range(1, heads):
        tell(me, lax.rem(mine + j, heads))

    base = me * rows
    starts, last = [0], base + rows - 1
    for e in range(lengths_ref.shape[0] - 1):
        starts.append(starts[-1] + lengths_ref[e])
    open_at = jnp.int32(0)
    for s in starts[1:]:
        open_at = jnp.where(s <= last, s, open_at)

    def opened(shape):
        place = lax.broadcasted_iota(jnp.int32, shape, 0) + base
        seg = jnp.zeros(shape, jnp.int32)
        for s in starts[1:]:
            seg = jnp.where(place >= s, s, seg)
        return place, seg

    place, seg = opened((rows, size))
    keep[...] = jnp.where(place >= open_at, 1.0, 0.0)
    carry[...] = jnp.where(seg < base, 1.0, 0.0)
    place, seg = opened((rows, rows))
    source = lax.broadcasted_iota(jnp.int32, (rows, rows), 1) + base
    allowed[...] = jnp.where((source <= place) & (source >= seg), 1.0, 0.0)
    goes_on = jnp.where(open_at < base, 1.0, 0.0)

    pl.semaphore_wait(barrier, 3 + slots // 2 + heads - 1)

    def strip(k):
        return pl.ds(pl.multiple_of(k * share, 16), share)

    def to_beside(k):
        return remote(w_ref.at[strip(k)], wall.at[1, strip(k)], y_s.at[k], y_r.at[k], beside, mine)

    def to_far(q, k):
        return remote(
            w_ref.at[strip(k)],
            wall.at[2 * q, strip(k)],
            m_s.at[q, k],
            m_r.at[q, k],
            flip(me, 4 * q, n),
            mine,
        )

    def pass_far(q, k):
        return remote(
            wall.at[2 * q, strip(k)],
            wall.at[2 * q + 1, strip(k)],
            f_s.at[q, k],
            f_r.at[q, k],
            beside,
            mine,
        )

    own = pltpu.make_async_copy(w_ref, wall.at[0], here)
    for k in range(2):
        to_far(1, k).start()
    for k in range(pieces):
        to_beside(k).start()
    own.start()

    def columns(h):
        return pl.ds(pl.multiple_of(h * size, size), size)

    def lifted(ref, h):
        x = ref[:, columns(h)].astype(f32)
        return x / (1.0 + jnp.exp(-x))

    @pl.loop(0, local)
    def _(h):
        kept = lifted(k_ref, h) * keep[...]
        fresh[h] = jnp.dot(
            kept.T.astype(bf16), v_ref[:, columns(h)], preferred_element_type=f32
        )

    bundle = local // 4

    def chain(g):
        some = pl.ds(g * bundle, bundle)
        return remote(
            after.at[some],
            before.at[some],
            c_s.at[g],
            c_r.at[g],
            lax.rem(me + 1, n),
            mine,
        )

    @pl.when(me == 0)
    def _():
        before[...] = jnp.zeros_like(before)

    def turn():
        @pl.loop(0, 4)
        def _(g):
            @pl.when(me > 0)
            def _():
                chain(g).wait_recv()

            @pl.when(me < n - 1)
            def _():
                some = pl.ds(g * bundle, bundle)
                after[some] = (fresh[some] + goes_on * before[some].astype(f32)).astype(bf16)
                chain(g).start()

    def inside(h):
        scores = lax.dot_general(
            lifted(q_ref, h).astype(bf16),
            lifted(k_ref, h).astype(bf16),
            (((1,), (1,)), ((), ())),
            preferred_element_type=f32,
        )
        attn[:, columns(h)] = jnp.dot(
            (scores * allowed[...]).astype(bf16), v_ref[:, columns(h)], preferred_element_type=f32
        )

    services = pieces * (slots // 2 - 1)
    many = -(-local // services)

    def serve(j):
        q, k = lax.div(j, pieces) + 1, lax.rem(j, pieces)
        to_far(q, k).wait_recv()
        pass_far(q, k).start()

        @pl.when(j + 2 < services)
        def _():
            to_far(lax.div(j + 2, pieces) + 1, lax.rem(j + 2, pieces)).start()

    moment = jnp.minimum(lax.div(10 * me + 18, 27), services - 1)

    def stage(j):
        @pl.when(j == moment)
        def _():
            turn()

        @pl.loop(j * many, (j + 1) * many)
        def _(h):
            @pl.when(h < local)
            def _():
                inside(h)

    @pl.loop(0, services - 1)
    def _(j):
        stage(j)
        serve(j)

    stage(services - 1)

    def finish(h):
        outside = jnp.dot(lifted(q_ref, h).astype(bf16), before[h], preferred_element_type=f32)
        full = attn[:, columns(h)] + outside * carry[...]
        mean_square = jnp.mean(full * full, axis=1, keepdims=True)
        scaled = full * lax.rsqrt(mean_square + 1e-06) * gain_ref[:, columns(h)]
        headed[0, :, columns(h)] = scaled.astype(bf16)

    def exchange(p):
        wide = feats // 2
        at = pl.ds(p * wide, wide)
        return remote(
            headed.at[0, :, at], headed.at[1, :, at], e_s.at[p], e_r.at[p], across, mine
        )

    for p in range(2):

        @pl.loop(p * local // 2, (p + 1) * local // 2)
        def _(h):
            finish(h)

        exchange(p).start()

    def mask_of(s):
        return 4 * lax.div(s, 2) + lax.rem(s, 2)

    def block_of(s):
        return flip(me, mask_of(s), n)

    def deliver(s, which, to, rel):
        return remote(
            mixed.at[which, s],
            parts.at[which, s, rel],
            r_s.at[which, s],
            r_r.at[which, s, rel],
            me,
            to,
        )

    def project(s, which):
        value = jnp.dot(headed[which], wall[s], preferred_element_type=f32)
        owner = lax.div(block_of(s), group)
        acc[which, s] = value

        @pl.when(owner != mine)
        def _():
            mixed[which, s] = value.astype(bf16)
            deliver(s, which, owner, lax.rem(mine - owner + heads, heads)).start()

    own.wait()
    project(0, 0)
    for k in range(pieces):
        to_beside(k).wait_recv()
    project(1, 0)
    serve(services - 1)

    @pl.loop(2, slots)
    def _(s):
        @pl.when(lax.rem(s, 2) == 1)
        def _():
            for k in range(pieces):
                pass_far(lax.div(s, 2), k).wait_recv()

        project(s, 0)

    for p in range(2):
        exchange(p).wait_recv()

    @pl.loop(0, slots)
    def _(s):
        project(s, 1)

    def summed(s, which):
        value = acc[which, s]
        for rel in range(1, heads):
            deliver(s, which, mine, rel).wait_recv()
            value = value + parts[which, s, rel].astype(f32)
        return value

    def cell(ref, p):
        if flat:
            return ref.at[:, pl.ds(pl.multiple_of(p * col, 128), col)]
        return ref.at[p]

    def hand_over(s):
        return remote(sum_out.at[s], sum_in.at[s], o_s.at[s], o_r.at[s], across, mine)

    def settle(block, value):
        p = block - group * mine
        total = value + cell(res_ref, p)[...].astype(f32)
        cell(hidden_ref, p)[...] = total
        ones = jnp.ones((8, col), f32)
        sq_own[...] += lax.dot_general(
            ones,
            total * total,
            (((1,), (1,)), ((), ())),
            precision=highest,
            preferred_element_type=f32,
        )

    sq_own[...] = jnp.zeros_like(sq_own)

    @pl.loop(0, slots)
    def _(s):
        block = block_of(s)

        @pl.when(lax.div(block, group) == mine)
        def _():
            settle(block, summed(s, 0))

    @pl.loop(0, slots)
    def _(s):
        @pl.when(lax.div(block_of(s), group) == mine)
        def _():
            sum_out[s] = summed(s, 1).astype(bf16)
            hand_over(s).start()

    @pl.loop(0, slots)
    def _(s):
        block = flip(across, mask_of(s), n)

        @pl.when(lax.div(block, group) == mine)
        def _():
            hand_over(s).wait_recv()
            settle(block, sum_in[s].astype(f32))

    def spread(j, to, slot):
        return remote(sq_own, sq_all.at[slot], q_s.at[j], q_r.at[j], me, to)

    for j in range(1, heads):
        spread(j, lax.rem(mine + j, heads), j).start()
    squares = sq_own[...]
    for j in range(1, heads):
        spread(j, mine, j).wait_recv()
        squares = squares + sq_all[j]
    scale = lax.rsqrt(squares / (col * n) + 1e-06).T[:, 0:1]
    if flat:
        normed_ref[...] = (hidden_ref[...] * scale * norm_ref[...]).astype(bf16)
    else:
        for p in range(group):
            normed_ref[p] = (hidden_ref[p] * scale * norm_ref[p]).astype(bf16)

    for j in range(1, heads):
        spread(j, mine, j).wait_send()
    for p in range(2):
        exchange(p).wait_send()
    for k in range(pieces):
        to_beside(k).wait_send()

    @pl.loop(0, services)
    def _(j):
        q, k = lax.div(j, pieces) + 1, lax.rem(j, pieces)
        to_far(q, k).wait_send()
        pass_far(q, k).wait_send()

    @pl.when(me < n - 1)
    def _():
        for g in range(4):
            chain(g).wait_send()

    @pl.loop(0, slots)
    def _(s):
        own_it = lax.div(block_of(s), group) == mine

        @pl.when(own_it)
        def _():
            hand_over(s).wait_send()

        @pl.when(jnp.logical_not(own_it))
        def _():
            for which in range(2):
                deliver(s, which, mine, 1).wait_send()


def attend(lengths, query, key, value, gain, weight, residual, norm_gain, n, heads):
    rows, feats = query.shape
    col, group, slots = weight.shape[1], n // heads, n // 2
    local, flat = feats // HEAD_DIM, col % 128 == 0
    dma = pltpu.SemaphoreType.DMA
    bf16, f32 = jnp.bfloat16, jnp.float32
    vmem = pl.BlockSpec(memory_space=pltpu.VMEM)
    gain_shape = (1, group * col) if flat else (group, 1, col)
    shape = (rows, group * col) if flat else (group, rows, col)
    if not flat:
        residual = jnp.swapaxes(residual.reshape(rows, group, col), 0, 1)
    hidden, normed = pl.pallas_call(
        functools.partial(attend_kernel, n, heads, flat),
        out_shape=(jax.ShapeDtypeStruct(shape, f32), jax.ShapeDtypeStruct(shape, bf16)),
        in_specs=[pl.BlockSpec(memory_space=pltpu.SMEM)]
        + [vmem] * 4
        + [pl.BlockSpec(memory_space=pl.ANY)]
        + [vmem] * 2,
        out_specs=(vmem, vmem),
        scratch_shapes=[
            pltpu.VMEM((slots,) + weight.shape, bf16),
            pltpu.VMEM((rows, rows), f32),
            pltpu.VMEM((rows, HEAD_DIM), f32),
            pltpu.VMEM((rows, HEAD_DIM), f32),
            pltpu.VMEM((local, HEAD_DIM, HEAD_DIM), f32),
            pltpu.VMEM((local, HEAD_DIM, HEAD_DIM), bf16),
            pltpu.VMEM((local, HEAD_DIM, HEAD_DIM), bf16),
            pltpu.VMEM((rows, feats), f32),
            pltpu.VMEM((2, rows, feats), bf16),
            pltpu.VMEM((2, slots, rows, col), f32),
            pltpu.VMEM((2, slots, rows, col), bf16),
            pltpu.VMEM((2, slots, heads, rows, col), bf16),
            pltpu.VMEM((slots, rows, col), bf16),
            pltpu.VMEM((slots, rows, col), bf16),
            pltpu.VMEM((8, rows), f32),
            pltpu.VMEM((heads, 8, rows), f32),
            dma,
            dma((4,)),
            dma((4,)),
            dma((slots // 2, 4)),
            dma((slots // 2, 4)),
            dma((slots // 2, 4)),
            dma((slots // 2, 4)),
            dma((4,)),
            dma((4,)),
            dma((2,)),
            dma((2,)),
            dma((2, slots)),
            dma((2, slots, heads)),
            dma((slots,)),
            dma((slots,)),
            dma((heads,)),
            dma((heads,)),
        ],
        compiler_params=pltpu.CompilerParams(
            collective_id=2, has_side_effects=True, vmem_limit_bytes=60 * 1024 * 1024
        ),
        name="attend",
    )(lengths, query, key, value, gain, weight, residual, norm_gain.reshape(gain_shape))
    if not flat:
        hidden, normed = (jnp.swapaxes(a, 0, 1).reshape(rows, -1) for a in (hidden, normed))
    return hidden, normed


def on_device(
    query,
    key,
    value,
    episode_lengths,
    attn_gain,
    out_weight,
    residual,
    norm_gain,
    expert_ids,
    route_weights,
    gate_weight,
    up_weight,
    down_weight,
):
    n, heads = lax.axis_size("ctx"), lax.axis_size("head")
    hidden, normed = attend(
        episode_lengths,
        query,
        key,
        value,
        attn_gain[None, :],
        out_weight,
        residual,
        norm_gain,
        n,
        heads,
    )
    return experts(
        hidden,
        normed,
        expert_ids.T,
        route_weights.T,
        gate_weight[0],
        up_weight[0],
        down_weight[0],
        n,
        heads,
    )


def solution(mesh):
    placed = (
        P("ctx", "head"),
        P("ctx", "head"),
        P("ctx", "head"),
        P(),
        P("head"),
        P("head", "ctx"),
        P("ctx", "head"),
        P("head"),
        P("ctx", None),
        P("ctx", None),
        P("ctx", None, "head"),
        P("ctx", None, "head"),
        P("ctx", "head", None),
    )
    return jax.shard_map(
        on_device, mesh=mesh, in_specs=placed, out_specs=P("ctx", "head"), check_vma=False
    )
```

```python
import functools

import jax
import jax.numpy as jnp
from jax import lax
from jax.experimental import pallas as pl
from jax.experimental.pallas import tpu as pltpu
from jax.sharding import PartitionSpec as P

HEAD_DIM = 128
WINDOW = 1
AHEAD = 2


highest = lax.Precision.HIGHEST


MESH = pl.DeviceIdType.MESH


def remote(src, dst, send, recv, ctx, head):
    return pltpu.make_async_remote_copy(
        src_ref=src,
        dst_ref=dst,
        send_sem=send,
        recv_sem=recv,
        device_id=(ctx, head),
        device_id_type=MESH,
    )


def seat():
    head = lax.axis_index("head")
    return lax.axis_index("ctx"), lax.div(head, 2), lax.rem(head, 2)


def flip(me, i, n):
    if n & (n - 1):
        return lax.rem(i - me + 2 * n, n)
    other, bit = me, 1
    while bit < n:
        on = lax.rem(lax.div(me, bit), 2)
        other = other + lax.rem(lax.div(i, bit), 2) * bit * (1 - 2 * on)
        bit *= 2
    return other


def moe_kernel(
    n,
    chips,
    hidden_ref,
    normed_ref,
    ids_ref,
    route_ref,
    gate_ref,
    up_ref,
    down_ref,
    layer_ref,
    gate_w,
    up_w,
    down_w,
    outb,
    full,
    gated,
    part,
    pair,
    out_x,
    in_x,
    total,
    ret,
    acc,
    rank_row,
    rank_col,
    weight_col,
    w_s,
    a_s,
    a_r,
    p_s,
    p_r,
    x_s,
    x_r,
    f_s,
    f_r,
    s_s,
    s_r,
    c_s,
    c_r,
    h_s,
    h_r,
):
    me, chip, core = seat()
    f32, bf16 = jnp.float32, jnp.bfloat16
    tokens, width = normed_ref.shape
    cap = full.shape[1]
    mine, partner = chip * 2 + core, chip * 2 + 1 - core

    weights = [
        pltpu.make_async_copy(gate_ref, gate_w, w_s.at[0]),
        pltpu.make_async_copy(up_ref, up_w, w_s.at[1]),
        pltpu.make_async_copy(down_ref, down_w, w_s.at[2]),
    ]
    for copy in weights:
        copy.start()

    barrier = pltpu.get_barrier_semaphore()

    def tell(ctx, head):
        pl.semaphore_signal(barrier, inc=1, device_id=(ctx, head), device_id_type=MESH)

    tell(me, partner)
    for j in range(1, chips):
        tell(me, lax.rem(chip + j, chips) * 2 + core)

    @pl.loop(1, n)
    def _(i):
        tell(lax.rem(me + i, n), mine)

    expert = lax.broadcasted_iota(jnp.int32, (n, tokens), 0)
    first = ids_ref[0:1, :] == expert
    second = ids_ref[1:2, :] == expert
    raw = route_ref[...].astype(f32)
    shares = raw / (raw[0:1, :] + raw[1:2, :])
    weight = jnp.where(first, shares[0:1, :], 0.0) + jnp.where(second, shares[1:2, :], 0.0)
    named = first | second
    before = (
        lax.broadcasted_iota(jnp.int32, (tokens, tokens), 0)
        < lax.broadcasted_iota(jnp.int32, (tokens, tokens), 1)
    ).astype(f32)
    count = jnp.dot(
        jnp.where(named, 1.0, 0.0).astype(bf16), before.astype(bf16), preferred_element_type=f32
    )
    rank = jnp.where(named, count, -1.0)
    for e in range(n):
        rank_row[e] = jnp.broadcast_to(rank[e : e + 1, :], rank_row.shape[1:])

    def spread_of(i):
        row = rank_row[flip(me, i, n)][0:1, :]
        place = lax.broadcasted_iota(jnp.int32, (cap, tokens), 0).astype(f32)
        chosen = jnp.where(place == row, 1.0, 0.0).astype(bf16)
        return jnp.dot(chosen, normed_ref[...], preferred_element_type=f32).astype(bf16)

    def cell(ref, block, head):
        return ref.at[block, :, pl.ds(pl.multiple_of(head * width, 128), width)]

    full[0, :, pl.ds(pl.multiple_of(mine * width, 128), width)] = spread_of(0)

    pl.semaphore_wait(barrier, chips + n - 1)

    def to_partner(i, head):
        b = cell(full, i, head)
        return remote(b, b, p_s.at[i], p_r.at[i], me, partner)

    def to_chip(i, j):
        b = cell(full, i, mine)
        return remote(b, b, x_s.at[j, i], x_r.at[j, i], me, lax.rem(chip + j, chips) * 2 + core)

    def from_chip(i, j):
        b = cell(full, i, lax.rem(chip - j + chips, chips) * 2 + core)
        return remote(b, b, x_s.at[j, i], x_r.at[j, i], me, partner)

    def forward(i, j, which):
        b = cell(full, i, lax.rem(chip - j + chips, chips) * 2 + which)
        return remote(b, b, f_s.at[j, i], f_r.at[j, i], me, partner)

    def sent(i):
        return remote(
            outb.at[i], cell(full, i, mine), a_s.at[i], a_r.at[i], flip(me, i, n), mine
        )

    def spread(i):
        for j in range(1, chips):
            to_chip(i, j).start()
        to_partner(i, mine).start()

    spread(0)
    rank_col[...] = rank.T
    weight_col[...] = weight.T
    half = n // 2
    share = half // 4

    def issue(i):
        outb[i] = spread_of(i)
        sent(i).start()

    def near(b, body, skip=0):
        @pl.loop(b * share + skip, (b + 1) * share)
        def _(i):
            body(i)

    def far(b, body):
        near(b, lambda i: body(half + i))

    def both(b, body, skip=0):
        far(b, body)
        near(b, body, skip)

    far(0, issue)
    near(0, issue, 1)
    for b in range(1, 4):
        if b < WINDOW:
            far(b, issue)
        near(b, issue)

    def arrive(i):
        sent(i).wait_recv()
        spread(i)

    def arrive_far(b):
        far(b, arrive)
        if b + WINDOW < 4:
            far(b + WINDOW, issue)

    def relay(i):
        for j in range(1, chips):
            from_chip(i, j).wait_recv()
            forward(i, j, core).start()

    def complete(i):
        to_partner(i, partner).wait_recv()
        for j in range(1, chips):
            forward(i, j, 1 - core).wait_recv()

    def pick_rows(b):
        rows = [full[pl.ds(at + b * share, share)] for at in (0, half)]
        return jnp.concatenate([r.reshape(share * cap, r.shape[2]) for r in rows], axis=0)

    def expand(b):
        both(b, complete)
        tile = 256 if gate_w.shape[1] % 256 == 0 else gate_w.shape[1]

        @pl.loop(0, gate_w.shape[1] // tile)
        def _(t):
            rows = pick_rows(b)
            at = pl.ds(pl.multiple_of(t * tile, 128), tile)
            gate = jnp.dot(rows, gate_w[:, at], preferred_element_type=f32)
            up = jnp.dot(rows, up_w[:, at], preferred_element_type=f32)
            gated[:, at] = (gate / (1.0 + jnp.exp(-gate)) * up).astype(bf16)

    def column(j):
        return lax.rem(chip + j, chips)

    def swap(i, j):
        return remote(
            cell(part, i, column(j) * 2 + 1 - core),
            pair.at[i, j],
            s_s.at[j, i],
            s_r.at[j, i],
            me,
            partner,
        )

    def cross(i, j):
        return remote(
            out_x.at[i, j], in_x.at[i, j], c_s.at[j, i], c_r.at[j, i], me, column(j) * 2 + core
        )

    def home(i):
        return remote(total.at[i], ret.at[i], h_s.at[i], h_r.at[i], flip(me, i, n), mine)

    def contract(b):
        tile = 256

        @pl.loop(0, part.shape[2] // tile)
        def _(t):
            at = pl.ds(pl.multiple_of(t * tile, 128), tile)
            value = jnp.dot(gated[...], down_w[:, at], preferred_element_type=f32)
            value = value.astype(bf16).reshape(2, share, cap, tile)
            for side in range(2):
                part[pl.ds(side * half + b * share, share), :, at] = value[side]

        def begin(i):
            for j in list(range(1, chips)) + [0]:
                swap(i, j).start()

        both(b, begin)

    def paired(i, j):
        swap(i, j).wait_recv()
        head = pl.multiple_of((column(j) * 2 + core) * width, 128)
        return part[i, :, pl.ds(head, width)].astype(f32) + pair[i, j].astype(f32)

    def pass_on(i):
        for j in range(1, chips):
            out_x[i, j] = paired(i, j).astype(bf16)
            cross(i, j).start()

    def gather(i):
        value = paired(i, 0)
        for j in range(1, chips):
            cross(i, j).wait_recv()
            value = value + in_x[i, j].astype(f32)
        return value.astype(bf16)

    def send_home(i):
        total[i] = gather(i)
        home(i).start()

    def combine(i):
        e = flip(me, i, n)
        place = lax.broadcasted_iota(jnp.int32, (tokens, cap), 1).astype(f32)
        chosen = lax.broadcasted_iota(jnp.int32, (tokens, n), 1) == e

        def own_column(ref):
            return jnp.sum(jnp.where(chosen, ref[...], 0.0), axis=1, keepdims=True)

        pick = jnp.where(own_column(rank_col) == place, 1.0, 0.0).astype(bf16)
        value = jnp.dot(pick, ret[i], preferred_element_type=f32)
        acc[...] += own_column(weight_col) * value

    def receive(i):
        home(i).wait_recv()
        combine(i)

    near(0, arrive, 1)
    near(1, arrive)
    near(0, relay)
    near(2, arrive)
    arrive_far(0)
    near(1, relay)
    near(3, arrive)
    acc[...] = hidden_ref[...]
    near(2, relay)
    far(0, relay)
    near(3, relay)
    for copy in weights:
        copy.wait()
    for b in range(4):
        expand(b)
        if b < 3:
            arrive_far(b + 1)
        contract(b)
        if b == 1:
            far(0, send_home)
            ret[0] = gather(0)
            near(0, send_home, 1)
        elif b > 1:
            both(b - 1, send_home)
        if b < 3:
            far(b + 1, relay)
        both(b, pass_on)
    combine(0)
    near(0, receive, 1)
    near(1, receive)
    far(0, receive)
    both(3, send_home)
    near(2, receive)
    far(1, receive)
    far(2, receive)
    near(3, receive)
    far(3, receive)
    layer_ref[...] = acc[...].astype(bf16)

    @pl.loop(0, n)
    def _(i):
        to_partner(i, mine).wait_send()
        for j in range(1, chips):
            forward(i, j, core).wait_send()
            to_chip(i, j).wait_send()
            cross(i, j).wait_send()
        for j in range(chips):
            swap(i, j).wait_send()

    @pl.loop(1, n)
    def _(i):
        sent(i).wait_send()
        home(i).wait_send()


def experts(hidden, normed, ids, route, gate, up, down, n, heads):
    chips = heads // 2
    tokens, width = normed.shape
    cap = -(-3 * tokens // n // 16) * 16
    dma = pltpu.SemaphoreType.DMA
    bf16, f32 = jnp.bfloat16, jnp.float32
    vmem, hbm = pl.BlockSpec(memory_space=pltpu.VMEM), pl.BlockSpec(memory_space=pl.ANY)
    block = pltpu.VMEM((n, cap, width), bf16)
    piece = pltpu.VMEM((n, chips, cap, width), bf16)
    wide = pltpu.VMEM((n, cap, width * heads), bf16)
    column = pltpu.VMEM((tokens, n), f32)
    return pl.pallas_call(
        functools.partial(moe_kernel, n, chips),
        out_shape=jax.ShapeDtypeStruct((tokens, width), bf16),
        in_specs=[vmem] * 4 + [hbm] * 3,
        out_specs=vmem,
        scratch_shapes=[
            pltpu.VMEM(gate.shape, gate.dtype),
            pltpu.VMEM(up.shape, up.dtype),
            pltpu.VMEM(down.shape, down.dtype),
            block,
            wide,
            pltpu.VMEM((n // 4 * cap, gate.shape[1]), bf16),
            wide,
            piece,
            piece,
            piece,
            block,
            block,
            pltpu.VMEM((tokens, width), f32),
            pltpu.VMEM((n, 8, tokens), f32),
            column,
            column,
        ]
        + [dma((3,))]
        + [dma((n,))] * 4
        + [dma((chips, n))] * 8
        + [dma((n,))] * 2,
        compiler_params=pltpu.CompilerParams(
            collective_id=0, has_side_effects=True, vmem_limit_bytes=60 * 1024 * 1024
        ),
        name="experts",
    )(hidden, normed, ids, route, gate, up, down)


def attend_kernel(
    n,
    heads,
    flat,
    lengths_ref,
    q_ref,
    k_ref,
    v_ref,
    gain_ref,
    w_ref,
    res_ref,
    norm_ref,
    hidden_ref,
    normed_ref,
    wall,
    allowed,
    keep,
    carry,
    fresh,
    peer,
    before,
    after,
    state,
    attn,
    headed,
    acc,
    mixed,
    parts,
    sum_out,
    sum_in,
    sq_own,
    sq_all,
    here,
    y_s,
    y_r,
    m_s,
    m_r,
    f_s,
    f_r,
    b_s,
    b_r,
    c_s,
    c_r,
    d_s,
    d_r,
    e_s,
    e_r,
    r_s,
    r_r,
    o_s,
    o_r,
    q_s,
    q_r,
):
    me, chip, core = seat()
    mine = chip * 2 + core
    rows, feats = q_ref.shape
    size = HEAD_DIM
    local, slots, group, col = feats // size, n // 2, n // heads, w_ref.shape[1]
    pieces, share = 4, w_ref.shape[0] // 4
    f32, bf16 = jnp.float32, jnp.bfloat16
    beside, across = flip(me, 1, n), flip(me, 2, n)

    barrier = pltpu.get_barrier_semaphore()

    def tell(ctx, head):
        pl.semaphore_signal(barrier, inc=1, device_id=(ctx, head), device_id_type=MESH)

    tell(beside, mine)
    tell(across, mine)
    for q in range(1, slots // 2):
        tell(flip(me, 4 * q, n), mine)
    for step in (1, 2, n - 1, n - 2):
        tell(lax.rem(me + step, n), mine)
    for j in range(1, heads):
        tell(me, lax.rem(mine + j, heads))

    base = me * rows
    starts, last = [0], base + rows - 1
    for e in range(lengths_ref.shape[0] - 1):
        starts.append(starts[-1] + lengths_ref[e])
    open_at, open_before = jnp.int32(0), jnp.int32(0)
    for s in starts[1:]:
        open_at = jnp.where(s <= last, s, open_at)
        open_before = jnp.where(s < base, s, open_before)

    def opened(shape):
        place = lax.broadcasted_iota(jnp.int32, shape, 0) + base
        seg = jnp.zeros(shape, jnp.int32)
        for s in starts[1:]:
            seg = jnp.where(place >= s, s, seg)
        return place, seg

    place, seg = opened((rows, size))
    keep[...] = jnp.where(place >= open_at, 1.0, 0.0)
    carry[...] = jnp.where(seg < base, 1.0, 0.0)
    place, seg = opened((rows, rows))
    source = lax.broadcasted_iota(jnp.int32, (rows, rows), 1) + base
    allowed[...] = jnp.where((source <= place) & (source >= seg), 1.0, 0.0)
    goes_on = jnp.where(open_at < base, 1.0, 0.0)
    went_on = jnp.where(open_before < base - rows, 1.0, 0.0)

    pl.semaphore_wait(barrier, 5 + slots // 2 + heads - 1)

    def strip(k):
        return pl.ds(pl.multiple_of(k * share, 16), share)

    def to_beside(k):
        return remote(w_ref.at[strip(k)], wall.at[1, strip(k)], y_s.at[k], y_r.at[k], beside, mine)

    def to_far(q, k):
        return remote(
            w_ref.at[strip(k)],
            wall.at[2 * q, strip(k)],
            m_s.at[q, k],
            m_r.at[q, k],
            flip(me, 4 * q, n),
            mine,
        )

    def pass_far(q, k):
        return remote(
            wall.at[2 * q, strip(k)],
            wall.at[2 * q + 1, strip(k)],
            f_s.at[q, k],
            f_r.at[q, k],
            beside,
            mine,
        )

    own = pltpu.make_async_copy(w_ref, wall.at[0], here)
    for k in range(AHEAD):
        to_far(1, k).start()
    for k in range(2):
        to_beside(k).start()
    own.start()

    def columns(h):
        return pl.ds(pl.multiple_of(h * size, size), size)

    def lifted(ref, h):
        x = ref[:, columns(h)].astype(f32)
        return x / (1.0 + jnp.exp(-x))

    @pl.loop(0, local)
    def _(h):
        kept = lifted(k_ref, h) * keep[...]
        fresh[h] = jnp.dot(
            kept.T.astype(bf16), v_ref[:, columns(h)], preferred_element_type=f32
        )

    bundle = local // 4

    odd, pair = lax.rem(me, 2), lax.div(me, 2)
    later = pair < n // 2 - 1

    def some(g):
        return pl.ds(g * bundle, bundle)

    def to_peer(g):
        return remote(after.at[some(g)], peer.at[some(g)], b_s.at[g], b_r.at[g], beside, mine)

    def chain(g):
        to = lax.rem(me + 2, n)
        return remote(after.at[some(g)], before.at[some(g)], c_s.at[g], c_r.at[g], to, mine)

    def branch(g):
        to = lax.rem(me + 1, n)
        return remote(after.at[some(g)], before.at[some(g)], d_s.at[g], d_r.at[g], to, mine)

    @pl.when(pair == 0)
    def _():
        before[...] = jnp.zeros_like(before)

    @pl.when(odd == 0)
    def _():
        after[...] = fresh[...].astype(bf16)
        for g in range(4):
            to_peer(g).start()

    def turn():
        @pl.when(odd == 1)
        def _():
            @pl.loop(0, 4)
            def _(g):
                to_peer(g).wait_recv()

                @pl.when(pair > 0)
                def _():
                    chain(g).wait_recv()

                held = peer[some(g)].astype(f32) + went_on * before[some(g)].astype(f32)
                state[some(g)] = held.astype(bf16)

                @pl.when(later)
                def _():
                    after[some(g)] = (fresh[some(g)] + goes_on * held).astype(bf16)
                    chain(g).start()
                    branch(g).start()

        @pl.when(odd == 0)
        def _():
            @pl.when(pair > 0)
            def _():
                for g in range(4):
                    branch(g).wait_recv()

            state[...] = before[...]

    def inside(h):
        scores = lax.dot_general(
            lifted(q_ref, h).astype(bf16),
            lifted(k_ref, h).astype(bf16),
            (((1,), (1,)), ((), ())),
            preferred_element_type=f32,
        )
        attn[:, columns(h)] = jnp.dot(
            (scores * allowed[...]).astype(bf16), v_ref[:, columns(h)], preferred_element_type=f32
        )

    services = pieces * (slots // 2 - 1)
    many = -(-local // services)

    def serve(j):
        q, k = lax.div(j, pieces) + 1, lax.rem(j, pieces)
        to_far(q, k).wait_recv()
        pass_far(q, k).start()

        @pl.when(j + AHEAD < services)
        def _():
            to_far(lax.div(j + AHEAD, pieces) + 1, lax.rem(j + AHEAD, pieces)).start()

        @pl.when(j < pieces - 2)
        def _():
            to_beside(j + 2).start()

    moment = jnp.minimum(lax.div(2 * pair + 1, 3), services - 1)

    def insides(j):
        @pl.loop(j * many, (j + 1) * many)
        def _(h):
            @pl.when(h < local)
            def _():
                inside(h)

    def stage(j):
        @pl.when(j == moment)
        def _():
            turn()

        insides(j + 1)

    insides(0)

    @pl.loop(0, services - 1)
    def _(j):
        stage(j)
        serve(j)

    stage(services - 1)

    part_rows = rows // 2

    def lines(p):
        return pl.ds(p * part_rows, part_rows)

    def finish(h, p):
        x = q_ref[lines(p), columns(h)].astype(f32)
        query = (x / (1.0 + jnp.exp(-x))).astype(bf16)
        outside = jnp.dot(query, state[h], preferred_element_type=f32)
        full = attn[lines(p), columns(h)] + outside * carry[lines(p)]
        mean_square = jnp.mean(full * full, axis=1, keepdims=True)
        scaled = full * lax.rsqrt(mean_square + 1e-06) * gain_ref[:, columns(h)]
        headed[p, :, columns(h)] = scaled.astype(bf16)

    def exchange(p):
        return remote(headed.at[p], headed.at[2 + p], e_s.at[p], e_r.at[p], across, mine)

    for p in range(2):

        @pl.loop(0, local)
        def _(h):
            finish(h, p)

        exchange(p).start()

    def mask_of(s):
        return 4 * lax.div(s, 2) + lax.rem(s, 2)

    def block_of(s):
        return flip(me, mask_of(s), n)

    def deliver(s, which, to, rel):
        return remote(
            mixed.at[which, s],
            parts.at[which, s, rel],
            r_s.at[which, s],
            r_r.at[which, s, rel],
            me,
            to,
        )

    def project(s, which):
        value = jnp.dot(headed[which], wall[s], preferred_element_type=f32)
        owner = lax.div(block_of(s), group)
        acc[which, s] = value

        @pl.when(owner != mine)
        def _():
            mixed[which, s] = value.astype(bf16)
            deliver(s, which, owner, lax.rem(mine - owner + heads, heads)).start()

    own.wait()
    for p in range(2):
        project(0, p)
    for k in range(pieces):
        to_beside(k).wait_recv()
    for p in range(2):
        project(1, p)
    serve(services - 1)

    @pl.loop(2, slots)
    def _(s):
        @pl.when(lax.rem(s, 2) == 1)
        def _():
            for k in range(pieces):
                pass_far(lax.div(s, 2), k).wait_recv()

        for p in range(2):
            project(s, p)

    for p in range(2):
        exchange(p).wait_recv()

        @pl.loop(0, slots)
        def _(s):
            project(s, 2 + p)

    def summed(s, which):
        value = acc[which, s]
        for rel in range(1, heads):
            deliver(s, which, mine, rel).wait_recv()
            value = value + parts[which, s, rel].astype(f32)
        return value

    def cell(ref, c, p):
        if flat:
            return ref.at[lines(p), pl.ds(pl.multiple_of(c * col, 128), col)]
        return ref.at[c, lines(p)]

    def hand_over(s, p):
        return remote(
            sum_out.at[p, s], sum_in.at[p, s], o_s.at[p, s], o_r.at[p, s], across, mine
        )

    def settle(block, p, value):
        c = block - group * mine
        total = value + cell(res_ref, c, p)[...].astype(f32)
        cell(hidden_ref, c, p)[...] = total
        ones = jnp.ones((8, col), f32)
        sq_own[:, lines(p)] += lax.dot_general(
            ones,
            total * total,
            (((1,), (1,)), ((), ())),
            precision=highest,
            preferred_element_type=f32,
        )

    sq_own[...] = jnp.zeros_like(sq_own)

    def reduce_own(p):
        @pl.loop(0, slots)
        def _(s):
            block = block_of(s)

            @pl.when(lax.div(block, group) == mine)
            def _():
                settle(block, p, summed(s, p))

    def reduce_other(p):
        @pl.loop(0, slots)
        def _(s):
            @pl.when(lax.div(block_of(s), group) == mine)
            def _():
                sum_out[p, s] = summed(s, 2 + p).astype(bf16)
                hand_over(s, p).start()

    def take(p):
        @pl.loop(0, slots)
        def _(s):
            block = flip(across, mask_of(s), n)

            @pl.when(lax.div(block, group) == mine)
            def _():
                hand_over(s, p).wait_recv()
                settle(block, p, sum_in[p, s].astype(f32))

    reduce_other(0)
    reduce_own(0)
    reduce_own(1)
    reduce_other(1)
    take(0)
    take(1)

    def spread(j, to, slot):
        return remote(sq_own, sq_all.at[slot], q_s.at[j], q_r.at[j], me, to)

    for j in range(1, heads):
        spread(j, lax.rem(mine + j, heads), j).start()
    squares = sq_own[...]
    for j in range(1, heads):
        spread(j, mine, j).wait_recv()
        squares = squares + sq_all[j]
    scale = lax.rsqrt(squares / (col * n) + 1e-06).T[:, 0:1]
    if flat:
        normed_ref[...] = (hidden_ref[...] * scale * norm_ref[...]).astype(bf16)
    else:
        for p in range(group):
            normed_ref[p] = (hidden_ref[p] * scale * norm_ref[p]).astype(bf16)

    for j in range(1, heads):
        spread(j, mine, j).wait_send()
    for p in range(2):
        exchange(p).wait_send()
    for k in range(pieces):
        to_beside(k).wait_send()

    @pl.loop(0, services)
    def _(j):
        q, k = lax.div(j, pieces) + 1, lax.rem(j, pieces)
        to_far(q, k).wait_send()
        pass_far(q, k).wait_send()

    @pl.when(odd == 0)
    def _():
        for g in range(4):
            to_peer(g).wait_send()

    @pl.when((odd == 1) & later)
    def _():
        for g in range(4):
            chain(g).wait_send()
            branch(g).wait_send()

    @pl.loop(0, slots)
    def _(s):
        own_it = lax.div(block_of(s), group) == mine

        @pl.when(own_it)
        def _():
            for p in range(2):
                hand_over(s, p).wait_send()

        @pl.when(jnp.logical_not(own_it))
        def _():
            for which in range(4):
                deliver(s, which, mine, 1).wait_send()


def attend(lengths, query, key, value, gain, weight, residual, norm_gain, n, heads):
    rows, feats = query.shape
    col, group, slots = weight.shape[1], n // heads, n // 2
    local, flat = feats // HEAD_DIM, col % 128 == 0
    dma = pltpu.SemaphoreType.DMA
    bf16, f32 = jnp.bfloat16, jnp.float32
    vmem = pl.BlockSpec(memory_space=pltpu.VMEM)
    gain_shape = (1, group * col) if flat else (group, 1, col)
    shape = (rows, group * col) if flat else (group, rows, col)
    if not flat:
        residual = jnp.swapaxes(residual.reshape(rows, group, col), 0, 1)
    hidden, normed = pl.pallas_call(
        functools.partial(attend_kernel, n, heads, flat),
        out_shape=(jax.ShapeDtypeStruct(shape, f32), jax.ShapeDtypeStruct(shape, bf16)),
        in_specs=[pl.BlockSpec(memory_space=pltpu.SMEM)]
        + [vmem] * 4
        + [pl.BlockSpec(memory_space=pl.ANY)]
        + [vmem] * 2,
        out_specs=(vmem, vmem),
        scratch_shapes=[
            pltpu.VMEM((slots,) + weight.shape, bf16),
            pltpu.VMEM((rows, rows), f32),
            pltpu.VMEM((rows, HEAD_DIM), f32),
            pltpu.VMEM((rows, HEAD_DIM), f32),
            pltpu.VMEM((local, HEAD_DIM, HEAD_DIM), f32),
        ]
        + [pltpu.VMEM((local, HEAD_DIM, HEAD_DIM), bf16)] * 4
        + [
            pltpu.VMEM((rows, feats), f32),
            pltpu.VMEM((4, rows // 2, feats), bf16),
            pltpu.VMEM((4, slots, rows // 2, col), f32),
            pltpu.VMEM((4, slots, rows // 2, col), bf16),
            pltpu.VMEM((4, slots, heads, rows // 2, col), bf16),
            pltpu.VMEM((2, slots, rows // 2, col), bf16),
            pltpu.VMEM((2, slots, rows // 2, col), bf16),
            pltpu.VMEM((8, rows), f32),
            pltpu.VMEM((heads, 8, rows), f32),
            dma,
            dma((4,)),
            dma((4,)),
            dma((slots // 2, 4)),
            dma((slots // 2, 4)),
            dma((slots // 2, 4)),
            dma((slots // 2, 4)),
            dma((4,)),
            dma((4,)),
            dma((4,)),
            dma((4,)),
            dma((4,)),
            dma((4,)),
            dma((2,)),
            dma((2,)),
            dma((4, slots)),
            dma((4, slots, heads)),
            dma((2, slots)),
            dma((2, slots)),
            dma((heads,)),
            dma((heads,)),
        ],
        compiler_params=pltpu.CompilerParams(
            collective_id=2, has_side_effects=True, vmem_limit_bytes=60 * 1024 * 1024
        ),
        name="attend",
    )(lengths, query, key, value, gain, weight, residual, norm_gain.reshape(gain_shape))
    if not flat:
        hidden, normed = (jnp.swapaxes(a, 0, 1).reshape(rows, -1) for a in (hidden, normed))
    return hidden, normed


def on_device(
    query,
    key,
    value,
    episode_lengths,
    attn_gain,
    out_weight,
    residual,
    norm_gain,
    expert_ids,
    route_weights,
    gate_weight,
    up_weight,
    down_weight,
):
    n, heads = lax.axis_size("ctx"), lax.axis_size("head")
    hidden, normed = attend(
        episode_lengths,
        query,
        key,
        value,
        attn_gain[None, :],
        out_weight,
        residual,
        norm_gain,
        n,
        heads,
    )
    return experts(
        hidden,
        normed,
        expert_ids.T,
        route_weights.T,
        gate_weight[0],
        up_weight[0],
        down_weight[0],
        n,
        heads,
    )


def solution(mesh):
    placed = (
        P("ctx", "head"),
        P("ctx", "head"),
        P("ctx", "head"),
        P(),
        P("head"),
        P("head", "ctx"),
        P("ctx", "head"),
        P("head"),
        P("ctx", None),
        P("ctx", None),
        P("ctx", None, "head"),
        P("ctx", None, "head"),
        P("ctx", "head", None),
    )
    return jax.shard_map(
        on_device, mesh=mesh, in_specs=placed, out_specs=P("ctx", "head"), check_vma=False
    )
```

```python
import functools

import jax
import jax.numpy as jnp
from jax import lax
from jax.experimental import pallas as pl
from jax.experimental.pallas import tpu as pltpu
from jax.sharding import PartitionSpec as P

HEAD_DIM = 128
WINDOW = 1
AHEAD = 2


highest = lax.Precision.HIGHEST


MESH = pl.DeviceIdType.MESH


def remote(src, dst, send, recv, ctx, head):
    return pltpu.make_async_remote_copy(
        src_ref=src,
        dst_ref=dst,
        send_sem=send,
        recv_sem=recv,
        device_id=(ctx, head),
        device_id_type=MESH,
    )


def seat():
    head = lax.axis_index("head")
    return lax.axis_index("ctx"), lax.div(head, 2), lax.rem(head, 2)


def flip(me, i, n):
    if n & (n - 1):
        return lax.rem(i - me + 2 * n, n)
    other, bit = me, 1
    while bit < n:
        on = lax.rem(lax.div(me, bit), 2)
        other = other + lax.rem(lax.div(i, bit), 2) * bit * (1 - 2 * on)
        bit *= 2
    return other


def moe_kernel(
    n,
    chips,
    hidden_ref,
    normed_ref,
    ids_ref,
    route_ref,
    gate_ref,
    up_ref,
    down_ref,
    layer_ref,
    gate_w,
    up_w,
    down_w,
    outb,
    full,
    gated,
    part,
    pair,
    out_x,
    in_x,
    total,
    ret,
    acc,
    rank_row,
    rank_col,
    weight_col,
    w_s,
    a_s,
    a_r,
    p_s,
    p_r,
    x_s,
    x_r,
    f_s,
    f_r,
    s_s,
    s_r,
    c_s,
    c_r,
    h_s,
    h_r,
):
    me, chip, core = seat()
    f32, bf16 = jnp.float32, jnp.bfloat16
    tokens, width = normed_ref.shape
    cap = full.shape[1]
    mine, partner = chip * 2 + core, chip * 2 + 1 - core

    weights = [
        pltpu.make_async_copy(gate_ref, gate_w, w_s.at[0]),
        pltpu.make_async_copy(up_ref, up_w, w_s.at[1]),
        pltpu.make_async_copy(down_ref, down_w, w_s.at[2]),
    ]
    for copy in weights:
        copy.start()

    barrier = pltpu.get_barrier_semaphore()

    def tell(ctx, head):
        pl.semaphore_signal(barrier, inc=1, device_id=(ctx, head), device_id_type=MESH)

    tell(me, partner)
    for j in range(1, chips):
        tell(me, lax.rem(chip + j, chips) * 2 + core)

    @pl.loop(1, n)
    def _(i):
        tell(lax.rem(me + i, n), mine)

    expert = lax.broadcasted_iota(jnp.int32, (n, tokens), 0)
    first = ids_ref[0:1, :] == expert
    second = ids_ref[1:2, :] == expert
    raw = route_ref[...].astype(f32)
    shares = raw / (raw[0:1, :] + raw[1:2, :])
    weight = jnp.where(first, shares[0:1, :], 0.0) + jnp.where(second, shares[1:2, :], 0.0)
    named = first | second
    before = (
        lax.broadcasted_iota(jnp.int32, (tokens, tokens), 0)
        < lax.broadcasted_iota(jnp.int32, (tokens, tokens), 1)
    ).astype(f32)
    count = jnp.dot(
        jnp.where(named, 1.0, 0.0).astype(bf16), before.astype(bf16), preferred_element_type=f32
    )
    rank = jnp.where(named, count, -1.0)
    for e in range(n):
        rank_row[e] = jnp.broadcast_to(rank[e : e + 1, :], rank_row.shape[1:])

    def spread_of(i):
        row = rank_row[flip(me, i, n)][0:1, :]
        place = lax.broadcasted_iota(jnp.int32, (cap, tokens), 0).astype(f32)
        chosen = jnp.where(place == row, 1.0, 0.0).astype(bf16)
        return jnp.dot(chosen, normed_ref[...], preferred_element_type=f32).astype(bf16)

    def cell(ref, block, head):
        return ref.at[block, :, pl.ds(pl.multiple_of(head * width, 128), width)]

    full[0, :, pl.ds(pl.multiple_of(mine * width, 128), width)] = spread_of(0)

    pl.semaphore_wait(barrier, chips + n - 1)

    def to_partner(i, head):
        b = cell(full, i, head)
        return remote(b, b, p_s.at[i], p_r.at[i], me, partner)

    def to_chip(i, j):
        b = cell(full, i, mine)
        return remote(b, b, x_s.at[j, i], x_r.at[j, i], me, lax.rem(chip + j, chips) * 2 + core)

    def from_chip(i, j):
        b = cell(full, i, lax.rem(chip - j + chips, chips) * 2 + core)
        return remote(b, b, x_s.at[j, i], x_r.at[j, i], me, partner)

    def forward(i, j, which):
        b = cell(full, i, lax.rem(chip - j + chips, chips) * 2 + which)
        return remote(b, b, f_s.at[j, i], f_r.at[j, i], me, partner)

    def sent(i):
        return remote(
            outb.at[i], cell(full, i, mine), a_s.at[i], a_r.at[i], flip(me, i, n), mine
        )

    def spread(i):
        for j in range(1, chips):
            to_chip(i, j).start()
        to_partner(i, mine).start()

    spread(0)
    rank_col[...] = rank.T
    weight_col[...] = weight.T
    half = n // 2
    share = half // 4

    def issue(i):
        outb[i] = spread_of(i)
        sent(i).start()

    def near(b, body, skip=0):
        @pl.loop(b * share + skip, (b + 1) * share)
        def _(i):
            body(i)

    def far(b, body):
        near(b, lambda i: body(half + i))

    def both(b, body, skip=0):
        far(b, body)
        near(b, body, skip)

    far(0, issue)
    near(0, issue, 1)
    for b in range(1, 4):
        if b < WINDOW:
            far(b, issue)
        near(b, issue)

    def arrive(i):
        sent(i).wait_recv()
        spread(i)

    def arrive_far(b):
        far(b, arrive)
        if b + WINDOW < 4:
            far(b + WINDOW, issue)

    def relay(i):
        for j in range(1, chips):
            from_chip(i, j).wait_recv()
            forward(i, j, core).start()

    def complete(i):
        to_partner(i, partner).wait_recv()
        for j in range(1, chips):
            forward(i, j, 1 - core).wait_recv()

    def pick_rows(b):
        rows = [full[pl.ds(at + b * share, share)] for at in (0, half)]
        return jnp.concatenate([r.reshape(share * cap, r.shape[2]) for r in rows], axis=0)

    def expand(b):
        both(b, complete)
        tile = 256 if gate_w.shape[1] % 256 == 0 else gate_w.shape[1]

        @pl.loop(0, gate_w.shape[1] // tile)
        def _(t):
            rows = pick_rows(b)
            at = pl.ds(pl.multiple_of(t * tile, 128), tile)
            gate = jnp.dot(rows, gate_w[:, at], preferred_element_type=f32)
            up = jnp.dot(rows, up_w[:, at], preferred_element_type=f32)
            gated[:, at] = (gate / (1.0 + jnp.exp(-gate)) * up).astype(bf16)

    def column(j):
        return lax.rem(chip + j, chips)

    def swap(i, j):
        return remote(
            cell(part, i, column(j) * 2 + 1 - core),
            pair.at[i, j],
            s_s.at[j, i],
            s_r.at[j, i],
            me,
            partner,
        )

    def cross(i, j):
        return remote(
            out_x.at[i, j], in_x.at[i, j], c_s.at[j, i], c_r.at[j, i], me, column(j) * 2 + core
        )

    def home(i):
        return remote(total.at[i], ret.at[i], h_s.at[i], h_r.at[i], flip(me, i, n), mine)

    def contract(b):
        tile = 256

        @pl.loop(0, part.shape[2] // tile)
        def _(t):
            at = pl.ds(pl.multiple_of(t * tile, 128), tile)
            value = jnp.dot(gated[...], down_w[:, at], preferred_element_type=f32)
            value = value.astype(bf16).reshape(2, share, cap, tile)
            for side in range(2):
                part[pl.ds(side * half + b * share, share), :, at] = value[side]

        def begin(i):
            for j in list(range(1, chips)) + [0]:
                swap(i, j).start()

        both(b, begin)

    def paired(i, j):
        swap(i, j).wait_recv()
        head = pl.multiple_of((column(j) * 2 + core) * width, 128)
        return part[i, :, pl.ds(head, width)].astype(f32) + pair[i, j].astype(f32)

    def pass_on(i):
        for j in range(1, chips):
            out_x[i, j] = paired(i, j).astype(bf16)
            cross(i, j).start()

    def gather(i):
        value = paired(i, 0)
        for j in range(1, chips):
            cross(i, j).wait_recv()
            value = value + in_x[i, j].astype(f32)
        return value.astype(bf16)

    def send_home(i):
        total[i] = gather(i)
        home(i).start()

    def combine(i):
        e = flip(me, i, n)
        place = lax.broadcasted_iota(jnp.int32, (tokens, cap), 1).astype(f32)
        chosen = lax.broadcasted_iota(jnp.int32, (tokens, n), 1) == e

        def own_column(ref):
            return jnp.sum(jnp.where(chosen, ref[...], 0.0), axis=1, keepdims=True)

        pick = jnp.where(own_column(rank_col) == place, 1.0, 0.0).astype(bf16)
        value = jnp.dot(pick, ret[i], preferred_element_type=f32)
        acc[...] += own_column(weight_col) * value

    def receive(i):
        home(i).wait_recv()
        combine(i)

    near(0, arrive, 1)
    near(1, arrive)
    near(0, relay)
    near(2, arrive)
    arrive_far(0)
    near(1, relay)
    near(3, arrive)
    acc[...] = hidden_ref[...]
    near(2, relay)
    far(0, relay)
    near(3, relay)
    for copy in weights:
        copy.wait()
    for b in range(4):
        expand(b)
        if b < 3:
            arrive_far(b + 1)
        contract(b)
        if b == 1:
            far(0, send_home)
            ret[0] = gather(0)
            near(0, send_home, 1)
        elif b > 1:
            both(b - 1, send_home)
        if b < 3:
            far(b + 1, relay)
        both(b, pass_on)
    combine(0)
    near(0, receive, 1)
    near(1, receive)
    far(0, receive)
    both(3, send_home)
    near(2, receive)
    far(1, receive)
    far(2, receive)
    near(3, receive)
    far(3, receive)
    layer_ref[...] = acc[...].astype(bf16)

    @pl.loop(0, n)
    def _(i):
        to_partner(i, mine).wait_send()
        for j in range(1, chips):
            forward(i, j, core).wait_send()
            to_chip(i, j).wait_send()
            cross(i, j).wait_send()
        for j in range(chips):
            swap(i, j).wait_send()

    @pl.loop(1, n)
    def _(i):
        sent(i).wait_send()
        home(i).wait_send()


def experts(hidden, normed, ids, route, gate, up, down, n, heads):
    chips = heads // 2
    tokens, width = normed.shape
    cap = -(-3 * tokens // n // 16) * 16
    dma = pltpu.SemaphoreType.DMA
    bf16, f32 = jnp.bfloat16, jnp.float32
    vmem, hbm = pl.BlockSpec(memory_space=pltpu.VMEM), pl.BlockSpec(memory_space=pl.ANY)
    block = pltpu.VMEM((n, cap, width), bf16)
    piece = pltpu.VMEM((n, chips, cap, width), bf16)
    wide = pltpu.VMEM((n, cap, width * heads), bf16)
    column = pltpu.VMEM((tokens, n), f32)
    return pl.pallas_call(
        functools.partial(moe_kernel, n, chips),
        out_shape=jax.ShapeDtypeStruct((tokens, width), bf16),
        in_specs=[vmem] * 4 + [hbm] * 3,
        out_specs=vmem,
        scratch_shapes=[
            pltpu.VMEM(gate.shape, gate.dtype),
            pltpu.VMEM(up.shape, up.dtype),
            pltpu.VMEM(down.shape, down.dtype),
            block,
            wide,
            pltpu.VMEM((n // 4 * cap, gate.shape[1]), bf16),
            wide,
            piece,
            piece,
            piece,
            block,
            block,
            pltpu.VMEM((tokens, width), f32),
            pltpu.VMEM((n, 8, tokens), f32),
            column,
            column,
        ]
        + [dma((3,))]
        + [dma((n,))] * 4
        + [dma((chips, n))] * 8
        + [dma((n,))] * 2,
        compiler_params=pltpu.CompilerParams(
            collective_id=0, has_side_effects=True, vmem_limit_bytes=60 * 1024 * 1024
        ),
        name="experts",
    )(hidden, normed, ids, route, gate, up, down)


def attend_kernel(
    n,
    heads,
    flat,
    lengths_ref,
    q_ref,
    k_ref,
    v_ref,
    gain_ref,
    w_ref,
    res_ref,
    norm_ref,
    hidden_ref,
    normed_ref,
    wall,
    allowed,
    keep,
    carry,
    fresh,
    give,
    peer,
    before,
    after,
    lend,
    state,
    attn,
    headed,
    acc,
    mixed,
    beside_core,
    parts,
    sum_out,
    sum_in,
    sq_own,
    sq_all,
    here,
    y_s,
    y_r,
    m_s,
    m_r,
    f_s,
    f_r,
    b_s,
    b_r,
    c_s,
    c_r,
    d_s,
    d_r,
    e_s,
    e_r,
    k_s,
    k_r,
    r_s,
    r_r,
    o_s,
    o_r,
    q_s,
    q_r,
):
    me, chip, core = seat()
    mine = chip * 2 + core
    rows, feats = q_ref.shape
    size = HEAD_DIM
    local, slots, group, col = feats // size, n // 2, n // heads, w_ref.shape[1]
    chips = heads // 2
    pieces, share = 4, w_ref.shape[0] // 4
    f32, bf16 = jnp.float32, jnp.bfloat16
    beside, across = flip(me, 1, n), flip(me, 2, n)

    barrier = pltpu.get_barrier_semaphore()

    def tell(ctx, head):
        pl.semaphore_signal(barrier, inc=1, device_id=(ctx, head), device_id_type=MESH)

    tell(beside, mine)
    tell(across, mine)
    for q in range(1, slots // 2):
        tell(flip(me, 4 * q, n), mine)
    for step in (2, n - 2):
        tell(lax.rem(me + step, n), mine)
    for j in range(1, heads):
        tell(me, lax.rem(mine + j, heads))

    base = me * rows
    starts, last = [0], base + rows - 1
    for e in range(lengths_ref.shape[0] - 1):
        starts.append(starts[-1] + lengths_ref[e])
    odd, pair = lax.rem(me, 2), lax.div(me, 2)
    middle = (2 * pair + 1) * rows
    open_at, open_middle, open_end = jnp.int32(0), jnp.int32(0), jnp.int32(0)
    for s in starts[1:]:
        open_at = jnp.where(s <= last, s, open_at)
        open_middle = jnp.where(s < middle, s, open_middle)
        open_end = jnp.where(s < middle + rows, s, open_end)

    def opened(shape):
        place = lax.broadcasted_iota(jnp.int32, shape, 0) + base
        seg = jnp.zeros(shape, jnp.int32)
        for s in starts[1:]:
            seg = jnp.where(place >= s, s, seg)
        return place, seg

    place, seg = opened((rows, size))
    keep[...] = jnp.where(place >= open_at, 1.0, 0.0)
    carry[...] = jnp.where(seg < base, 1.0, 0.0)
    place, seg = opened((rows, rows))
    source = lax.broadcasted_iota(jnp.int32, (rows, rows), 1) + base
    allowed[...] = jnp.where((source <= place) & (source >= seg), 1.0, 0.0)
    even_joins = jnp.where(open_middle < middle - rows, 1.0, 0.0)
    odd_joins = jnp.where(open_end < middle, 1.0, 0.0)

    pl.semaphore_wait(barrier, 3 + slots // 2 + heads - 1)

    def strip(k):
        return pl.ds(pl.multiple_of(k * share, 16), share)

    def to_beside(k):
        return remote(w_ref.at[strip(k)], wall.at[1, strip(k)], y_s.at[k], y_r.at[k], beside, mine)

    def to_far(q, k):
        return remote(
            w_ref.at[strip(k)],
            wall.at[2 * q, strip(k)],
            m_s.at[q, k],
            m_r.at[q, k],
            flip(me, 4 * q, n),
            mine,
        )

    def pass_far(q, k):
        return remote(
            wall.at[2 * q, strip(k)],
            wall.at[2 * q + 1, strip(k)],
            f_s.at[q, k],
            f_r.at[q, k],
            beside,
            mine,
        )

    own = pltpu.make_async_copy(w_ref, wall.at[0], here)
    for k in range(AHEAD):
        to_far(1, k).start()
    own.start()

    def columns(h):
        return pl.ds(pl.multiple_of(h * size, size), size)

    def lifted(ref, h):
        x = ref[:, columns(h)].astype(f32)
        return x / (1.0 + jnp.exp(-x))

    def fresh_state(h):
        kept = lifted(k_ref, h) * keep[...]
        return jnp.dot(kept.T.astype(bf16), v_ref[:, columns(h)], preferred_element_type=f32)

    half = local // 2
    bundle = half // 2
    mine_at, other_at = odd * half, (1 - odd) * half

    def some(g):
        return pl.ds(g * bundle, bundle)

    def my_some(g):
        return pl.ds(mine_at + g * bundle, bundle)

    def to_peer(g):
        return remote(give.at[some(g)], peer.at[some(g)], b_s.at[g], b_r.at[g], beside, mine)

    def chain(g):
        to = lax.rem(me + 2, n)
        return remote(after.at[some(g)], before.at[some(g)], c_s.at[g], c_r.at[g], to, mine)

    def to_state(g):
        return remote(lend.at[some(g)], state.at[my_some(g)], d_s.at[g], d_r.at[g], beside, mine)

    for g in range(2):

        @pl.loop(g * bundle, (g + 1) * bundle)
        def _(i):
            give[i] = fresh_state(other_at + i).astype(bf16)

        to_peer(g).start()

    for k in range(2):
        to_beside(k).start()

    @pl.loop(0, half)
    def _(i):
        fresh[i] = fresh_state(mine_at + i)

    @pl.when(pair == 0)
    def _():
        before[...] = jnp.zeros_like(before)

    def turn():
        @pl.loop(0, 2)
        def _(g):
            to_peer(g).wait_recv()

            @pl.when(pair > 0)
            def _():
                chain(g).wait_recv()

            held, theirs = fresh[some(g)], peer[some(g)].astype(f32)
            past = before[some(g)].astype(f32)
            between = jnp.where(odd == 0, held, theirs) + even_joins * past

            @pl.when(pair < n // 2 - 1)
            def _():
                total = jnp.where(odd == 0, theirs, held) + odd_joins * between
                after[some(g)] = total.astype(bf16)
                chain(g).start()

            lend[some(g)] = jnp.where(odd == 0, between, past).astype(bf16)
            to_state(g).start()
            state[my_some(g)] = jnp.where(odd == 0, past, between).astype(bf16)

    def inside(h):
        scores = lax.dot_general(
            lifted(q_ref, h).astype(bf16),
            lifted(k_ref, h).astype(bf16),
            (((1,), (1,)), ((), ())),
            preferred_element_type=f32,
        )
        attn[:, columns(h)] = jnp.dot(
            (scores * allowed[...]).astype(bf16), v_ref[:, columns(h)], preferred_element_type=f32
        )

    services = pieces * (slots // 2 - 1)
    many = -(-local // services)

    def serve(j):
        q, k = lax.div(j, pieces) + 1, lax.rem(j, pieces)
        to_far(q, k).wait_recv()
        pass_far(q, k).start()

        @pl.when(j + AHEAD < services)
        def _():
            to_far(lax.div(j + AHEAD, pieces) + 1, lax.rem(j + AHEAD, pieces)).start()

        @pl.when(j < pieces - 2)
        def _():
            to_beside(j + 2).start()

    moment = jnp.minimum(lax.div(2 * pair + 1, 3), services - 2)

    def insides(j):
        @pl.loop(j * many, (j + 1) * many)
        def _(h):
            @pl.when(h < local)
            def _():
                inside(h)

    def stage(j):
        @pl.when(j == moment)
        def _():
            turn()

        insides(j + 1)

    insides(0)

    @pl.loop(0, services - 2)
    def _(j):
        stage(j)
        serve(j)

    stage(services - 2)
    for g in range(2):
        to_state(g).wait_recv()

    part_rows = rows // 2

    def lines(p):
        return pl.ds(p * part_rows, part_rows)

    def finish(h, p):
        x = q_ref[lines(p), columns(h)].astype(f32)
        query = (x / (1.0 + jnp.exp(-x))).astype(bf16)
        outside = jnp.dot(query, state[h], preferred_element_type=f32)
        full = attn[lines(p), columns(h)] + outside * carry[lines(p)]
        mean_square = jnp.mean(full * full, axis=1, keepdims=True)
        scaled = full * lax.rsqrt(mean_square + 1e-06) * gain_ref[:, columns(h)]
        headed[p, :, columns(h)] = scaled.astype(bf16)

    def exchange(p):
        return remote(headed.at[p], headed.at[2 + p], e_s.at[p], e_r.at[p], across, mine)

    for p in range(2):

        @pl.loop(0, local)
        def _(h):
            finish(h, p)

        exchange(p).start()

    def mask_of(s):
        return 4 * lax.div(s, 2) + lax.rem(s, 2)

    def block_of(s):
        return flip(me, mask_of(s), n)

    def owner_of(s):
        head = lax.div(block_of(s), group)
        return lax.div(head, 2), lax.rem(head, 2)

    def to_core(s, u):
        return remote(
            mixed.at[u, s],
            beside_core.at[u, s],
            k_s.at[u, s],
            k_r.at[u, s],
            me,
            chip * 2 + 1 - core,
        )

    def to_owner(s, u, to, rel):
        return remote(
            mixed.at[u, s], parts.at[u, s, rel], r_s.at[u, s], r_r.at[u, s, rel], me, to
        )

    def project(s, u):
        value = jnp.dot(headed[u], wall[s], preferred_element_type=f32)
        acc[u, s] = value

        @pl.when(owner_of(s)[1] != core)
        def _():
            mixed[u, s] = value.astype(bf16)
            to_core(s, u).start()

    def presum(s, u):
        owner_chip, owner_core = owner_of(s)

        @pl.when(owner_core == core)
        def _():
            to_core(s, u).wait_recv()
            value = acc[u, s] + beside_core[u, s].astype(f32)
            acc[u, s] = value

            @pl.when(owner_chip != chip)
            def _():
                mixed[u, s] = value.astype(bf16)
                rel = lax.rem(chip - owner_chip + chips, chips)
                to_owner(s, u, owner_chip * 2 + core, rel).start()

    def work(low, high, units):
        for u in units:

            @pl.loop(low, high)
            def _(s):
                project(s, u)

        for u in units:

            @pl.loop(low, high)
            def _(s):
                presum(s, u)

    own.wait()
    for k in range(pieces):
        to_beside(k).wait_recv()
    work(0, 2, (0, 1))
    serve(services - 2)
    serve(services - 1)
    exchange(0).wait_recv()
    work(0, 2, (2,))

    @pl.loop(1, slots // 2)
    def _(q):
        for k in range(pieces):
            pass_far(q, k).wait_recv()

    work(2, slots, (2,))
    exchange(1).wait_recv()
    work(0, slots, (3,))
    work(2, slots, (0, 1))

    def summed(s, u):
        value = acc[u, s]
        for rel in range(1, chips):
            to_owner(s, u, mine, rel).wait_recv()
            value = value + parts[u, s, rel].astype(f32)
        return value

    def cell(ref, c, p):
        if flat:
            return ref.at[lines(p), pl.ds(pl.multiple_of(c * col, 128), col)]
        return ref.at[c, lines(p)]

    def hand_over(s, p):
        return remote(
            sum_out.at[p, s], sum_in.at[p, s], o_s.at[p, s], o_r.at[p, s], across, mine
        )

    def settle(block, p, value):
        c = block - group * mine
        total = value + cell(res_ref, c, p)[...].astype(f32)
        cell(hidden_ref, c, p)[...] = total
        ones = jnp.ones((8, col), f32)
        sq_own[:, lines(p)] += lax.dot_general(
            ones,
            total * total,
            (((1,), (1,)), ((), ())),
            precision=highest,
            preferred_element_type=f32,
        )

    sq_own[...] = jnp.zeros_like(sq_own)

    def reduce_own(p):
        @pl.loop(0, slots)
        def _(s):
            block = block_of(s)

            @pl.when(lax.div(block, group) == mine)
            def _():
                settle(block, p, summed(s, p))

    def reduce_other(p):
        @pl.loop(0, slots)
        def _(s):
            @pl.when(lax.div(block_of(s), group) == mine)
            def _():
                sum_out[p, s] = summed(s, 2 + p).astype(bf16)
                hand_over(s, p).start()

    def take(p):
        @pl.loop(0, slots)
        def _(s):
            block = flip(across, mask_of(s), n)

            @pl.when(lax.div(block, group) == mine)
            def _():
                hand_over(s, p).wait_recv()
                settle(block, p, sum_in[p, s].astype(f32))

    reduce_other(0)
    reduce_other(1)
    reduce_own(0)
    reduce_own(1)
    take(0)
    take(1)

    def spread(j, to, slot):
        return remote(sq_own, sq_all.at[slot], q_s.at[j], q_r.at[j], me, to)

    for j in range(1, heads):
        spread(j, lax.rem(mine + j, heads), j).start()
    squares = sq_own[...]
    for j in range(1, heads):
        spread(j, mine, j).wait_recv()
        squares = squares + sq_all[j]
    scale = lax.rsqrt(squares / (col * n) + 1e-06).T[:, 0:1]
    if flat:
        normed_ref[...] = (hidden_ref[...] * scale * norm_ref[...]).astype(bf16)
    else:
        for p in range(group):
            normed_ref[p] = (hidden_ref[p] * scale * norm_ref[p]).astype(bf16)

    for j in range(1, heads):
        spread(j, mine, j).wait_send()
    for p in range(2):
        exchange(p).wait_send()
    for k in range(pieces):
        to_beside(k).wait_send()

    @pl.loop(0, services)
    def _(j):
        q, k = lax.div(j, pieces) + 1, lax.rem(j, pieces)
        to_far(q, k).wait_send()
        pass_far(q, k).wait_send()

    for g in range(2):
        to_peer(g).wait_send()
        to_state(g).wait_send()

    @pl.when(pair < n // 2 - 1)
    def _():
        for g in range(2):
            chain(g).wait_send()

    @pl.loop(0, slots)
    def _(s):
        owner_chip, owner_core = owner_of(s)
        relay = owner_core == core

        @pl.when(jnp.logical_not(relay))
        def _():
            for u in range(4):
                to_core(s, u).wait_send()

        @pl.when(relay & (owner_chip != chip))
        def _():
            for u in range(4):
                to_owner(s, u, mine, 0).wait_send()

        @pl.when(relay & (owner_chip == chip))
        def _():
            for p in range(2):
                hand_over(s, p).wait_send()


def attend(lengths, query, key, value, gain, weight, residual, norm_gain, n, heads):
    rows, feats = query.shape
    col, group, slots = weight.shape[1], n // heads, n // 2
    local, flat = feats // HEAD_DIM, col % 128 == 0
    dma = pltpu.SemaphoreType.DMA
    bf16, f32 = jnp.bfloat16, jnp.float32
    vmem = pl.BlockSpec(memory_space=pltpu.VMEM)
    gain_shape = (1, group * col) if flat else (group, 1, col)
    shape = (rows, group * col) if flat else (group, rows, col)
    if not flat:
        residual = jnp.swapaxes(residual.reshape(rows, group, col), 0, 1)
    hidden, normed = pl.pallas_call(
        functools.partial(attend_kernel, n, heads, flat),
        out_shape=(jax.ShapeDtypeStruct(shape, f32), jax.ShapeDtypeStruct(shape, bf16)),
        in_specs=[pl.BlockSpec(memory_space=pltpu.SMEM)]
        + [vmem] * 4
        + [pl.BlockSpec(memory_space=pl.ANY)]
        + [vmem] * 2,
        out_specs=(vmem, vmem),
        scratch_shapes=[
            pltpu.VMEM((slots,) + weight.shape, bf16),
            pltpu.VMEM((rows, rows), f32),
            pltpu.VMEM((rows, HEAD_DIM), f32),
            pltpu.VMEM((rows, HEAD_DIM), f32),
            pltpu.VMEM((local // 2, HEAD_DIM, HEAD_DIM), f32),
        ]
        + [pltpu.VMEM((local // 2, HEAD_DIM, HEAD_DIM), bf16)] * 5
        + [
            pltpu.VMEM((local, HEAD_DIM, HEAD_DIM), bf16),
            pltpu.VMEM((rows, feats), f32),
            pltpu.VMEM((4, rows // 2, feats), bf16),
            pltpu.VMEM((4, slots, rows // 2, col), f32),
            pltpu.VMEM((4, slots, rows // 2, col), bf16),
            pltpu.VMEM((4, slots, rows // 2, col), bf16),
            pltpu.VMEM((4, slots, heads // 2, rows // 2, col), bf16),
            pltpu.VMEM((2, slots, rows // 2, col), bf16),
            pltpu.VMEM((2, slots, rows // 2, col), bf16),
            pltpu.VMEM((8, rows), f32),
            pltpu.VMEM((heads, 8, rows), f32),
            dma,
            dma((4,)),
            dma((4,)),
            dma((slots // 2, 4)),
            dma((slots // 2, 4)),
            dma((slots // 2, 4)),
            dma((slots // 2, 4)),
            dma((2,)),
            dma((2,)),
            dma((2,)),
            dma((2,)),
            dma((2,)),
            dma((2,)),
            dma((2,)),
            dma((2,)),
            dma((4, slots)),
            dma((4, slots)),
            dma((4, slots)),
            dma((4, slots, heads // 2)),
            dma((2, slots)),
            dma((2, slots)),
            dma((heads,)),
            dma((heads,)),
        ],
        compiler_params=pltpu.CompilerParams(
            collective_id=2, has_side_effects=True, vmem_limit_bytes=60 * 1024 * 1024
        ),
        name="attend",
    )(lengths, query, key, value, gain, weight, residual, norm_gain.reshape(gain_shape))
    if not flat:
        hidden, normed = (jnp.swapaxes(a, 0, 1).reshape(rows, -1) for a in (hidden, normed))
    return hidden, normed


def on_device(
    query,
    key,
    value,
    episode_lengths,
    attn_gain,
    out_weight,
    residual,
    norm_gain,
    expert_ids,
    route_weights,
    gate_weight,
    up_weight,
    down_weight,
):
    n, heads = lax.axis_size("ctx"), lax.axis_size("head")
    hidden, normed = attend(
        episode_lengths,
        query,
        key,
        value,
        attn_gain[None, :],
        out_weight,
        residual,
        norm_gain,
        n,
        heads,
    )
    return experts(
        hidden,
        normed,
        expert_ids.T,
        route_weights.T,
        gate_weight[0],
        up_weight[0],
        down_weight[0],
        n,
        heads,
    )


def solution(mesh):
    placed = (
        P("ctx", "head"),
        P("ctx", "head"),
        P("ctx", "head"),
        P(),
        P("head"),
        P("head", "ctx"),
        P("ctx", "head"),
        P("head"),
        P("ctx", None),
        P("ctx", None),
        P("ctx", None, "head"),
        P("ctx", None, "head"),
        P("ctx", "head", None),
    )
    return jax.shard_map(
        on_device, mesh=mesh, in_specs=placed, out_specs=P("ctx", "head"), check_vma=False
    )
```

```python
import functools

import jax
import jax.numpy as jnp
from jax import lax
from jax.experimental import pallas as pl
from jax.experimental.pallas import tpu as pltpu
from jax.sharding import PartitionSpec as P

HEAD_DIM = 128
WINDOW = 1
AHEAD = 2


highest = lax.Precision.HIGHEST


MESH = pl.DeviceIdType.MESH


def remote(src, dst, send, recv, ctx, head):
    return pltpu.make_async_remote_copy(
        src_ref=src,
        dst_ref=dst,
        send_sem=send,
        recv_sem=recv,
        device_id=(ctx, head),
        device_id_type=MESH,
    )


def seat():
    head = lax.axis_index("head")
    return lax.axis_index("ctx"), lax.div(head, 2), lax.rem(head, 2)


def flip(me, i, n):
    if n & (n - 1):
        return lax.rem(i - me + 2 * n, n)
    other, bit = me, 1
    while bit < n:
        on = lax.rem(lax.div(me, bit), 2)
        other = other + lax.rem(lax.div(i, bit), 2) * bit * (1 - 2 * on)
        bit *= 2
    return other


def moe_kernel(
    n,
    chips,
    hidden_ref,
    normed_ref,
    ids_ref,
    route_ref,
    gate_ref,
    up_ref,
    down_ref,
    layer_ref,
    gate_w,
    up_w,
    down_w,
    outb,
    full,
    gated,
    part,
    pair,
    out_x,
    in_x,
    total,
    ret,
    acc,
    rank_row,
    rank_col,
    weight_col,
    w_s,
    a_s,
    a_r,
    p_s,
    p_r,
    x_s,
    x_r,
    f_s,
    f_r,
    s_s,
    s_r,
    c_s,
    c_r,
    h_s,
    h_r,
):
    me, chip, core = seat()
    f32, bf16 = jnp.float32, jnp.bfloat16
    tokens, width = normed_ref.shape
    cap = full.shape[1]
    mine, partner = chip * 2 + core, chip * 2 + 1 - core

    weights = [
        pltpu.make_async_copy(gate_ref, gate_w, w_s.at[0]),
        pltpu.make_async_copy(up_ref, up_w, w_s.at[1]),
        pltpu.make_async_copy(down_ref, down_w, w_s.at[2]),
    ]
    for copy in weights:
        copy.start()

    barrier = pltpu.get_barrier_semaphore()

    def tell(ctx, head):
        pl.semaphore_signal(barrier, inc=1, device_id=(ctx, head), device_id_type=MESH)

    tell(me, partner)
    for j in range(1, chips):
        tell(me, lax.rem(chip + j, chips) * 2 + core)

    @pl.loop(1, n)
    def _(i):
        tell(lax.rem(me + i, n), mine)

    expert = lax.broadcasted_iota(jnp.int32, (n, tokens), 0)
    first = ids_ref[0:1, :] == expert
    second = ids_ref[1:2, :] == expert
    raw = route_ref[...].astype(f32)
    shares = raw / (raw[0:1, :] + raw[1:2, :])
    weight = jnp.where(first, shares[0:1, :], 0.0) + jnp.where(second, shares[1:2, :], 0.0)
    named = first | second
    before = (
        lax.broadcasted_iota(jnp.int32, (tokens, tokens), 0)
        < lax.broadcasted_iota(jnp.int32, (tokens, tokens), 1)
    ).astype(f32)
    count = jnp.dot(
        jnp.where(named, 1.0, 0.0).astype(bf16), before.astype(bf16), preferred_element_type=f32
    )
    rank = jnp.where(named, count, -1.0)
    for e in range(n):
        rank_row[e] = jnp.broadcast_to(rank[e : e + 1, :], rank_row.shape[1:])

    def spread_of(i):
        row = rank_row[flip(me, i, n)][0:1, :]
        place = lax.broadcasted_iota(jnp.int32, (cap, tokens), 0).astype(f32)
        chosen = jnp.where(place == row, 1.0, 0.0).astype(bf16)
        return jnp.dot(chosen, normed_ref[...], preferred_element_type=f32).astype(bf16)

    def cell(ref, block, head):
        return ref.at[block, :, pl.ds(pl.multiple_of(head * width, 128), width)]

    full[0, :, pl.ds(pl.multiple_of(mine * width, 128), width)] = spread_of(0)

    pl.semaphore_wait(barrier, chips + n - 1)

    def to_partner(i, head):
        b = cell(full, i, head)
        return remote(b, b, p_s.at[i], p_r.at[i], me, partner)

    def to_chip(i, j):
        b = cell(full, i, mine)
        return remote(b, b, x_s.at[j, i], x_r.at[j, i], me, lax.rem(chip + j, chips) * 2 + core)

    def from_chip(i, j):
        b = cell(full, i, lax.rem(chip - j + chips, chips) * 2 + core)
        return remote(b, b, x_s.at[j, i], x_r.at[j, i], me, partner)

    def forward(i, j, which):
        b = cell(full, i, lax.rem(chip - j + chips, chips) * 2 + which)
        return remote(b, b, f_s.at[j, i], f_r.at[j, i], me, partner)

    def sent(i):
        return remote(
            outb.at[i], cell(full, i, mine), a_s.at[i], a_r.at[i], flip(me, i, n), mine
        )

    def spread(i):
        for j in range(1, chips):
            to_chip(i, j).start()
        to_partner(i, mine).start()

    spread(0)
    rank_col[...] = rank.T
    weight_col[...] = weight.T
    half = n // 2
    share = half // 4

    def issue(i):
        outb[i] = spread_of(i)
        sent(i).start()

    def near(b, body, skip=0):
        @pl.loop(b * share + skip, (b + 1) * share)
        def _(i):
            body(i)

    def far(b, body):
        near(b, lambda i: body(half + i))

    def both(b, body, skip=0):
        far(b, body)
        near(b, body, skip)

    far(0, issue)
    near(0, issue, 1)
    for b in range(1, 4):
        if b < WINDOW:
            far(b, issue)
        near(b, issue)

    def arrive(i):
        sent(i).wait_recv()
        spread(i)

    def arrive_far(b):
        far(b, arrive)
        if b + WINDOW < 4:
            far(b + WINDOW, issue)

    def relay(i):
        for j in range(1, chips):
            from_chip(i, j).wait_recv()
            forward(i, j, core).start()

    def complete(i):
        to_partner(i, partner).wait_recv()
        for j in range(1, chips):
            forward(i, j, 1 - core).wait_recv()

    def pick_rows(b):
        rows = [full[pl.ds(at + b * share, share)] for at in (0, half)]
        return jnp.concatenate([r.reshape(share * cap, r.shape[2]) for r in rows], axis=0)

    def expand(b):
        both(b, complete)
        tile = 256 if gate_w.shape[1] % 256 == 0 else gate_w.shape[1]

        @pl.loop(0, gate_w.shape[1] // tile)
        def _(t):
            rows = pick_rows(b)
            at = pl.ds(pl.multiple_of(t * tile, 128), tile)
            gate = jnp.dot(rows, gate_w[:, at], preferred_element_type=f32)
            up = jnp.dot(rows, up_w[:, at], preferred_element_type=f32)
            gated[:, at] = (gate / (1.0 + jnp.exp(-gate)) * up).astype(bf16)

    def column(j):
        return lax.rem(chip + j, chips)

    def swap(i, j):
        return remote(
            cell(part, i, column(j) * 2 + 1 - core),
            pair.at[i, j],
            s_s.at[j, i],
            s_r.at[j, i],
            me,
            partner,
        )

    def cross(i, j):
        return remote(
            out_x.at[i, j], in_x.at[i, j], c_s.at[j, i], c_r.at[j, i], me, column(j) * 2 + core
        )

    def home(i):
        return remote(total.at[i], ret.at[i], h_s.at[i], h_r.at[i], flip(me, i, n), mine)

    def contract(b):
        tile = 256

        @pl.loop(0, part.shape[2] // tile)
        def _(t):
            at = pl.ds(pl.multiple_of(t * tile, 128), tile)
            value = jnp.dot(gated[...], down_w[:, at], preferred_element_type=f32)
            value = value.astype(bf16).reshape(2, share, cap, tile)
            for side in range(2):
                part[pl.ds(side * half + b * share, share), :, at] = value[side]

        def begin(i):
            for j in list(range(1, chips)) + [0]:
                swap(i, j).start()

        both(b, begin)

    def paired(i, j):
        swap(i, j).wait_recv()
        head = pl.multiple_of((column(j) * 2 + core) * width, 128)
        return part[i, :, pl.ds(head, width)].astype(f32) + pair[i, j].astype(f32)

    def pass_on(i):
        for j in range(1, chips):
            out_x[i, j] = paired(i, j).astype(bf16)
            cross(i, j).start()

    def gather(i):
        value = paired(i, 0)
        for j in range(1, chips):
            cross(i, j).wait_recv()
            value = value + in_x[i, j].astype(f32)
        return value.astype(bf16)

    def send_home(i):
        total[i] = gather(i)
        home(i).start()

    def combine(i):
        e = flip(me, i, n)
        place = lax.broadcasted_iota(jnp.int32, (tokens, cap), 1).astype(f32)
        chosen = lax.broadcasted_iota(jnp.int32, (tokens, n), 1) == e

        def own_column(ref):
            return jnp.sum(jnp.where(chosen, ref[...], 0.0), axis=1, keepdims=True)

        pick = jnp.where(own_column(rank_col) == place, 1.0, 0.0).astype(bf16)
        value = jnp.dot(pick, ret[i], preferred_element_type=f32)
        acc[...] += own_column(weight_col) * value

    def receive(i):
        home(i).wait_recv()
        combine(i)

    near(0, arrive, 1)
    near(1, arrive)
    near(0, relay)
    near(2, arrive)
    arrive_far(0)
    near(1, relay)
    near(3, arrive)
    acc[...] = hidden_ref[...]
    near(2, relay)
    far(0, relay)
    near(3, relay)
    for copy in weights:
        copy.wait()
    for b in range(4):
        expand(b)
        if b < 3:
            arrive_far(b + 1)
        contract(b)
        if b == 1:
            far(0, send_home)
            ret[0] = gather(0)
            near(0, send_home, 1)
        elif b > 1:
            both(b - 1, send_home)
        if b < 3:
            far(b + 1, relay)
        both(b, pass_on)
    combine(0)
    near(0, receive, 1)
    near(1, receive)
    far(0, receive)
    both(3, send_home)
    near(2, receive)
    far(1, receive)
    far(2, receive)
    near(3, receive)
    far(3, receive)
    layer_ref[...] = acc[...].astype(bf16)

    @pl.loop(0, n)
    def _(i):
        to_partner(i, mine).wait_send()
        for j in range(1, chips):
            forward(i, j, core).wait_send()
            to_chip(i, j).wait_send()
            cross(i, j).wait_send()
        for j in range(chips):
            swap(i, j).wait_send()

    @pl.loop(1, n)
    def _(i):
        sent(i).wait_send()
        home(i).wait_send()


def experts(hidden, normed, ids, route, gate, up, down, n, heads):
    chips = heads // 2
    tokens, width = normed.shape
    cap = -(-3 * tokens // n // 16) * 16
    dma = pltpu.SemaphoreType.DMA
    bf16, f32 = jnp.bfloat16, jnp.float32
    vmem, hbm = pl.BlockSpec(memory_space=pltpu.VMEM), pl.BlockSpec(memory_space=pl.ANY)
    block = pltpu.VMEM((n, cap, width), bf16)
    piece = pltpu.VMEM((n, chips, cap, width), bf16)
    wide = pltpu.VMEM((n, cap, width * heads), bf16)
    column = pltpu.VMEM((tokens, n), f32)
    return pl.pallas_call(
        functools.partial(moe_kernel, n, chips),
        out_shape=jax.ShapeDtypeStruct((tokens, width), bf16),
        in_specs=[vmem] * 4 + [hbm] * 3,
        out_specs=vmem,
        scratch_shapes=[
            pltpu.VMEM(gate.shape, gate.dtype),
            pltpu.VMEM(up.shape, up.dtype),
            pltpu.VMEM(down.shape, down.dtype),
            block,
            wide,
            pltpu.VMEM((n // 4 * cap, gate.shape[1]), bf16),
            wide,
            piece,
            piece,
            piece,
            block,
            block,
            pltpu.VMEM((tokens, width), f32),
            pltpu.VMEM((n, 8, tokens), f32),
            column,
            column,
        ]
        + [dma((3,))]
        + [dma((n,))] * 4
        + [dma((chips, n))] * 8
        + [dma((n,))] * 2,
        compiler_params=pltpu.CompilerParams(
            collective_id=0, has_side_effects=True, vmem_limit_bytes=60 * 1024 * 1024
        ),
        name="experts",
    )(hidden, normed, ids, route, gate, up, down)


def attend_kernel(
    n,
    heads,
    flat,
    lengths_ref,
    q_ref,
    k_ref,
    v_ref,
    gain_ref,
    w_ref,
    res_ref,
    norm_ref,
    hidden_ref,
    normed_ref,
    wall,
    allowed,
    keep,
    carry,
    fresh,
    give,
    peer,
    before,
    after,
    lend,
    state,
    attn,
    headed,
    acc,
    mixed,
    beside_core,
    parts,
    sum_out,
    sum_in,
    sq_own,
    sq_all,
    here,
    y_s,
    y_r,
    m_s,
    m_r,
    f_s,
    f_r,
    b_s,
    b_r,
    c_s,
    c_r,
    d_s,
    d_r,
    e_s,
    e_r,
    k_s,
    k_r,
    r_s,
    r_r,
    o_s,
    o_r,
    q_s,
    q_r,
):
    me, chip, core = seat()
    mine = chip * 2 + core
    rows, feats = q_ref.shape
    size = HEAD_DIM
    local, slots, group, col = feats // size, n // 2, n // heads, w_ref.shape[1]
    chips = heads // 2
    strips, width = wall.shape[1], wall.shape[3]
    pieces, share = 2 * strips, w_ref.shape[0] // 2
    f32, bf16 = jnp.float32, jnp.bfloat16
    beside, across = flip(me, 1, n), flip(me, 2, n)

    own = [
        pltpu.make_async_copy(
            w_ref.at[:, pl.ds(c * width, width)], wall.at[0, c], here.at[c]
        )
        for c in range(strips)
    ]
    for copy in own:
        copy.start()

    barrier = pltpu.get_barrier_semaphore()

    def tell(ctx, head):
        pl.semaphore_signal(barrier, inc=1, device_id=(ctx, head), device_id_type=MESH)

    tell(beside, mine)
    tell(across, mine)
    for q in range(1, slots // 2):
        tell(flip(me, 4 * q, n), mine)
    for step in (2, n - 2):
        tell(lax.rem(me + step, n), mine)
    for j in range(1, heads):
        tell(me, lax.rem(mine + j, heads))

    base = me * rows
    starts, last = [0], base + rows - 1
    for e in range(lengths_ref.shape[0] - 1):
        starts.append(starts[-1] + lengths_ref[e])
    odd, pair = lax.rem(me, 2), lax.div(me, 2)
    middle = (2 * pair + 1) * rows
    open_at, open_middle, open_end = jnp.int32(0), jnp.int32(0), jnp.int32(0)
    for s in starts[1:]:
        open_at = jnp.where(s <= last, s, open_at)
        open_middle = jnp.where(s < middle, s, open_middle)
        open_end = jnp.where(s < middle + rows, s, open_end)

    def opened(shape):
        place = lax.broadcasted_iota(jnp.int32, shape, 0) + base
        seg = jnp.zeros(shape, jnp.int32)
        for s in starts[1:]:
            seg = jnp.where(place >= s, s, seg)
        return place, seg

    place, seg = opened((rows, size))
    keep[...] = jnp.where(place >= open_at, 1.0, 0.0)
    carry[...] = jnp.where(seg < base, 1.0, 0.0)
    place, seg = opened((rows, rows))
    source = lax.broadcasted_iota(jnp.int32, (rows, rows), 1) + base
    allowed[...] = jnp.where((source <= place) & (source >= seg), 1.0, 0.0)
    even_joins = jnp.where(open_middle < middle - rows, 1.0, 0.0)
    odd_joins = jnp.where(open_end < middle, 1.0, 0.0)

    pl.semaphore_wait(barrier, 3 + slots // 2 + heads - 1)

    def piece(slot, k):
        return wall.at[slot, lax.div(k, 2), pl.ds(lax.rem(k, 2) * share, share)]

    def to_beside(k):
        return remote(piece(0, k), piece(1, k), y_s.at[k], y_r.at[k], beside, mine)

    def to_far(q, k):
        to = flip(me, 4 * q, n)
        return remote(piece(0, k), piece(2 * q, k), m_s.at[q, k], m_r.at[q, k], to, mine)

    def pass_far(q, k):
        return remote(
            piece(2 * q, k), piece(2 * q + 1, k), f_s.at[q, k], f_r.at[q, k], beside, mine
        )

    for c in range(strips):
        own[c].wait()
        if 2 * c < AHEAD:
            for k in range(2 * c, min(2 * c + 2, AHEAD)):
                to_far(1, k).start()

    def columns(h):
        return pl.ds(pl.multiple_of(h * size, size), size)

    def lifted(ref, h):
        x = ref[:, columns(h)].astype(f32)
        return x / (1.0 + jnp.exp(-x))

    def fresh_state(h):
        kept = lifted(k_ref, h) * keep[...]
        return jnp.dot(kept.T.astype(bf16), v_ref[:, columns(h)], preferred_element_type=f32)

    half = local // 2
    bundle = half // 2
    mine_at, other_at = odd * half, (1 - odd) * half

    def some(g):
        return pl.ds(g * bundle, bundle)

    def my_some(g):
        return pl.ds(mine_at + g * bundle, bundle)

    def to_peer(g):
        return remote(give.at[some(g)], peer.at[some(g)], b_s.at[g], b_r.at[g], beside, mine)

    def chain(g):
        to = lax.rem(me + 2, n)
        return remote(after.at[some(g)], before.at[some(g)], c_s.at[g], c_r.at[g], to, mine)

    def to_state(g):
        return remote(lend.at[some(g)], state.at[my_some(g)], d_s.at[g], d_r.at[g], beside, mine)

    for g in range(2):

        @pl.loop(g * bundle, (g + 1) * bundle)
        def _(i):
            give[i] = fresh_state(other_at + i).astype(bf16)

        to_peer(g).start()

    for k in range(2):
        to_beside(k).start()

    @pl.loop(0, half)
    def _(i):
        fresh[i] = fresh_state(mine_at + i)

    @pl.when(pair == 0)
    def _():
        before[...] = jnp.zeros_like(before)

    def turn():
        @pl.loop(0, 2)
        def _(g):
            to_peer(g).wait_recv()

            @pl.when(pair > 0)
            def _():
                chain(g).wait_recv()

            held, theirs = fresh[some(g)], peer[some(g)].astype(f32)
            past = before[some(g)].astype(f32)
            between = jnp.where(odd == 0, held, theirs) + even_joins * past

            @pl.when(pair < n // 2 - 1)
            def _():
                total = jnp.where(odd == 0, theirs, held) + odd_joins * between
                after[some(g)] = total.astype(bf16)
                chain(g).start()

            lend[some(g)] = jnp.where(odd == 0, between, past).astype(bf16)
            to_state(g).start()
            state[my_some(g)] = jnp.where(odd == 0, past, between).astype(bf16)

    def inside(h):
        scores = lax.dot_general(
            lifted(q_ref, h).astype(bf16),
            lifted(k_ref, h).astype(bf16),
            (((1,), (1,)), ((), ())),
            preferred_element_type=f32,
        )
        attn[:, columns(h)] = jnp.dot(
            (scores * allowed[...]).astype(bf16), v_ref[:, columns(h)], preferred_element_type=f32
        )

    services = pieces * (slots // 2 - 1)
    many = -(-local // 3)

    def serve(j):
        q, k = lax.div(j, pieces) + 1, lax.rem(j, pieces)
        to_far(q, k).wait_recv()
        pass_far(q, k).start()

        @pl.when(j + AHEAD < services)
        def _():
            to_far(lax.div(j + AHEAD, pieces) + 1, lax.rem(j + AHEAD, pieces)).start()

        @pl.when(j < pieces - 2)
        def _():
            to_beside(j + 2).start()

    moment = jnp.minimum(pair, services - 3)

    def insides(j):
        @pl.loop(j * many, (j + 1) * many)
        def _(h):
            @pl.when(h < local)
            def _():
                inside(h)

    def finish(h):
        outside = jnp.dot(lifted(q_ref, h).astype(bf16), state[h], preferred_element_type=f32)
        full = attn[:, columns(h)] + outside * carry[...]
        mean_square = jnp.mean(full * full, axis=1, keepdims=True)
        scaled = full * lax.rsqrt(mean_square + 1e-06) * gain_ref[:, columns(h)]
        at = pl.multiple_of(lax.rem(h, half) * size, size)
        headed[lax.div(h, half), :, pl.ds(at, size)] = scaled.astype(bf16)

    def exchange(p):
        return remote(headed.at[p], headed.at[2 + p], e_s.at[p], e_r.at[p], across, mine)

    def finish_all():
        for g in range(2):
            to_state(g).wait_recv()
        for p in range(2):

            @pl.loop(p * half, (p + 1) * half)
            def _(h):
                finish(h)

            exchange(p).start()

    @pl.loop(0, services - 2)
    def _(j):
        @pl.when(j == moment)
        def _():
            turn()

        insides(j)

        @pl.when(j == jnp.maximum(moment, 2))
        def _():
            finish_all()

        serve(j)

    def mask_of(s):
        return 4 * lax.div(s, 2) + lax.rem(s, 2)

    def block_of(s):
        return flip(me, mask_of(s), n)

    def owner_of(s):
        head = lax.div(block_of(s), group)
        return lax.div(head, 2), lax.rem(head, 2)

    def to_core(s, c, u):
        at = s * strips + c
        return remote(
            mixed.at[u, at],
            beside_core.at[u, at],
            k_s.at[u, at],
            k_r.at[u, at],
            me,
            chip * 2 + 1 - core,
        )

    def to_owner(s, c, u, to, rel):
        at = s * strips + c
        return remote(
            mixed.at[u, at], parts.at[u, at, rel], r_s.at[u, at], r_r.at[u, at, rel], me, to
        )

    def project(s, c, u):
        deep = wall.shape[2] // 2
        value = jnp.dot(headed[2 * u], wall[s, c, 0:deep], preferred_element_type=f32)
        value += jnp.dot(headed[2 * u + 1], wall[s, c, deep:], preferred_element_type=f32)
        acc[u, s * strips + c] = value

        @pl.when(owner_of(s)[1] != core)
        def _():
            mixed[u, s * strips + c] = value.astype(bf16)
            to_core(s, c, u).start()

    def presum(s, c, u):
        owner_chip, owner_core = owner_of(s)

        @pl.when(owner_core == core)
        def _():
            at = s * strips + c
            to_core(s, c, u).wait_recv()
            value = acc[u, at] + beside_core[u, at].astype(f32)
            acc[u, at] = value

            @pl.when(owner_chip != chip)
            def _():
                mixed[u, at] = value.astype(bf16)
                rel = lax.rem(chip - owner_chip + chips, chips)
                to_owner(s, c, u, owner_chip * 2 + core, rel).start()

    def work(low, high, step, first, last, u):
        for body in (project, presum):

            @pl.loop(0, (high - low) // step)
            def _(i):
                @pl.loop(first, last)
                def _(c):
                    body(low + i * step, c, u)

    def passed(k):
        @pl.loop(1, slots // 2)
        def _(q):
            pass_far(q, k).wait_recv()

    for k in range(pieces):
        to_beside(k).wait_recv()
    work(0, 2, 1, 0, strips, 0)
    work(2, slots, 2, 0, strips - 1, 0)
    serve(services - 2)
    for k in range(pieces - 2):
        passed(k)
    work(3, slots + 1, 2, 0, strips - 1, 0)
    serve(services - 1)
    for p in range(2):
        exchange(p).wait_recv()
    work(0, slots, 1, 0, strips - 1, 1)
    work(2, slots, 2, strips - 1, strips, 1)
    work(0, 2, 1, strips - 1, strips, 1)
    passed(pieces - 2)
    passed(pieces - 1)
    work(3, slots + 1, 2, strips - 1, strips, 1)
    work(2, slots, 1, strips - 1, strips, 0)

    def summed(s, c, u):
        value = acc[u, s * strips + c]
        for rel in range(1, chips):
            to_owner(s, c, u, mine, rel).wait_recv()
            value = value + parts[u, s * strips + c, rel].astype(f32)
        return value

    def cell(ref, b, c):
        if flat:
            return ref.at[:, pl.ds(pl.multiple_of(b * col + c * width, 128), width)]
        return ref.at[b]

    def hand_over(s, c):
        at = s * strips + c
        return remote(sum_out.at[at], sum_in.at[at], o_s.at[at], o_r.at[at], across, mine)

    def settle(block, c, value):
        b = block - group * mine
        total = value + cell(res_ref, b, c)[...].astype(f32)
        cell(hidden_ref, b, c)[...] = total
        sq_own[...] += lax.dot_general(
            jnp.ones((8, width), f32),
            total * total,
            (((1,), (1,)), ((), ())),
            precision=highest,
            preferred_element_type=f32,
        )

    sq_own[...] = jnp.zeros_like(sq_own)

    def owned(first, last, body, seat_of=None):
        @pl.loop(0, slots)
        def _(s):
            block = block_of(s) if seat_of is None else flip(seat_of, mask_of(s), n)

            @pl.when(lax.div(block, group) == mine)
            def _():
                @pl.loop(first, last)
                def _(c):
                    body(block, s, c)

    def reduce_other(block, s, c):
        sum_out[s * strips + c] = summed(s, c, 1).astype(bf16)
        hand_over(s, c).start()

    def reduce_own(block, s, c):
        settle(block, c, summed(s, c, 0))

    def take(block, s, c):
        hand_over(s, c).wait_recv()
        settle(block, c, sum_in[s * strips + c].astype(f32))

    owned(0, strips - 1, reduce_other)
    owned(0, strips - 1, reduce_own)
    owned(strips - 1, strips, reduce_other)
    owned(strips - 1, strips, reduce_own)
    owned(0, strips, take, across)

    def spread(j, to, slot):
        return remote(sq_own, sq_all.at[slot], q_s.at[j], q_r.at[j], me, to)

    for j in range(1, heads):
        spread(j, lax.rem(mine + j, heads), j).start()
    squares = sq_own[...]
    for j in range(1, heads):
        spread(j, mine, j).wait_recv()
        squares = squares + sq_all[j]
    scale = lax.rsqrt(squares / (col * n) + 1e-06).T[:, 0:1]
    if flat:
        normed_ref[...] = (hidden_ref[...] * scale * norm_ref[...]).astype(bf16)
    else:
        for p in range(group):
            normed_ref[p] = (hidden_ref[p] * scale * norm_ref[p]).astype(bf16)

    for j in range(1, heads):
        spread(j, mine, j).wait_send()
    for p in range(2):
        exchange(p).wait_send()
    for k in range(pieces):
        to_beside(k).wait_send()

    @pl.loop(0, services)
    def _(j):
        q, k = lax.div(j, pieces) + 1, lax.rem(j, pieces)
        to_far(q, k).wait_send()
        pass_far(q, k).wait_send()

    for g in range(2):
        to_peer(g).wait_send()
        to_state(g).wait_send()

    @pl.when(pair < n // 2 - 1)
    def _():
        for g in range(2):
            chain(g).wait_send()

    @pl.loop(0, slots)
    def _(s):
        owner_chip, owner_core = owner_of(s)
        relay = owner_core == core

        @pl.loop(0, strips)
        def _(c):
            @pl.when(jnp.logical_not(relay))
            def _():
                for u in range(2):
                    to_core(s, c, u).wait_send()

            @pl.when(relay & (owner_chip != chip))
            def _():
                for u in range(2):
                    to_owner(s, c, u, mine, 0).wait_send()

            @pl.when(relay & (owner_chip == chip))
            def _():
                hand_over(s, c).wait_send()


def attend(lengths, query, key, value, gain, weight, residual, norm_gain, n, heads):
    rows, feats = query.shape
    col, group, slots = weight.shape[1], n // heads, n // 2
    local, flat = feats // HEAD_DIM, col % 128 == 0
    strips = col // 128 if flat else 1
    width, depth = col // strips, weight.shape[0]
    dma = pltpu.SemaphoreType.DMA
    bf16, f32 = jnp.bfloat16, jnp.float32
    vmem = pl.BlockSpec(memory_space=pltpu.VMEM)
    gain_shape = (1, group * col) if flat else (group, 1, col)
    shape = (rows, group * col) if flat else (group, rows, col)
    if not flat:
        residual = jnp.swapaxes(residual.reshape(rows, group, col), 0, 1)
    hidden, normed = pl.pallas_call(
        functools.partial(attend_kernel, n, heads, flat),
        out_shape=(jax.ShapeDtypeStruct(shape, f32), jax.ShapeDtypeStruct(shape, bf16)),
        in_specs=[pl.BlockSpec(memory_space=pltpu.SMEM)]
        + [vmem] * 4
        + [pl.BlockSpec(memory_space=pl.ANY)]
        + [vmem] * 2,
        out_specs=(vmem, vmem),
        scratch_shapes=[
            pltpu.VMEM((slots, strips, depth, width), bf16),
            pltpu.VMEM((rows, rows), f32),
            pltpu.VMEM((rows, HEAD_DIM), f32),
            pltpu.VMEM((rows, HEAD_DIM), f32),
            pltpu.VMEM((local // 2, HEAD_DIM, HEAD_DIM), f32),
        ]
        + [pltpu.VMEM((local // 2, HEAD_DIM, HEAD_DIM), bf16)] * 5
        + [
            pltpu.VMEM((local, HEAD_DIM, HEAD_DIM), bf16),
            pltpu.VMEM((rows, feats), f32),
            pltpu.VMEM((4, rows, feats // 2), bf16),
            pltpu.VMEM((2, slots * strips, rows, width), f32),
            pltpu.VMEM((2, slots * strips, rows, width), bf16),
            pltpu.VMEM((2, slots * strips, rows, width), bf16),
            pltpu.VMEM((2, slots * strips, heads // 2, rows, width), bf16),
            pltpu.VMEM((slots * strips, rows, width), bf16),
            pltpu.VMEM((slots * strips, rows, width), bf16),
            pltpu.VMEM((8, rows), f32),
            pltpu.VMEM((heads, 8, rows), f32),
            dma((strips,)),
        ]
        + [dma((2 * strips,))] * 2
        + [dma((slots // 2, 2 * strips))] * 4
        + [dma((2,))] * 8
        + [dma((2, slots * strips))] * 3
        + [
            dma((2, slots * strips, heads // 2)),
            dma((slots * strips,)),
            dma((slots * strips,)),
            dma((heads,)),
            dma((heads,)),
        ],
        compiler_params=pltpu.CompilerParams(
            collective_id=2, has_side_effects=True, vmem_limit_bytes=60 * 1024 * 1024
        ),
        name="attend",
    )(lengths, query, key, value, gain, weight, residual, norm_gain.reshape(gain_shape))
    if not flat:
        hidden, normed = (jnp.swapaxes(a, 0, 1).reshape(rows, -1) for a in (hidden, normed))
    return hidden, normed


def on_device(
    query,
    key,
    value,
    episode_lengths,
    attn_gain,
    out_weight,
    residual,
    norm_gain,
    expert_ids,
    route_weights,
    gate_weight,
    up_weight,
    down_weight,
):
    n, heads = lax.axis_size("ctx"), lax.axis_size("head")
    hidden, normed = attend(
        episode_lengths,
        query,
        key,
        value,
        attn_gain[None, :],
        out_weight,
        residual,
        norm_gain,
        n,
        heads,
    )
    return experts(
        hidden,
        normed,
        expert_ids.T,
        route_weights.T,
        gate_weight[0],
        up_weight[0],
        down_weight[0],
        n,
        heads,
    )


def solution(mesh):
    placed = (
        P("ctx", "head"),
        P("ctx", "head"),
        P("ctx", "head"),
        P(),
        P("head"),
        P("head", "ctx"),
        P("ctx", "head"),
        P("head"),
        P("ctx", None),
        P("ctx", None),
        P("ctx", None, "head"),
        P("ctx", None, "head"),
        P("ctx", "head", None),
    )
    return jax.shard_map(
        on_device, mesh=mesh, in_specs=placed, out_specs=P("ctx", "head"), check_vma=False
    )
```

```python
import functools

import jax
import jax.numpy as jnp
from jax import lax
from jax.experimental import pallas as pl
from jax.experimental.pallas import tpu as pltpu
from jax.sharding import PartitionSpec as P

HEAD_DIM = 128
AHEAD = 2


highest = lax.Precision.HIGHEST


MESH = pl.DeviceIdType.MESH


def remote(src, dst, send, recv, ctx, head):
    return pltpu.make_async_remote_copy(
        src_ref=src,
        dst_ref=dst,
        send_sem=send,
        recv_sem=recv,
        device_id=(ctx, head),
        device_id_type=MESH,
    )


def seat():
    head = lax.axis_index("head")
    return lax.axis_index("ctx"), lax.div(head, 2), lax.rem(head, 2)


def flip(me, i, n):
    if n & (n - 1):
        return lax.rem(i - me + 2 * n, n)
    other, bit = me, 1
    while bit < n:
        on = lax.rem(lax.div(me, bit), 2)
        other = other + lax.rem(lax.div(i, bit), 2) * bit * (1 - 2 * on)
        bit *= 2
    return other


def moe_kernel(
    n,
    chips,
    hidden_ref,
    normed_ref,
    ids_ref,
    route_ref,
    gate_ref,
    up_ref,
    down_ref,
    layer_ref,
    gate_w,
    up_w,
    down_w,
    outb,
    full,
    gated,
    part,
    pair,
    out_x,
    in_x,
    total,
    ret,
    acc,
    rank_row,
    rank_col,
    weight_col,
    w_s,
    a_s,
    a_r,
    p_s,
    p_r,
    x_s,
    x_r,
    f_s,
    f_r,
    s_s,
    s_r,
    c_s,
    c_r,
    h_s,
    h_r,
):
    me, chip, core = seat()
    f32, bf16 = jnp.float32, jnp.bfloat16
    tokens, width = normed_ref.shape
    cap = full.shape[1]
    mine, partner = chip * 2 + core, chip * 2 + 1 - core

    weights = [
        pltpu.make_async_copy(gate_ref, gate_w, w_s.at[0]),
        pltpu.make_async_copy(up_ref, up_w, w_s.at[1]),
        pltpu.make_async_copy(down_ref, down_w, w_s.at[2]),
    ]
    for copy in weights:
        copy.start()

    barrier = pltpu.get_barrier_semaphore()

    def tell(ctx, head):
        pl.semaphore_signal(barrier, inc=1, device_id=(ctx, head), device_id_type=MESH)

    tell(me, partner)
    for j in range(1, chips):
        tell(me, lax.rem(chip + j, chips) * 2 + core)

    @pl.loop(1, n)
    def _(i):
        tell(lax.rem(me + i, n), mine)

    expert = lax.broadcasted_iota(jnp.int32, (n, tokens), 0)
    first = ids_ref[0:1, :] == expert
    second = ids_ref[1:2, :] == expert
    raw = route_ref[...].astype(f32)
    shares = raw / (raw[0:1, :] + raw[1:2, :])
    weight = jnp.where(first, shares[0:1, :], 0.0) + jnp.where(second, shares[1:2, :], 0.0)
    named = first | second
    before = (
        lax.broadcasted_iota(jnp.int32, (tokens, tokens), 0)
        < lax.broadcasted_iota(jnp.int32, (tokens, tokens), 1)
    ).astype(f32)
    count = jnp.dot(
        jnp.where(named, 1.0, 0.0).astype(bf16), before.astype(bf16), preferred_element_type=f32
    )
    rank = jnp.where(named, count, -1.0)
    for e in range(n):
        rank_row[e] = jnp.broadcast_to(rank[e : e + 1, :], rank_row.shape[1:])

    def spread_of(i):
        row = rank_row[flip(me, i, n)][0:1, :]
        place = lax.broadcasted_iota(jnp.int32, (cap, tokens), 0).astype(f32)
        chosen = jnp.where(place == row, 1.0, 0.0).astype(bf16)
        return jnp.dot(chosen, normed_ref[...], preferred_element_type=f32).astype(bf16)

    def cell(ref, block, head):
        return ref.at[block, :, pl.ds(pl.multiple_of(head * width, 128), width)]

    full[0, :, pl.ds(pl.multiple_of(mine * width, 128), width)] = spread_of(0)

    pl.semaphore_wait(barrier, chips + n - 1)

    def to_partner(i, head):
        b = cell(full, i, head)
        return remote(b, b, p_s.at[i], p_r.at[i], me, partner)

    def to_chip(i, j):
        b = cell(full, i, mine)
        return remote(b, b, x_s.at[j, i], x_r.at[j, i], me, lax.rem(chip + j, chips) * 2 + core)

    def from_chip(i, j):
        b = cell(full, i, lax.rem(chip - j + chips, chips) * 2 + core)
        return remote(b, b, x_s.at[j, i], x_r.at[j, i], me, partner)

    def forward(i, j, which):
        b = cell(full, i, lax.rem(chip - j + chips, chips) * 2 + which)
        return remote(b, b, f_s.at[j, i], f_r.at[j, i], me, partner)

    def sent(i):
        return remote(
            outb.at[i], cell(full, i, mine), a_s.at[i], a_r.at[i], flip(me, i, n), mine
        )

    def spread(i):
        for j in range(1, chips):
            to_chip(i, j).start()
        to_partner(i, mine).start()

    spread(0)
    rank_col[...] = rank.T
    weight_col[...] = weight.T
    half = n // 2
    share = half // 4

    def issue(i):
        outb[i] = spread_of(i)
        sent(i).start()

    def near(b, body, skip=0):
        @pl.loop(b * share + skip, (b + 1) * share)
        def _(i):
            body(i)

    def far(b, body):
        near(b, lambda i: body(half + i))

    def both(b, body, skip=0):
        far(b, body)
        near(b, body, skip)

    far(0, issue)
    near(0, issue, 1)
    for b in range(1, 4):
        near(b, issue)

    def arrive(i):
        sent(i).wait_recv()
        spread(i)

    def arrive_far(b):
        far(b, arrive)
        if b < 2:
            far(b + 2, issue)

    def relay(i):
        for j in range(1, chips):
            from_chip(i, j).wait_recv()
            forward(i, j, core).start()

    def complete(i):
        to_partner(i, partner).wait_recv()
        for j in range(1, chips):
            forward(i, j, 1 - core).wait_recv()

    def pick_rows(b):
        rows = [full[pl.ds(at + b * share, share)] for at in (0, half)]
        return jnp.concatenate([r.reshape(share * cap, r.shape[2]) for r in rows], axis=0)

    def expand(b):
        both(b, complete)
        tile = 256 if gate_w.shape[1] % 256 == 0 else gate_w.shape[1]

        for t in range(gate_w.shape[1] // tile):
            rows = pick_rows(b)
            at = pl.ds(t * tile, tile)
            gate = jnp.dot(rows, gate_w[:, at], preferred_element_type=f32)
            up = jnp.dot(rows, up_w[:, at], preferred_element_type=f32)
            gated[:, at] = (gate / (1.0 + jnp.exp(-gate)) * up).astype(bf16)

    def column(j):
        return lax.rem(chip + j, chips)

    def swap(i, j):
        return remote(
            cell(part, i, column(j) * 2 + 1 - core),
            pair.at[i, j],
            s_s.at[j, i],
            s_r.at[j, i],
            me,
            partner,
        )

    def cross(i, j):
        return remote(
            out_x.at[i, j], in_x.at[i, j], c_s.at[j, i], c_r.at[j, i], me, column(j) * 2 + core
        )

    def home(i):
        return remote(total.at[i], ret.at[i], h_s.at[i], h_r.at[i], flip(me, i, n), mine)

    def contract(b):
        tile = 256

        for t in range(part.shape[2] // tile):
            at = pl.ds(t * tile, tile)
            value = jnp.dot(gated[...], down_w[:, at], preferred_element_type=f32)
            value = value.astype(bf16).reshape(2, share, cap, tile)
            for side in range(2):
                part[pl.ds(side * half + b * share, share), :, at] = value[side]

        def begin(i):
            for j in list(range(1, chips)) + [0]:
                swap(i, j).start()

        both(b, begin)

    def paired(i, j):
        swap(i, j).wait_recv()
        head = pl.multiple_of((column(j) * 2 + core) * width, 128)
        return part[i, :, pl.ds(head, width)].astype(f32) + pair[i, j].astype(f32)

    def pass_on(i):
        for j in range(1, chips):
            out_x[i, j] = paired(i, j).astype(bf16)
            cross(i, j).start()

    def gather(i):
        value = paired(i, 0)
        for j in range(1, chips):
            cross(i, j).wait_recv()
            value = value + in_x[i, j].astype(f32)
        return value.astype(bf16)

    def send_home(i):
        total[i] = gather(i)
        home(i).start()

    def combine(i):
        e = flip(me, i, n)
        place = lax.broadcasted_iota(jnp.int32, (tokens, cap), 1).astype(f32)
        chosen = lax.broadcasted_iota(jnp.int32, (tokens, n), 1) == e

        def own_column(ref):
            return jnp.sum(jnp.where(chosen, ref[...], 0.0), axis=1, keepdims=True)

        pick = jnp.where(own_column(rank_col) == place, 1.0, 0.0).astype(bf16)
        value = jnp.dot(pick, ret[i], preferred_element_type=f32)
        acc[...] += own_column(weight_col) * value

    def receive(i):
        home(i).wait_recv()
        combine(i)

    near(0, arrive, 1)
    near(1, arrive)
    far(1, issue)
    near(0, relay)
    near(2, arrive)
    arrive_far(0)
    near(1, relay)
    near(3, arrive)
    acc[...] = hidden_ref[...]
    near(2, relay)
    far(0, relay)
    near(3, relay)
    for copy in weights:
        copy.wait()
    for b in range(4):
        expand(b)
        if b > 0:
            far(b - 1, send_home)
        if b < 3:
            arrive_far(b + 1)
        contract(b)
        far(b, pass_on)
        if b < 3:
            far(b + 1, relay)
        if b == 1:
            ret[0] = gather(0)
            near(0, send_home, 1)
        elif b > 1:
            near(b - 1, send_home)
        near(b, pass_on)
    combine(0)
    near(0, receive, 1)
    near(1, receive)
    far(3, send_home)
    near(3, send_home)
    far(0, receive)
    near(2, receive)
    far(1, receive)
    far(2, receive)
    near(3, receive)
    far(3, receive)
    layer_ref[...] = acc[...].astype(bf16)

    @pl.loop(0, n)
    def _(i):
        to_partner(i, mine).wait_send()
        for j in range(1, chips):
            forward(i, j, core).wait_send()
            to_chip(i, j).wait_send()
            cross(i, j).wait_send()
        for j in range(chips):
            swap(i, j).wait_send()

    @pl.loop(1, n)
    def _(i):
        sent(i).wait_send()
        home(i).wait_send()


def experts(hidden, normed, ids, route, gate, up, down, n, heads):
    chips = heads // 2
    tokens, width = normed.shape
    cap = -(-3 * tokens // n // 16) * 16
    dma = pltpu.SemaphoreType.DMA
    bf16, f32 = jnp.bfloat16, jnp.float32
    vmem, hbm = pl.BlockSpec(memory_space=pltpu.VMEM), pl.BlockSpec(memory_space=pl.ANY)
    block = pltpu.VMEM((n, cap, width), bf16)
    piece = pltpu.VMEM((n, chips, cap, width), bf16)
    wide = pltpu.VMEM((n, cap, width * heads), bf16)
    column = pltpu.VMEM((tokens, n), f32)
    return pl.pallas_call(
        functools.partial(moe_kernel, n, chips),
        out_shape=jax.ShapeDtypeStruct((tokens, width), bf16),
        in_specs=[vmem] * 4 + [hbm] * 3,
        out_specs=vmem,
        scratch_shapes=[
            pltpu.VMEM(gate.shape, gate.dtype),
            pltpu.VMEM(up.shape, up.dtype),
            pltpu.VMEM(down.shape, down.dtype),
            block,
            wide,
            pltpu.VMEM((n // 4 * cap, gate.shape[1]), bf16),
            wide,
            piece,
            piece,
            piece,
            block,
            block,
            pltpu.VMEM((tokens, width), f32),
            pltpu.VMEM((n, 8, tokens), f32),
            column,
            column,
        ]
        + [dma((3,))]
        + [dma((n,))] * 4
        + [dma((chips, n))] * 8
        + [dma((n,))] * 2,
        compiler_params=pltpu.CompilerParams(
            collective_id=0, has_side_effects=True, vmem_limit_bytes=60 * 1024 * 1024
        ),
        name="experts",
    )(hidden, normed, ids, route, gate, up, down)


def attend_kernel(
    n,
    heads,
    flat,
    lengths_ref,
    q_ref,
    k_ref,
    v_ref,
    gain_ref,
    w_ref,
    res_ref,
    norm_ref,
    hidden_ref,
    normed_ref,
    wall,
    allowed,
    keep,
    carry,
    fresh,
    give,
    peer,
    before,
    after,
    lend,
    state,
    attn,
    headed,
    acc,
    mixed,
    beside_core,
    parts,
    sum_out,
    sum_in,
    sq_own,
    sq_all,
    here,
    y_s,
    y_r,
    m_s,
    m_r,
    f_s,
    f_r,
    b_s,
    b_r,
    c_s,
    c_r,
    d_s,
    d_r,
    e_s,
    e_r,
    k_s,
    k_r,
    r_s,
    r_r,
    o_s,
    o_r,
    q_s,
    q_r,
):
    me, chip, core = seat()
    mine = chip * 2 + core
    rows, feats = q_ref.shape
    size = HEAD_DIM
    local, slots, group, col = feats // size, n // 2, n // heads, w_ref.shape[1]
    chips = heads // 2
    strips, width = wall.shape[1], wall.shape[3]
    pieces, share = 2 * strips, w_ref.shape[0] // 2
    f32, bf16 = jnp.float32, jnp.bfloat16
    beside, across = flip(me, 1, n), flip(me, 2, n)

    own = [
        pltpu.make_async_copy(
            w_ref.at[:, pl.ds(c * width, width)], wall.at[0, c], here.at[c]
        )
        for c in range(strips)
    ]
    for copy in own:
        copy.start()

    barrier = pltpu.get_barrier_semaphore()

    def tell(ctx, head):
        pl.semaphore_signal(barrier, inc=1, device_id=(ctx, head), device_id_type=MESH)

    tell(beside, mine)
    tell(across, mine)
    for q in range(1, slots // 2):
        tell(flip(me, 4 * q, n), mine)
    for step in (2, n - 2):
        tell(lax.rem(me + step, n), mine)
    for j in range(1, heads):
        tell(me, lax.rem(mine + j, heads))

    base = me * rows
    starts, last = [0], base + rows - 1
    for e in range(lengths_ref.shape[0] - 1):
        starts.append(starts[-1] + lengths_ref[e])
    odd, pair = lax.rem(me, 2), lax.div(me, 2)
    middle = (2 * pair + 1) * rows
    open_at, open_middle, open_end = jnp.int32(0), jnp.int32(0), jnp.int32(0)
    for s in starts[1:]:
        open_at = jnp.where(s <= last, s, open_at)
        open_middle = jnp.where(s < middle, s, open_middle)
        open_end = jnp.where(s < middle + rows, s, open_end)

    def opened(shape):
        place = lax.broadcasted_iota(jnp.int32, shape, 0) + base
        seg = jnp.zeros(shape, jnp.int32)
        for s in starts[1:]:
            seg = jnp.where(place >= s, s, seg)
        return place, seg

    place, seg = opened((rows, size))
    keep[...] = jnp.where(place >= open_at, 1.0, 0.0)
    carry[...] = jnp.where(seg < base, 1.0, 0.0)
    place, seg = opened((rows, rows))
    source = lax.broadcasted_iota(jnp.int32, (rows, rows), 1) + base
    allowed[...] = jnp.where((source <= place) & (source >= seg), 1.0, 0.0)
    even_joins = jnp.where(open_middle < middle - rows, 1.0, 0.0)
    odd_joins = jnp.where(open_end < middle, 1.0, 0.0)

    pl.semaphore_wait(barrier, 3 + slots // 2 + heads - 1)

    def piece(slot, k):
        return wall.at[slot, lax.div(k, 2), pl.ds(lax.rem(k, 2) * share, share)]

    def to_beside(k):
        return remote(piece(0, k), piece(1, k), y_s.at[k], y_r.at[k], beside, mine)

    def to_far(q, k):
        to = flip(me, 4 * q, n)
        return remote(piece(0, k), piece(2 * q, k), m_s.at[q, k], m_r.at[q, k], to, mine)

    def pass_far(q, k):
        return remote(
            piece(2 * q, k), piece(2 * q + 1, k), f_s.at[q, k], f_r.at[q, k], beside, mine
        )

    for c in range(strips):
        own[c].wait()
        if 2 * c < AHEAD:
            for k in range(2 * c, min(2 * c + 2, AHEAD)):
                to_far(1, k).start()

    def columns(h):
        return pl.ds(pl.multiple_of(h * size, size), size)

    def lifted(ref, h):
        x = ref[:, columns(h)].astype(f32)
        return x / (1.0 + jnp.exp(-x))

    def fresh_state(h):
        kept = lifted(k_ref, h) * keep[...]
        return jnp.dot(kept.T.astype(bf16), v_ref[:, columns(h)], preferred_element_type=f32)

    half = local // 2
    bundle = half // 2
    mine_at, other_at = odd * half, (1 - odd) * half

    def some(g):
        return pl.ds(g * bundle, bundle)

    def my_some(g):
        return pl.ds(mine_at + g * bundle, bundle)

    def to_peer(g):
        return remote(give.at[some(g)], peer.at[some(g)], b_s.at[g], b_r.at[g], beside, mine)

    def chain(g):
        to = lax.rem(me + 2, n)
        return remote(after.at[some(g)], before.at[some(g)], c_s.at[g], c_r.at[g], to, mine)

    def to_state(g):
        return remote(lend.at[some(g)], state.at[my_some(g)], d_s.at[g], d_r.at[g], beside, mine)

    for g in range(2):

        @pl.loop(g * bundle, (g + 1) * bundle)
        def _(i):
            give[i] = fresh_state(other_at + i).astype(bf16)

        to_peer(g).start()

    for k in range(2):
        to_beside(k).start()

    @pl.loop(0, half)
    def _(i):
        fresh[i] = fresh_state(mine_at + i)

    @pl.when(pair == 0)
    def _():
        before[...] = jnp.zeros_like(before)

    def turn():
        @pl.loop(0, 2)
        def _(g):
            to_peer(g).wait_recv()

            @pl.when(pair > 0)
            def _():
                chain(g).wait_recv()

            held, theirs = fresh[some(g)], peer[some(g)].astype(f32)
            past = before[some(g)].astype(f32)
            between = jnp.where(odd == 0, held, theirs) + even_joins * past

            @pl.when(pair < n // 2 - 1)
            def _():
                total = jnp.where(odd == 0, theirs, held) + odd_joins * between
                after[some(g)] = total.astype(bf16)
                chain(g).start()

            lend[some(g)] = jnp.where(odd == 0, between, past).astype(bf16)
            to_state(g).start()
            state[my_some(g)] = jnp.where(odd == 0, past, between).astype(bf16)

    def inside(h):
        scores = lax.dot_general(
            lifted(q_ref, h).astype(bf16),
            lifted(k_ref, h).astype(bf16),
            (((1,), (1,)), ((), ())),
            preferred_element_type=f32,
        )
        attn[:, columns(h)] = jnp.dot(
            (scores * allowed[...]).astype(bf16), v_ref[:, columns(h)], preferred_element_type=f32
        )

    services = pieces * (slots // 2 - 1)
    many = -(-local // 3)

    def serve(j):
        q, k = lax.div(j, pieces) + 1, lax.rem(j, pieces)
        to_far(q, k).wait_recv()
        pass_far(q, k).start()

        @pl.when(j + AHEAD < services)
        def _():
            to_far(lax.div(j + AHEAD, pieces) + 1, lax.rem(j + AHEAD, pieces)).start()

        @pl.when(j < pieces - 2)
        def _():
            to_beside(j + 2).start()

    moment = jnp.minimum(pair, services - 3)

    def insides(j):
        @pl.loop(j * many, (j + 1) * many)
        def _(h):
            @pl.when(h < local)
            def _():
                inside(h)

    def finish(h):
        outside = jnp.dot(lifted(q_ref, h).astype(bf16), state[h], preferred_element_type=f32)
        full = attn[:, columns(h)] + outside * carry[...]
        mean_square = jnp.mean(full * full, axis=1, keepdims=True)
        scaled = full * lax.rsqrt(mean_square + 1e-06) * gain_ref[:, columns(h)]
        at = pl.multiple_of(lax.rem(h, half) * size, size)
        headed[lax.div(h, half), :, pl.ds(at, size)] = scaled.astype(bf16)

    def exchange(p):
        return remote(headed.at[p], headed.at[2 + p], e_s.at[p], e_r.at[p], across, mine)

    def finish_all():
        for g in range(2):
            to_state(g).wait_recv()
        for p in range(2):

            @pl.loop(p * half, (p + 1) * half)
            def _(h):
                finish(h)

            exchange(p).start()

    @pl.loop(0, services - 2)
    def _(j):
        @pl.when(j == moment)
        def _():
            turn()

        insides(j)

        @pl.when(j == jnp.maximum(moment, 2))
        def _():
            finish_all()

        serve(j)

    def mask_of(s):
        return 4 * lax.div(s, 2) + lax.rem(s, 2)

    def block_of(s):
        return flip(me, mask_of(s), n)

    def owner_of(s):
        head = lax.div(block_of(s), group)
        return lax.div(head, 2), lax.rem(head, 2)

    def to_core(s, c, u):
        at = s * strips + c
        return remote(
            mixed.at[u, at],
            beside_core.at[u, at],
            k_s.at[u, at],
            k_r.at[u, at],
            me,
            chip * 2 + 1 - core,
        )

    def to_owner(s, c, u, to, rel):
        at = s * strips + c
        return remote(
            mixed.at[u, at], parts.at[u, at, rel], r_s.at[u, at], r_r.at[u, at, rel], me, to
        )

    def project(s, c, u):
        deep = wall.shape[2] // 2
        value = jnp.dot(headed[2 * u], wall[s, c, 0:deep], preferred_element_type=f32)
        value += jnp.dot(headed[2 * u + 1], wall[s, c, deep:], preferred_element_type=f32)
        acc[u, s * strips + c] = value

        @pl.when(owner_of(s)[1] != core)
        def _():
            mixed[u, s * strips + c] = value.astype(bf16)
            to_core(s, c, u).start()

    def presum(s, c, u):
        owner_chip, owner_core = owner_of(s)

        @pl.when(owner_core == core)
        def _():
            at = s * strips + c
            to_core(s, c, u).wait_recv()
            value = acc[u, at] + beside_core[u, at].astype(f32)
            acc[u, at] = value

            @pl.when(owner_chip != chip)
            def _():
                mixed[u, at] = value.astype(bf16)
                rel = lax.rem(chip - owner_chip + chips, chips)
                to_owner(s, c, u, owner_chip * 2 + core, rel).start()

    def work(low, high, step, first, last, u):
        for body in (project, presum):

            @pl.loop(0, (high - low) // step)
            def _(i):
                @pl.loop(first, last)
                def _(c):
                    body(low + i * step, c, u)

    def passed(k):
        @pl.loop(1, slots // 2)
        def _(q):
            pass_far(q, k).wait_recv()

    for k in range(pieces):
        to_beside(k).wait_recv()
    work(0, 2, 1, 0, strips, 0)
    work(2, slots, 2, 0, strips - 1, 0)
    serve(services - 2)
    for k in range(pieces - 2):
        passed(k)
    work(3, slots + 1, 2, 0, strips - 1, 0)
    serve(services - 1)
    for p in range(2):
        exchange(p).wait_recv()
    work(0, slots, 1, 0, strips - 1, 1)
    work(2, slots, 2, strips - 1, strips, 1)
    work(0, 2, 1, strips - 1, strips, 1)
    passed(pieces - 2)
    passed(pieces - 1)
    work(3, slots + 1, 2, strips - 1, strips, 1)
    work(2, slots, 1, strips - 1, strips, 0)

    def summed(s, c, u):
        value = acc[u, s * strips + c]
        for rel in range(1, chips):
            to_owner(s, c, u, mine, rel).wait_recv()
            value = value + parts[u, s * strips + c, rel].astype(f32)
        return value

    def cell(ref, b, c):
        if flat:
            return ref.at[:, pl.ds(pl.multiple_of(b * col + c * width, 128), width)]
        return ref.at[b]

    def hand_over(s, c):
        at = s * strips + c
        return remote(sum_out.at[at], sum_in.at[at], o_s.at[at], o_r.at[at], across, mine)

    def settle(block, c, value):
        b = block - group * mine
        total = value + cell(res_ref, b, c)[...].astype(f32)
        cell(hidden_ref, b, c)[...] = total
        sq_own[...] += lax.dot_general(
            jnp.ones((8, width), f32),
            total * total,
            (((1,), (1,)), ((), ())),
            precision=highest,
            preferred_element_type=f32,
        )

    sq_own[...] = jnp.zeros_like(sq_own)

    def owned(first, last, body, seat_of=None):
        @pl.loop(0, slots)
        def _(s):
            block = block_of(s) if seat_of is None else flip(seat_of, mask_of(s), n)

            @pl.when(lax.div(block, group) == mine)
            def _():
                @pl.loop(first, last)
                def _(c):
                    body(block, s, c)

    def reduce_other(block, s, c):
        sum_out[s * strips + c] = summed(s, c, 1).astype(bf16)
        hand_over(s, c).start()

    def reduce_own(block, s, c):
        settle(block, c, summed(s, c, 0))

    def take(block, s, c):
        hand_over(s, c).wait_recv()
        settle(block, c, sum_in[s * strips + c].astype(f32))

    owned(0, strips - 1, reduce_other)
    owned(0, strips - 1, reduce_own)
    owned(strips - 1, strips, reduce_other)
    owned(strips - 1, strips, reduce_own)
    owned(0, strips, take, across)

    def spread(j, to, slot):
        return remote(sq_own, sq_all.at[slot], q_s.at[j], q_r.at[j], me, to)

    for j in range(1, heads):
        spread(j, lax.rem(mine + j, heads), j).start()
    squares = sq_own[...]
    for j in range(1, heads):
        spread(j, mine, j).wait_recv()
        squares = squares + sq_all[j]
    scale = lax.rsqrt(squares / (col * n) + 1e-06).T[:, 0:1]
    if flat:
        normed_ref[...] = (hidden_ref[...] * scale * norm_ref[...]).astype(bf16)
    else:
        for p in range(group):
            normed_ref[p] = (hidden_ref[p] * scale * norm_ref[p]).astype(bf16)

    for j in range(1, heads):
        spread(j, mine, j).wait_send()
    for p in range(2):
        exchange(p).wait_send()
    for k in range(pieces):
        to_beside(k).wait_send()

    @pl.loop(0, services)
    def _(j):
        q, k = lax.div(j, pieces) + 1, lax.rem(j, pieces)
        to_far(q, k).wait_send()
        pass_far(q, k).wait_send()

    for g in range(2):
        to_peer(g).wait_send()
        to_state(g).wait_send()

    @pl.when(pair < n // 2 - 1)
    def _():
        for g in range(2):
            chain(g).wait_send()

    @pl.loop(0, slots)
    def _(s):
        owner_chip, owner_core = owner_of(s)
        relay = owner_core == core

        @pl.loop(0, strips)
        def _(c):
            @pl.when(jnp.logical_not(relay))
            def _():
                for u in range(2):
                    to_core(s, c, u).wait_send()

            @pl.when(relay & (owner_chip != chip))
            def _():
                for u in range(2):
                    to_owner(s, c, u, mine, 0).wait_send()

            @pl.when(relay & (owner_chip == chip))
            def _():
                hand_over(s, c).wait_send()


def attend(lengths, query, key, value, gain, weight, residual, norm_gain, n, heads):
    rows, feats = query.shape
    col, group, slots = weight.shape[1], n // heads, n // 2
    local, flat = feats // HEAD_DIM, col % 128 == 0
    strips = col // 128 if flat else 1
    width, depth = col // strips, weight.shape[0]
    dma = pltpu.SemaphoreType.DMA
    bf16, f32 = jnp.bfloat16, jnp.float32
    vmem = pl.BlockSpec(memory_space=pltpu.VMEM)
    gain_shape = (1, group * col) if flat else (group, 1, col)
    shape = (rows, group * col) if flat else (group, rows, col)
    if not flat:
        residual = jnp.swapaxes(residual.reshape(rows, group, col), 0, 1)
    hidden, normed = pl.pallas_call(
        functools.partial(attend_kernel, n, heads, flat),
        out_shape=(jax.ShapeDtypeStruct(shape, f32), jax.ShapeDtypeStruct(shape, bf16)),
        in_specs=[pl.BlockSpec(memory_space=pltpu.SMEM)]
        + [vmem] * 4
        + [pl.BlockSpec(memory_space=pl.ANY)]
        + [vmem] * 2,
        out_specs=(vmem, vmem),
        scratch_shapes=[
            pltpu.VMEM((slots, strips, depth, width), bf16),
            pltpu.VMEM((rows, rows), f32),
            pltpu.VMEM((rows, HEAD_DIM), f32),
            pltpu.VMEM((rows, HEAD_DIM), f32),
            pltpu.VMEM((local // 2, HEAD_DIM, HEAD_DIM), f32),
        ]
        + [pltpu.VMEM((local // 2, HEAD_DIM, HEAD_DIM), bf16)] * 5
        + [
            pltpu.VMEM((local, HEAD_DIM, HEAD_DIM), bf16),
            pltpu.VMEM((rows, feats), f32),
            pltpu.VMEM((4, rows, feats // 2), bf16),
            pltpu.VMEM((2, slots * strips, rows, width), f32),
            pltpu.VMEM((2, slots * strips, rows, width), bf16),
            pltpu.VMEM((2, slots * strips, rows, width), bf16),
            pltpu.VMEM((2, slots * strips, heads // 2, rows, width), bf16),
            pltpu.VMEM((slots * strips, rows, width), bf16),
            pltpu.VMEM((slots * strips, rows, width), bf16),
            pltpu.VMEM((8, rows), f32),
            pltpu.VMEM((heads, 8, rows), f32),
            dma((strips,)),
        ]
        + [dma((2 * strips,))] * 2
        + [dma((slots // 2, 2 * strips))] * 4
        + [dma((2,))] * 8
        + [dma((2, slots * strips))] * 3
        + [
            dma((2, slots * strips, heads // 2)),
            dma((slots * strips,)),
            dma((slots * strips,)),
            dma((heads,)),
            dma((heads,)),
        ],
        compiler_params=pltpu.CompilerParams(
            collective_id=2, has_side_effects=True, vmem_limit_bytes=60 * 1024 * 1024
        ),
        name="attend",
    )(lengths, query, key, value, gain, weight, residual, norm_gain.reshape(gain_shape))
    if not flat:
        hidden, normed = (jnp.swapaxes(a, 0, 1).reshape(rows, -1) for a in (hidden, normed))
    return hidden, normed


def on_device(
    query,
    key,
    value,
    episode_lengths,
    attn_gain,
    out_weight,
    residual,
    norm_gain,
    expert_ids,
    route_weights,
    gate_weight,
    up_weight,
    down_weight,
):
    n, heads = lax.axis_size("ctx"), lax.axis_size("head")
    hidden, normed = attend(
        episode_lengths,
        query,
        key,
        value,
        attn_gain[None, :],
        out_weight,
        residual,
        norm_gain,
        n,
        heads,
    )
    return experts(
        hidden,
        normed,
        expert_ids.T,
        route_weights.T,
        gate_weight[0],
        up_weight[0],
        down_weight[0],
        n,
        heads,
    )


def solution(mesh):
    placed = (
        P("ctx", "head"),
        P("ctx", "head"),
        P("ctx", "head"),
        P(),
        P("head"),
        P("head", "ctx"),
        P("ctx", "head"),
        P("head"),
        P("ctx", None),
        P("ctx", None),
        P("ctx", None, "head"),
        P("ctx", None, "head"),
        P("ctx", "head", None),
    )
    return jax.shard_map(
        on_device, mesh=mesh, in_specs=placed, out_specs=P("ctx", "head"), check_vma=False
    )
```

```python
import functools

import jax
import jax.numpy as jnp
from jax import lax
from jax.experimental import pallas as pl
from jax.experimental.pallas import tpu as pltpu
from jax.sharding import PartitionSpec as P

HEAD_DIM = 128
AHEAD = 2


highest = lax.Precision.HIGHEST


MESH = pl.DeviceIdType.MESH


def remote(src, dst, send, recv, ctx, head):
    return pltpu.make_async_remote_copy(
        src_ref=src,
        dst_ref=dst,
        send_sem=send,
        recv_sem=recv,
        device_id=(ctx, head),
        device_id_type=MESH,
    )


def seat():
    head = lax.axis_index("head")
    return lax.axis_index("ctx"), lax.div(head, 2), lax.rem(head, 2)


def flip(me, i, n):
    if n & (n - 1):
        return lax.rem(i - me + 2 * n, n)
    other, bit = me, 1
    while bit < n:
        on = lax.rem(lax.div(me, bit), 2)
        other = other + lax.rem(lax.div(i, bit), 2) * bit * (1 - 2 * on)
        bit *= 2
    return other


def moe_kernel(
    n,
    chips,
    hidden_ref,
    normed_ref,
    rank_row,
    rank_col,
    weight_col,
    gate_ref,
    up_ref,
    down_ref,
    layer_ref,
    gate_w,
    up_w,
    down_w,
    outb,
    full,
    gated,
    part,
    pair,
    out_x,
    in_x,
    total,
    ret,
    acc,
    w_s,
    a_s,
    a_r,
    p_s,
    p_r,
    x_s,
    x_r,
    f_s,
    f_r,
    s_s,
    s_r,
    c_s,
    c_r,
    h_s,
    h_r,
):
    me, chip, core = seat()
    f32, bf16 = jnp.float32, jnp.bfloat16
    tokens, width = normed_ref.shape
    cap = full.shape[1]
    mine, partner = chip * 2 + core, chip * 2 + 1 - core

    weights = [
        pltpu.make_async_copy(gate_ref, gate_w, w_s.at[0]),
        pltpu.make_async_copy(up_ref, up_w, w_s.at[1]),
        pltpu.make_async_copy(down_ref, down_w, w_s.at[2]),
    ]
    for copy in weights:
        copy.start()

    barrier = pltpu.get_barrier_semaphore()

    def tell(ctx, head):
        pl.semaphore_signal(barrier, inc=1, device_id=(ctx, head), device_id_type=MESH)

    tell(me, partner)
    for j in range(1, chips):
        tell(me, lax.rem(chip + j, chips) * 2 + core)

    @pl.loop(1, n)
    def _(i):
        tell(lax.rem(me + i, n), mine)

    def spread_of(i):
        row = rank_row[flip(me, i, n)][0:1, :]
        place = lax.broadcasted_iota(jnp.int32, (cap, tokens), 0).astype(f32)
        chosen = jnp.where(place == row, 1.0, 0.0).astype(bf16)
        return jnp.dot(chosen, normed_ref[...], preferred_element_type=f32).astype(bf16)

    def cell(ref, block, head):
        return ref.at[block, :, pl.ds(pl.multiple_of(head * width, 128), width)]

    full[0, :, pl.ds(pl.multiple_of(mine * width, 128), width)] = spread_of(0)

    pl.semaphore_wait(barrier, chips + n - 1)

    def to_partner(i, head):
        b = cell(full, i, head)
        return remote(b, b, p_s.at[i], p_r.at[i], me, partner)

    def to_chip(i, j):
        b = cell(full, i, mine)
        return remote(b, b, x_s.at[j, i], x_r.at[j, i], me, lax.rem(chip + j, chips) * 2 + core)

    def from_chip(i, j):
        b = cell(full, i, lax.rem(chip - j + chips, chips) * 2 + core)
        return remote(b, b, x_s.at[j, i], x_r.at[j, i], me, partner)

    def forward(i, j, which):
        b = cell(full, i, lax.rem(chip - j + chips, chips) * 2 + which)
        return remote(b, b, f_s.at[j, i], f_r.at[j, i], me, partner)

    def sent(i):
        return remote(
            outb.at[i], cell(full, i, mine), a_s.at[i], a_r.at[i], flip(me, i, n), mine
        )

    def spread(i):
        for j in range(1, chips):
            to_chip(i, j).start()
        to_partner(i, mine).start()

    spread(0)
    half = n // 2
    share = half // 4

    def issue(i):
        outb[i] = spread_of(i)
        sent(i).start()

    def near(b, body, skip=0):
        @pl.loop(b * share + skip, (b + 1) * share)
        def _(i):
            body(i)

    def far(b, body):
        near(b, lambda i: body(half + i))

    def both(b, body, skip=0):
        far(b, body)
        near(b, body, skip)

    far(0, issue)
    near(0, issue, 1)
    for b in range(1, 4):
        near(b, issue)

    def arrive(i):
        sent(i).wait_recv()
        spread(i)

    def arrive_far(b):
        far(b, arrive)
        if b < 2:
            far(b + 2, issue)

    def relay(i):
        for j in range(1, chips):
            from_chip(i, j).wait_recv()
            forward(i, j, core).start()

    def complete(i):
        to_partner(i, partner).wait_recv()
        for j in range(1, chips):
            forward(i, j, 1 - core).wait_recv()

    def pick_rows(b):
        rows = [full[pl.ds(at + b * share, share)] for at in (0, half)]
        return jnp.concatenate([r.reshape(share * cap, r.shape[2]) for r in rows], axis=0)

    def expand(b):
        both(b, complete)
        tile = 256 if gate_w.shape[1] % 256 == 0 else gate_w.shape[1]

        for t in range(gate_w.shape[1] // tile):
            rows = pick_rows(b)
            at = pl.ds(t * tile, tile)
            gate = jnp.dot(rows, gate_w[:, at], preferred_element_type=f32)
            up = jnp.dot(rows, up_w[:, at], preferred_element_type=f32)
            gated[:, at] = (gate / (1.0 + jnp.exp(-gate)) * up).astype(bf16)

    def column(j):
        return lax.rem(chip + j, chips)

    def swap(i, j):
        return remote(
            cell(part, i, column(j) * 2 + 1 - core),
            pair.at[i, j],
            s_s.at[j, i],
            s_r.at[j, i],
            me,
            partner,
        )

    def cross(i, j):
        return remote(
            out_x.at[i, j], in_x.at[i, j], c_s.at[j, i], c_r.at[j, i], me, column(j) * 2 + core
        )

    def home(i):
        return remote(total.at[i], ret.at[i], h_s.at[i], h_r.at[i], flip(me, i, n), mine)

    def contract(b):
        tile = 256

        for t in range(part.shape[2] // tile):
            at = pl.ds(t * tile, tile)
            value = jnp.dot(gated[...], down_w[:, at], preferred_element_type=f32)
            value = value.astype(bf16).reshape(2, share, cap, tile)
            for side in range(2):
                part[pl.ds(side * half + b * share, share), :, at] = value[side]

        def begin(i):
            for j in list(range(1, chips)) + [0]:
                swap(i, j).start()

        both(b, begin)

    def paired(i, j):
        swap(i, j).wait_recv()
        head = pl.multiple_of((column(j) * 2 + core) * width, 128)
        return part[i, :, pl.ds(head, width)].astype(f32) + pair[i, j].astype(f32)

    def pass_on(i):
        for j in range(1, chips):
            out_x[i, j] = paired(i, j).astype(bf16)
            cross(i, j).start()

    def gather(i):
        value = paired(i, 0)
        for j in range(1, chips):
            cross(i, j).wait_recv()
            value = value + in_x[i, j].astype(f32)
        return value.astype(bf16)

    def send_home(i):
        total[i] = gather(i)
        home(i).start()

    def combine(i):
        e = flip(me, i, n)
        place = lax.broadcasted_iota(jnp.int32, (tokens, cap), 1).astype(f32)
        chosen = lax.broadcasted_iota(jnp.int32, (tokens, n), 1) == e

        def own_column(ref):
            return jnp.sum(jnp.where(chosen, ref[...], 0.0), axis=1, keepdims=True)

        pick = jnp.where(own_column(rank_col) == place, 1.0, 0.0).astype(bf16)
        value = jnp.dot(pick, ret[i], preferred_element_type=f32)
        acc[...] += own_column(weight_col) * value

    def receive(i):
        home(i).wait_recv()
        combine(i)

    near(0, arrive, 1)
    near(1, arrive)
    far(1, issue)
    near(0, relay)
    near(2, arrive)
    arrive_far(0)
    near(1, relay)
    near(3, arrive)
    acc[...] = hidden_ref[...]
    near(2, relay)
    far(0, relay)
    near(3, relay)
    for copy in weights:
        copy.wait()
    for b in range(4):
        expand(b)
        if b > 0:
            far(b - 1, send_home)
        if b < 3:
            arrive_far(b + 1)
        contract(b)
        far(b, pass_on)
        if b < 3:
            far(b + 1, relay)
        if b == 1:
            ret[0] = gather(0)
            near(0, send_home, 1)
        elif b > 1:
            near(b - 1, send_home)
        near(b, pass_on)
    combine(0)
    near(0, receive, 1)
    near(1, receive)
    far(3, send_home)
    near(3, send_home)
    far(0, receive)
    near(2, receive)
    far(1, receive)
    far(2, receive)
    near(3, receive)
    far(3, receive)
    layer_ref[...] = acc[...].astype(bf16)

    @pl.loop(0, n)
    def _(i):
        to_partner(i, mine).wait_send()
        for j in range(1, chips):
            forward(i, j, core).wait_send()
            to_chip(i, j).wait_send()
            cross(i, j).wait_send()
        for j in range(chips):
            swap(i, j).wait_send()

    @pl.loop(1, n)
    def _(i):
        sent(i).wait_send()
        home(i).wait_send()


def experts(hidden, normed, ranks, rank_col, weight_col, gate, up, down, n, heads):
    chips = heads // 2
    tokens, width = normed.shape
    cap = -(-3 * tokens // n // 16) * 16
    dma = pltpu.SemaphoreType.DMA
    bf16, f32 = jnp.bfloat16, jnp.float32
    vmem, hbm = pl.BlockSpec(memory_space=pltpu.VMEM), pl.BlockSpec(memory_space=pl.ANY)
    block = pltpu.VMEM((n, cap, width), bf16)
    piece = pltpu.VMEM((n, chips, cap, width), bf16)
    wide = pltpu.VMEM((n, cap, width * heads), bf16)
    return pl.pallas_call(
        functools.partial(moe_kernel, n, chips),
        out_shape=jax.ShapeDtypeStruct((tokens, width), bf16),
        in_specs=[vmem] * 5 + [hbm] * 3,
        out_specs=vmem,
        scratch_shapes=[
            pltpu.VMEM(gate.shape, gate.dtype),
            pltpu.VMEM(up.shape, up.dtype),
            pltpu.VMEM(down.shape, down.dtype),
            block,
            wide,
            pltpu.VMEM((n // 4 * cap, gate.shape[1]), bf16),
            wide,
            piece,
            piece,
            piece,
            block,
            block,
            pltpu.VMEM((tokens, width), f32),
        ]
        + [dma((3,))]
        + [dma((n,))] * 4
        + [dma((chips, n))] * 8
        + [dma((n,))] * 2,
        compiler_params=pltpu.CompilerParams(
            collective_id=0, has_side_effects=True, vmem_limit_bytes=60 * 1024 * 1024
        ),
        name="experts",
    )(hidden, normed, ranks, rank_col, weight_col, gate, up, down)


def attend_kernel(
    n,
    heads,
    flat,
    lengths_ref,
    q_ref,
    k_ref,
    v_ref,
    gain_ref,
    w_ref,
    res_ref,
    norm_ref,
    ids_ref,
    route_ref,
    hidden_ref,
    normed_ref,
    rank_row,
    rank_col,
    weight_col,
    wall,
    allowed,
    keep,
    carry,
    fresh,
    give,
    peer,
    before,
    after,
    lend,
    state,
    attn,
    headed,
    acc,
    mixed,
    beside_core,
    parts,
    sum_out,
    sum_in,
    squared,
    sq_own,
    sq_all,
    here,
    y_s,
    y_r,
    m_s,
    m_r,
    f_s,
    f_r,
    b_s,
    b_r,
    c_s,
    c_r,
    d_s,
    d_r,
    e_s,
    e_r,
    k_s,
    k_r,
    r_s,
    r_r,
    o_s,
    o_r,
    q_s,
    q_r,
):
    me, chip, core = seat()
    mine = chip * 2 + core
    rows, feats = q_ref.shape
    size = HEAD_DIM
    local, slots, group, col = feats // size, n // 2, n // heads, w_ref.shape[1]
    chips = heads // 2
    strips, width = wall.shape[1], wall.shape[3]
    pieces, share = 2 * strips, w_ref.shape[0] // 2
    f32, bf16 = jnp.float32, jnp.bfloat16
    beside, across = flip(me, 1, n), flip(me, 2, n)

    own = [
        pltpu.make_async_copy(
            w_ref.at[:, pl.ds(c * width, width)], wall.at[0, c], here.at[c]
        )
        for c in range(strips)
    ]
    for copy in own:
        copy.start()

    barrier = pltpu.get_barrier_semaphore()

    def tell(ctx, head):
        pl.semaphore_signal(barrier, inc=1, device_id=(ctx, head), device_id_type=MESH)

    tell(beside, mine)
    tell(across, mine)
    for q in range(1, slots // 2):
        tell(flip(me, 4 * q, n), mine)
    for step in (2, n - 2):
        tell(lax.rem(me + step, n), mine)
    for j in range(1, heads):
        tell(me, lax.rem(mine + j, heads))

    pl.semaphore_wait(barrier, 3 + slots // 2 + heads - 1)

    def piece(slot, k):
        return wall.at[slot, lax.div(k, 2), pl.ds(lax.rem(k, 2) * share, share)]

    def to_beside(k):
        return remote(piece(0, k), piece(1, k), y_s.at[k], y_r.at[k], beside, mine)

    def to_far(q, k):
        to = flip(me, 4 * q, n)
        return remote(piece(0, k), piece(2 * q, k), m_s.at[q, k], m_r.at[q, k], to, mine)

    def pass_far(q, k):
        return remote(
            piece(2 * q, k), piece(2 * q + 1, k), f_s.at[q, k], f_r.at[q, k], beside, mine
        )

    for c in range(strips):
        own[c].wait()
        if c == 0:
            for k in range(AHEAD):
                to_far(1, k).start()

    base = me * rows
    starts, last = [0], base + rows - 1
    for e in range(lengths_ref.shape[0] - 1):
        starts.append(starts[-1] + lengths_ref[e])
    odd, pair = lax.rem(me, 2), lax.div(me, 2)
    middle = (2 * pair + 1) * rows
    open_at, open_middle, open_end = jnp.int32(0), jnp.int32(0), jnp.int32(0)
    for s in starts[1:]:
        open_at = jnp.where(s <= last, s, open_at)
        open_middle = jnp.where(s < middle, s, open_middle)
        open_end = jnp.where(s < middle + rows, s, open_end)

    def opened(shape):
        place = lax.broadcasted_iota(jnp.int32, shape, 0) + base
        seg = jnp.zeros(shape, jnp.int32)
        for s in starts[1:]:
            seg = jnp.where(place >= s, s, seg)
        return place, seg

    place, seg = opened((rows, size))
    keep[...] = jnp.where(place >= open_at, 1.0, 0.0)
    carry[...] = jnp.where(seg < base, 1.0, 0.0)
    place, seg = opened((rows, rows))
    source = lax.broadcasted_iota(jnp.int32, (rows, rows), 1) + base
    allowed[...] = jnp.where((source <= place) & (source >= seg), 1.0, 0.0)
    even_joins = jnp.where(open_middle < middle - rows, 1.0, 0.0)
    odd_joins = jnp.where(open_end < middle, 1.0, 0.0)

    def columns(h):
        return pl.ds(pl.multiple_of(h * size, size), size)

    def lifted(ref, h):
        x = ref[:, columns(h)].astype(f32)
        return x / (1.0 + jnp.exp(-x))

    def fresh_state(h):
        kept = lifted(k_ref, h) * keep[...]
        return jnp.dot(kept.T.astype(bf16), v_ref[:, columns(h)], preferred_element_type=f32)

    half = local // 2
    bundle = half // 2
    mine_at, other_at = odd * half, (1 - odd) * half

    def some(g):
        return pl.ds(g * bundle, bundle)

    def my_some(g):
        return pl.ds(mine_at + g * bundle, bundle)

    def to_peer(g):
        return remote(give.at[some(g)], peer.at[some(g)], b_s.at[g], b_r.at[g], beside, mine)

    def chain(g):
        to = lax.rem(me + 2, n)
        return remote(after.at[some(g)], before.at[some(g)], c_s.at[g], c_r.at[g], to, mine)

    def to_state(g):
        return remote(lend.at[some(g)], state.at[my_some(g)], d_s.at[g], d_r.at[g], beside, mine)

    for g in range(2):

        @pl.loop(g * bundle, (g + 1) * bundle)
        def _(i):
            give[i] = fresh_state(other_at + i).astype(bf16)

        to_peer(g).start()

    for k in range(2):
        to_beside(k).start()

    @pl.loop(0, half)
    def _(i):
        fresh[i] = fresh_state(mine_at + i)

    @pl.when(pair == 0)
    def _():
        before[...] = jnp.zeros_like(before)

    def turn():
        @pl.loop(0, 2)
        def _(g):
            to_peer(g).wait_recv()

            @pl.when(pair > 0)
            def _():
                chain(g).wait_recv()

            held, theirs = fresh[some(g)], peer[some(g)].astype(f32)
            past = before[some(g)].astype(f32)
            between = jnp.where(odd == 0, held, theirs) + even_joins * past

            @pl.when(pair < n // 2 - 1)
            def _():
                total = jnp.where(odd == 0, theirs, held) + odd_joins * between
                after[some(g)] = total.astype(bf16)
                chain(g).start()

            lend[some(g)] = jnp.where(odd == 0, between, past).astype(bf16)
            to_state(g).start()
            state[my_some(g)] = jnp.where(odd == 0, past, between).astype(bf16)

    def inside(h):
        scores = lax.dot_general(
            lifted(q_ref, h).astype(bf16),
            lifted(k_ref, h).astype(bf16),
            (((1,), (1,)), ((), ())),
            preferred_element_type=f32,
        )
        attn[:, columns(h)] = jnp.dot(
            (scores * allowed[...]).astype(bf16), v_ref[:, columns(h)], preferred_element_type=f32
        )

    services = pieces * (slots // 2 - 1)
    many = -(-local // 3)

    def serve(j):
        q, k = lax.div(j, pieces) + 1, lax.rem(j, pieces)
        to_far(q, k).wait_recv()
        pass_far(q, k).start()

        @pl.when(j + AHEAD < services)
        def _():
            to_far(lax.div(j + AHEAD, pieces) + 1, lax.rem(j + AHEAD, pieces)).start()

        @pl.when(j < pieces - 2)
        def _():
            to_beside(j + 2).start()

    moment = jnp.minimum(pair, services - 3)

    def insides(j):
        @pl.loop(j * many, (j + 1) * many)
        def _(h):
            @pl.when(h < local)
            def _():
                inside(h)

    def finish(h):
        outside = jnp.dot(lifted(q_ref, h).astype(bf16), state[h], preferred_element_type=f32)
        full = attn[:, columns(h)] + outside * carry[...]
        mean_square = jnp.mean(full * full, axis=1, keepdims=True)
        scaled = full * lax.rsqrt(mean_square + 1e-06) * gain_ref[:, columns(h)]
        at = pl.multiple_of(lax.rem(h, half) * size, size)
        headed[lax.div(h, half), :, pl.ds(at, size)] = scaled.astype(bf16)

    def exchange(p):
        return remote(headed.at[p], headed.at[2 + p], e_s.at[p], e_r.at[p], across, mine)

    def finish_all():
        for g in range(2):
            to_state(g).wait_recv()
        for p in range(2):

            @pl.loop(p * half, (p + 1) * half)
            def _(h):
                finish(h)

            exchange(p).start()

    @pl.loop(0, services - 2)
    def _(j):
        @pl.when(j == moment)
        def _():
            turn()

        insides(j)

        @pl.when(j == jnp.maximum(moment, 2))
        def _():
            finish_all()

        serve(j)

    def route():
        expert = lax.broadcasted_iota(jnp.int32, (n, rows), 0)
        first = ids_ref[0:1, :] == expert
        second = ids_ref[1:2, :] == expert
        raw = route_ref[...].astype(f32)
        shares = raw / (raw[0:1, :] + raw[1:2, :])
        weight = jnp.where(first, shares[0:1, :], 0.0) + jnp.where(second, shares[1:2, :], 0.0)
        named = first | second
        earlier = (
            lax.broadcasted_iota(jnp.int32, (rows, rows), 0)
            < lax.broadcasted_iota(jnp.int32, (rows, rows), 1)
        ).astype(f32)
        count = jnp.dot(
            jnp.where(named, 1.0, 0.0).astype(bf16), earlier.astype(bf16), preferred_element_type=f32
        )
        rank = jnp.where(named, count, -1.0)
        for e in range(n):
            rank_row[e] = jnp.broadcast_to(rank[e : e + 1, :], (8, rows))
        rank_col[...] = rank.T
        weight_col[...] = weight.T

    def mask_of(s):
        return 4 * lax.div(s, 2) + lax.rem(s, 2)

    def block_of(s):
        return flip(me, mask_of(s), n)

    def owner_of(s):
        head = lax.div(block_of(s), group)
        return lax.div(head, 2), lax.rem(head, 2)

    def to_core(s, c, u):
        at = s * strips + c
        return remote(
            mixed.at[u, at],
            beside_core.at[u, at],
            k_s.at[u, at],
            k_r.at[u, at],
            me,
            chip * 2 + 1 - core,
        )

    def to_owner(s, c, u, to, rel):
        at = s * strips + c
        return remote(
            mixed.at[u, at], parts.at[u, at, rel], r_s.at[u, at], r_r.at[u, at, rel], me, to
        )

    def project(s, some_strips, u):
        deep = wall.shape[2] // 2
        value = 0.0
        for p in range(2):
            block = [wall[s, c, p * deep : (p + 1) * deep] for c in some_strips]
            value += jnp.dot(
                headed[2 * u + p], jnp.concatenate(block, axis=1), preferred_element_type=f32
            )
        for i, c in enumerate(some_strips):
            tile = value[:, i * width : (i + 1) * width]
            acc[u, s * strips + c] = tile
            mixed[u, s * strips + c] = tile.astype(bf16)

    def send(s, some_strips, u):
        @pl.when(owner_of(s)[1] != core)
        def _():
            for c in some_strips:
                to_core(s, c, u).start()

    def presum(s, some_strips, u):
        owner_chip, owner_core = owner_of(s)

        @pl.when(owner_core == core)
        def _():
            for c in some_strips:
                at = s * strips + c
                to_core(s, c, u).wait_recv()
                value = acc[u, at] + beside_core[u, at].astype(f32)
                acc[u, at] = value
                mixed[u, at] = value.astype(bf16)

            @pl.when(owner_chip != chip)
            def _():
                rel = lax.rem(chip - owner_chip + chips, chips)
                for c in some_strips:
                    to_owner(s, c, u, owner_chip * 2 + core, rel).start()

    def work(low, high, step, first, last, u):
        some_strips = list(range(first, last))
        if not some_strips:
            return
        count = (high - low) // step
        for body in (project, send, presum):

            @pl.loop(0, count, unroll=count <= 4)
            def _(i):
                body(low + i * step, some_strips, u)

    def passed(k):
        @pl.loop(1, slots // 2)
        def _(q):
            pass_far(q, k).wait_recv()

    for k in range(pieces):
        to_beside(k).wait_recv()
    work(0, 2, 1, 0, strips, 0)
    work(2, slots, 2, 0, strips - 1, 0)
    route()
    serve(services - 2)
    for k in range(pieces - 2):
        passed(k)
    work(3, slots + 1, 2, 0, strips - 1, 0)
    serve(services - 1)
    for p in range(2):
        exchange(p).wait_recv()
    work(0, slots, 1, 0, strips - 1, 1)
    work(2, slots, 2, strips - 1, strips, 1)
    work(0, 2, 1, strips - 1, strips, 1)
    passed(pieces - 2)
    passed(pieces - 1)
    work(3, slots + 1, 2, strips - 1, strips, 1)
    work(2, slots, 1, strips - 1, strips, 0)

    def summed(s, c, u):
        value = acc[u, s * strips + c]
        for rel in range(1, chips):
            to_owner(s, c, u, mine, rel).wait_recv()
            value = value + parts[u, s * strips + c, rel].astype(f32)
        return value

    def cell(ref, b, c):
        if flat:
            return ref.at[:, pl.ds(pl.multiple_of(b * col + c * width, 128), width)]
        return ref.at[b]

    def hand_over(s, c):
        at = s * strips + c
        return remote(sum_out.at[at], sum_in.at[at], o_s.at[at], o_r.at[at], across, mine)

    def settle(block, c, value):
        b = block - group * mine
        total = value + cell(res_ref, b, c)[...].astype(f32)
        cell(hidden_ref, b, c)[...] = total
        squared[...] += total * total

    squared[...] = jnp.zeros_like(squared)

    def owned(first, last, body, seat_of=None):
        @pl.loop(0, slots)
        def _(s):
            block = block_of(s) if seat_of is None else flip(seat_of, mask_of(s), n)

            @pl.when(lax.div(block, group) == mine)
            def _():
                @pl.loop(first, last)
                def _(c):
                    body(block, s, c)

    def reduce_other(block, s, c):
        sum_out[s * strips + c] = summed(s, c, 1).astype(bf16)
        hand_over(s, c).start()

    def reduce_own(block, s, c):
        settle(block, c, summed(s, c, 0))

    def take(block, s, c):
        hand_over(s, c).wait_recv()
        settle(block, c, sum_in[s * strips + c].astype(f32))

    owned(0, strips - 1, reduce_other)
    owned(0, strips - 1, reduce_own)
    owned(strips - 1, strips, reduce_other)
    owned(strips - 1, strips, reduce_own)
    owned(0, strips, take, across)

    sq_own[...] = lax.dot_general(
        jnp.ones((8, width), f32),
        squared[...],
        (((1,), (1,)), ((), ())),
        precision=highest,
        preferred_element_type=f32,
    )

    def spread(j, to, slot):
        return remote(sq_own, sq_all.at[slot], q_s.at[j], q_r.at[j], me, to)

    for j in range(1, heads):
        spread(j, lax.rem(mine + j, heads), j).start()
    squares = sq_own[...]
    for j in range(1, heads):
        spread(j, mine, j).wait_recv()
        squares = squares + sq_all[j]
    scale = lax.rsqrt(squares / (col * n) + 1e-06).T[:, 0:1]
    if flat:
        normed_ref[...] = (hidden_ref[...] * scale * norm_ref[...][None, :]).astype(bf16)
    else:
        for p in range(group):
            normed_ref[p] = (hidden_ref[p] * scale * norm_ref[p]).astype(bf16)

    for j in range(1, heads):
        spread(j, mine, j).wait_send()
    for p in range(2):
        exchange(p).wait_send()
    for k in range(pieces):
        to_beside(k).wait_send()

    @pl.loop(0, services)
    def _(j):
        q, k = lax.div(j, pieces) + 1, lax.rem(j, pieces)
        to_far(q, k).wait_send()
        pass_far(q, k).wait_send()

    for g in range(2):
        to_peer(g).wait_send()
        to_state(g).wait_send()

    @pl.when(pair < n // 2 - 1)
    def _():
        for g in range(2):
            chain(g).wait_send()

    @pl.loop(0, slots)
    def _(s):
        owner_chip, owner_core = owner_of(s)
        relay = owner_core == core

        @pl.loop(0, strips)
        def _(c):
            @pl.when(jnp.logical_not(relay))
            def _():
                for u in range(2):
                    to_core(s, c, u).wait_send()

            @pl.when(relay & (owner_chip != chip))
            def _():
                for u in range(2):
                    to_owner(s, c, u, mine, 0).wait_send()

            @pl.when(relay & (owner_chip == chip))
            def _():
                hand_over(s, c).wait_send()


def attend(
    lengths, query, key, value, gain, weight, residual, norm_gain, ids, route, n, heads
):
    rows, feats = query.shape
    col, group, slots = weight.shape[1], n // heads, n // 2
    local, flat = feats // HEAD_DIM, col % 128 == 0
    strips = col // 128 if flat else 1
    width, depth = col // strips, weight.shape[0]
    dma = pltpu.SemaphoreType.DMA
    bf16, f32 = jnp.bfloat16, jnp.float32
    vmem = pl.BlockSpec(memory_space=pltpu.VMEM)
    if not flat:
        norm_gain = norm_gain.reshape(group, 1, col)
    shape = (rows, group * col) if flat else (group, rows, col)
    if not flat:
        residual = jnp.swapaxes(residual.reshape(rows, group, col), 0, 1)
    hidden, normed, *routing = pl.pallas_call(
        functools.partial(attend_kernel, n, heads, flat),
        out_shape=(
            jax.ShapeDtypeStruct(shape, f32),
            jax.ShapeDtypeStruct(shape, bf16),
            jax.ShapeDtypeStruct((n, 8, rows), f32),
            jax.ShapeDtypeStruct((rows, n), f32),
            jax.ShapeDtypeStruct((rows, n), f32),
        ),
        in_specs=[pl.BlockSpec(memory_space=pltpu.SMEM)]
        + [vmem] * 4
        + [pl.BlockSpec(memory_space=pl.ANY)]
        + [vmem] * 4,
        out_specs=(vmem,) * 5,
        scratch_shapes=[
            pltpu.VMEM((slots, strips, depth, width), bf16),
            pltpu.VMEM((rows, rows), f32),
            pltpu.VMEM((rows, HEAD_DIM), f32),
            pltpu.VMEM((rows, HEAD_DIM), f32),
            pltpu.VMEM((local // 2, HEAD_DIM, HEAD_DIM), f32),
        ]
        + [pltpu.VMEM((local // 2, HEAD_DIM, HEAD_DIM), bf16)] * 5
        + [
            pltpu.VMEM((local, HEAD_DIM, HEAD_DIM), bf16),
            pltpu.VMEM((rows, feats), f32),
            pltpu.VMEM((4, rows, feats // 2), bf16),
            pltpu.VMEM((2, slots * strips, rows, width), f32),
            pltpu.VMEM((2, slots * strips, rows, width), bf16),
            pltpu.VMEM((2, slots * strips, rows, width), bf16),
            pltpu.VMEM((2, slots * strips, heads // 2, rows, width), bf16),
            pltpu.VMEM((slots * strips, rows, width), bf16),
            pltpu.VMEM((slots * strips, rows, width), bf16),
            pltpu.VMEM((rows, width), f32),
            pltpu.VMEM((8, rows), f32),
            pltpu.VMEM((heads, 8, rows), f32),
            dma((strips,)),
        ]
        + [dma((2 * strips,))] * 2
        + [dma((slots // 2, 2 * strips))] * 4
        + [dma((2,))] * 8
        + [dma((2, slots * strips))] * 3
        + [
            dma((2, slots * strips, heads // 2)),
            dma((slots * strips,)),
            dma((slots * strips,)),
            dma((heads,)),
            dma((heads,)),
        ],
        compiler_params=pltpu.CompilerParams(
            collective_id=2, has_side_effects=True, vmem_limit_bytes=60 * 1024 * 1024
        ),
        name="attend",
    )(lengths, query, key, value, gain, weight, residual, norm_gain, ids, route)
    if not flat:
        hidden, normed = (jnp.swapaxes(a, 0, 1).reshape(rows, -1) for a in (hidden, normed))
    return hidden, normed, *routing


def on_device(
    query,
    key,
    value,
    episode_lengths,
    attn_gain,
    out_weight,
    residual,
    norm_gain,
    expert_ids,
    route_weights,
    gate_weight,
    up_weight,
    down_weight,
):
    n, heads = lax.axis_size("ctx"), lax.axis_size("head")
    tokens = attend(
        episode_lengths,
        query,
        key,
        value,
        attn_gain[None, :],
        out_weight,
        residual,
        norm_gain,
        expert_ids.T,
        route_weights.T,
        n,
        heads,
    )
    return experts(*tokens, gate_weight[0], up_weight[0], down_weight[0], n, heads)


def solution(mesh):
    placed = (
        P("ctx", "head"),
        P("ctx", "head"),
        P("ctx", "head"),
        P(),
        P("head"),
        P("head", "ctx"),
        P("ctx", "head"),
        P("head"),
        P("ctx", None),
        P("ctx", None),
        P("ctx", None, "head"),
        P("ctx", None, "head"),
        P("ctx", "head", None),
    )
    return jax.shard_map(
        on_device, mesh=mesh, in_specs=placed, out_specs=P("ctx", "head"), check_vma=False
    )
```

```python
import functools

import jax
import jax.numpy as jnp
from jax import lax
from jax.experimental import pallas as pl
from jax.experimental.pallas import tpu as pltpu
from jax.sharding import PartitionSpec as P

HEAD_DIM = 128
AHEAD = 2


highest = lax.Precision.HIGHEST


MESH = pl.DeviceIdType.MESH


def remote(src, dst, send, recv, ctx, head):
    return pltpu.make_async_remote_copy(
        src_ref=src,
        dst_ref=dst,
        send_sem=send,
        recv_sem=recv,
        device_id=(ctx, head),
        device_id_type=MESH,
    )


def seat():
    head = lax.axis_index("head")
    return lax.axis_index("ctx"), lax.div(head, 2), lax.rem(head, 2)


def flip(me, i, n):
    if n & (n - 1):
        return lax.rem(i - me + 2 * n, n)
    other, bit = me, 1
    while bit < n:
        on = lax.rem(lax.div(me, bit), 2)
        other = other + lax.rem(lax.div(i, bit), 2) * bit * (1 - 2 * on)
        bit *= 2
    return other


def moe_kernel(
    n,
    chips,
    hidden_ref,
    normed_ref,
    rank_row,
    rank_col,
    weight_col,
    gate_ref,
    up_ref,
    down_ref,
    layer_ref,
    gate_w,
    up_w,
    down_w,
    outb,
    full,
    gated,
    part,
    pair,
    out_x,
    in_x,
    total,
    ret,
    acc,
    w_s,
    a_s,
    a_r,
    p_s,
    p_r,
    x_s,
    x_r,
    f_s,
    f_r,
    s_s,
    s_r,
    c_s,
    c_r,
    h_s,
    h_r,
):
    me, chip, core = seat()
    f32, bf16 = jnp.float32, jnp.bfloat16
    tokens, width = normed_ref.shape
    cap = full.shape[1]
    mine, partner = chip * 2 + core, chip * 2 + 1 - core

    weights = [
        pltpu.make_async_copy(gate_ref, gate_w, w_s.at[0]),
        pltpu.make_async_copy(up_ref, up_w, w_s.at[1]),
        pltpu.make_async_copy(down_ref, down_w, w_s.at[2]),
    ]
    for copy in weights:
        copy.start()

    barrier = pltpu.get_barrier_semaphore()

    def tell(ctx, head):
        pl.semaphore_signal(barrier, inc=1, device_id=(ctx, head), device_id_type=MESH)

    tell(me, partner)
    for j in range(1, chips):
        tell(me, lax.rem(chip + j, chips) * 2 + core)

    @pl.loop(1, n)
    def _(i):
        tell(lax.rem(me + i, n), mine)

    def spread_of(i):
        row = rank_row[flip(me, i, n)][0:1, :]
        place = lax.broadcasted_iota(jnp.int32, (cap, tokens), 0).astype(f32)
        chosen = jnp.where(place == row, 1.0, 0.0).astype(bf16)
        return jnp.dot(chosen, normed_ref[...], preferred_element_type=f32).astype(bf16)

    def cell(ref, block, head):
        return ref.at[block, :, pl.ds(pl.multiple_of(head * width, 128), width)]

    full[0, :, pl.ds(pl.multiple_of(mine * width, 128), width)] = spread_of(0)

    pl.semaphore_wait(barrier, chips + n - 1)

    def to_partner(i, head):
        b = cell(full, i, head)
        return remote(b, b, p_s.at[i], p_r.at[i], me, partner)

    def to_chip(i, j):
        b = cell(full, i, mine)
        return remote(b, b, x_s.at[j, i], x_r.at[j, i], me, lax.rem(chip + j, chips) * 2 + core)

    def from_chip(i, j):
        b = cell(full, i, lax.rem(chip - j + chips, chips) * 2 + core)
        return remote(b, b, x_s.at[j, i], x_r.at[j, i], me, partner)

    def forward(i, j, which):
        b = cell(full, i, lax.rem(chip - j + chips, chips) * 2 + which)
        return remote(b, b, f_s.at[j, i], f_r.at[j, i], me, partner)

    def sent(i):
        return remote(
            outb.at[i], cell(full, i, mine), a_s.at[i], a_r.at[i], flip(me, i, n), mine
        )

    def spread(i):
        for j in range(1, chips):
            to_chip(i, j).start()
        to_partner(i, mine).start()

    spread(0)
    half = n // 2
    share = half // 4

    def issue(i):
        outb[i] = spread_of(i)
        sent(i).start()

    def near(b, body, skip=0):
        @pl.loop(b * share + skip, (b + 1) * share)
        def _(i):
            body(i)

    def far(b, body):
        near(b, lambda i: body(half + i))

    def both(b, body, skip=0):
        far(b, body)
        near(b, body, skip)

    far(0, issue)
    near(0, issue, 1)
    for b in range(1, 4):
        near(b, issue)

    def arrive(i):
        sent(i).wait_recv()
        spread(i)

    def relay(i):
        for j in range(1, chips):
            from_chip(i, j).wait_recv()
            forward(i, j, core).start()

    def complete(i):
        to_partner(i, partner).wait_recv()
        for j in range(1, chips):
            forward(i, j, 1 - core).wait_recv()

    def pick_rows(b):
        rows = [full[pl.ds(at + b * share, share)] for at in (0, half)]
        return jnp.concatenate([r.reshape(share * cap, r.shape[2]) for r in rows], axis=0)

    def expand(b):
        both(b, complete)
        tile = 256 if gate_w.shape[1] % 256 == 0 else gate_w.shape[1]

        for t in range(gate_w.shape[1] // tile):
            rows = pick_rows(b)
            at = pl.ds(t * tile, tile)
            gate = jnp.dot(rows, gate_w[:, at], preferred_element_type=f32)
            up = jnp.dot(rows, up_w[:, at], preferred_element_type=f32)
            gated[:, at] = (gate / (1.0 + jnp.exp(-gate)) * up).astype(bf16)

    def column(j):
        return lax.rem(chip + j, chips)

    def swap(i, j):
        return remote(
            cell(part, i, column(j) * 2 + 1 - core),
            pair.at[i, j],
            s_s.at[j, i],
            s_r.at[j, i],
            me,
            partner,
        )

    def cross(i, j):
        return remote(
            out_x.at[i, j], in_x.at[i, j], c_s.at[j, i], c_r.at[j, i], me, column(j) * 2 + core
        )

    def home(i):
        return remote(total.at[i], ret.at[i], h_s.at[i], h_r.at[i], flip(me, i, n), mine)

    def contract(b):
        tile = 256

        for t in range(part.shape[2] // tile):
            at = pl.ds(t * tile, tile)
            value = jnp.dot(gated[...], down_w[:, at], preferred_element_type=f32)
            value = value.astype(bf16).reshape(2, share, cap, tile)
            for side in range(2):
                part[pl.ds(side * half + b * share, share), :, at] = value[side]

        def begin(i):
            for j in list(range(1, chips)) + [0]:
                swap(i, j).start()

        both(b, begin)

    def paired(i, j):
        swap(i, j).wait_recv()
        head = pl.multiple_of((column(j) * 2 + core) * width, 128)
        return part[i, :, pl.ds(head, width)].astype(f32) + pair[i, j].astype(f32)

    def pass_on(i):
        for j in range(1, chips):
            out_x[i, j] = paired(i, j).astype(bf16)
            cross(i, j).start()

    def gather(i):
        value = paired(i, 0)
        for j in range(1, chips):
            cross(i, j).wait_recv()
            value = value + in_x[i, j].astype(f32)
        return value.astype(bf16)

    def send_home(i):
        total[i] = gather(i)
        home(i).start()

    def combine(i):
        e = flip(me, i, n)
        place = lax.broadcasted_iota(jnp.int32, (tokens, cap), 1).astype(f32)
        chosen = lax.broadcasted_iota(jnp.int32, (tokens, n), 1) == e

        def own_column(ref):
            return jnp.sum(jnp.where(chosen, ref[...], 0.0), axis=1, keepdims=True)

        pick = jnp.where(own_column(rank_col) == place, 1.0, 0.0).astype(bf16)
        value = jnp.dot(pick, ret[i], preferred_element_type=f32)
        acc[...] += own_column(weight_col) * value

    def receive(i):
        home(i).wait_recv()
        combine(i)

    near(0, arrive, 1)
    near(1, arrive)
    far(1, issue)
    near(0, relay)
    near(2, arrive)
    far(0, arrive)
    far(2, issue)
    near(1, relay)
    near(3, arrive)
    acc[...] = hidden_ref[...]
    near(2, relay)
    far(0, relay)
    near(3, relay)
    for copy in weights:
        copy.wait()
    @pl.loop(0, 4)
    def _(b):
        expand(b)

        @pl.when(b > 0)
        def _():
            far(b - 1, send_home)

        @pl.when(b < 3)
        def _():
            far(b + 1, arrive)

        @pl.when(b < 1)
        def _():
            far(b + 3, issue)

        contract(b)
        far(b, pass_on)

        @pl.when(b < 3)
        def _():
            far(b + 1, relay)

        @pl.when(b == 1)
        def _():
            ret[0] = gather(0)
            near(0, send_home, 1)

        @pl.when(b > 1)
        def _():
            near(b - 1, send_home)

        near(b, pass_on)

    combine(0)
    near(0, receive, 1)
    near(1, receive)
    far(3, send_home)
    near(3, send_home)
    far(0, receive)
    near(2, receive)
    far(1, receive)
    far(2, receive)
    near(3, receive)
    far(3, receive)
    layer_ref[...] = acc[...].astype(bf16)

    @pl.loop(0, n)
    def _(i):
        to_partner(i, mine).wait_send()
        for j in range(1, chips):
            forward(i, j, core).wait_send()
            to_chip(i, j).wait_send()
            cross(i, j).wait_send()
        for j in range(chips):
            swap(i, j).wait_send()

    @pl.loop(1, n)
    def _(i):
        sent(i).wait_send()
        home(i).wait_send()


def experts(hidden, normed, ranks, rank_col, weight_col, gate, up, down, n, heads):
    chips = heads // 2
    tokens, width = normed.shape
    cap = -(-3 * tokens // n // 16) * 16
    dma = pltpu.SemaphoreType.DMA
    bf16, f32 = jnp.bfloat16, jnp.float32
    vmem, hbm = pl.BlockSpec(memory_space=pltpu.VMEM), pl.BlockSpec(memory_space=pl.ANY)
    block = pltpu.VMEM((n, cap, width), bf16)
    piece = pltpu.VMEM((n, chips, cap, width), bf16)
    wide = pltpu.VMEM((n, cap, width * heads), bf16)
    return pl.pallas_call(
        functools.partial(moe_kernel, n, chips),
        out_shape=jax.ShapeDtypeStruct((tokens, width), bf16),
        in_specs=[vmem] * 5 + [hbm] * 3,
        out_specs=vmem,
        scratch_shapes=[
            pltpu.VMEM(gate.shape, gate.dtype),
            pltpu.VMEM(up.shape, up.dtype),
            pltpu.VMEM(down.shape, down.dtype),
            block,
            wide,
            pltpu.VMEM((n // 4 * cap, gate.shape[1]), bf16),
            wide,
            piece,
            piece,
            piece,
            block,
            block,
            pltpu.VMEM((tokens, width), f32),
        ]
        + [dma((3,))]
        + [dma((n,))] * 4
        + [dma((chips, n))] * 8
        + [dma((n,))] * 2,
        compiler_params=pltpu.CompilerParams(
            collective_id=0, has_side_effects=True, vmem_limit_bytes=60 * 1024 * 1024
        ),
        name="experts",
    )(hidden, normed, ranks, rank_col, weight_col, gate, up, down)


def attend_kernel(
    n,
    heads,
    flat,
    lengths_ref,
    q_ref,
    k_ref,
    v_ref,
    gain_ref,
    w_ref,
    res_ref,
    norm_ref,
    ids_ref,
    route_ref,
    hidden_ref,
    normed_ref,
    rank_row,
    rank_col,
    weight_col,
    wall,
    allowed,
    keep,
    carry,
    fresh,
    give,
    peer,
    before,
    after,
    lend,
    state,
    attn,
    headed,
    acc,
    mixed,
    beside_core,
    parts,
    sum_out,
    sum_in,
    squared,
    sq_own,
    sq_all,
    here,
    y_s,
    y_r,
    m_s,
    m_r,
    f_s,
    f_r,
    b_s,
    b_r,
    c_s,
    c_r,
    d_s,
    d_r,
    e_s,
    e_r,
    k_s,
    k_r,
    r_s,
    r_r,
    o_s,
    o_r,
    q_s,
    q_r,
):
    me, chip, core = seat()
    mine = chip * 2 + core
    rows, feats = q_ref.shape
    size = HEAD_DIM
    local, slots, group, col = feats // size, n // 2, n // heads, w_ref.shape[1]
    chips = heads // 2
    strips, width = wall.shape[1], wall.shape[3]
    pieces, share = 2 * strips, w_ref.shape[0] // 2
    f32, bf16 = jnp.float32, jnp.bfloat16
    beside, across = flip(me, 1, n), flip(me, 2, n)

    own = [
        pltpu.make_async_copy(
            w_ref.at[:, pl.ds(c * width, width)], wall.at[0, c], here.at[c]
        )
        for c in range(strips)
    ]
    for copy in own:
        copy.start()

    barrier = pltpu.get_barrier_semaphore()

    def tell(ctx, head):
        pl.semaphore_signal(barrier, inc=1, device_id=(ctx, head), device_id_type=MESH)

    tell(beside, mine)
    tell(across, mine)
    for q in range(1, slots // 2):
        tell(flip(me, 4 * q, n), mine)
    for step in (2, n - 2):
        tell(lax.rem(me + step, n), mine)
    for j in range(1, heads):
        tell(me, lax.rem(mine + j, heads))

    pl.semaphore_wait(barrier, 3 + slots // 2 + heads - 1)

    def piece(slot, k):
        return wall.at[slot, lax.div(k, 2), pl.ds(lax.rem(k, 2) * share, share)]

    def to_beside(k):
        return remote(piece(0, k), piece(1, k), y_s.at[k], y_r.at[k], beside, mine)

    def to_far(q, k):
        to = flip(me, 4 * q, n)
        return remote(piece(0, k), piece(2 * q, k), m_s.at[q, k], m_r.at[q, k], to, mine)

    def pass_far(q, k):
        return remote(
            piece(2 * q, k), piece(2 * q + 1, k), f_s.at[q, k], f_r.at[q, k], beside, mine
        )

    for c in range(strips):
        own[c].wait()
        if c == 0:
            for k in range(AHEAD):
                to_far(1, k).start()

    base = me * rows
    starts, last = [0], base + rows - 1
    for e in range(lengths_ref.shape[0] - 1):
        starts.append(starts[-1] + lengths_ref[e])
    odd, pair = lax.rem(me, 2), lax.div(me, 2)
    middle = (2 * pair + 1) * rows
    open_at, open_middle, open_end = jnp.int32(0), jnp.int32(0), jnp.int32(0)
    for s in starts[1:]:
        open_at = jnp.where(s <= last, s, open_at)
        open_middle = jnp.where(s < middle, s, open_middle)
        open_end = jnp.where(s < middle + rows, s, open_end)

    def opened(shape):
        place = lax.broadcasted_iota(jnp.int32, shape, 0) + base
        seg = jnp.zeros(shape, jnp.int32)
        for s in starts[1:]:
            seg = jnp.where(place >= s, s, seg)
        return place, seg

    place, seg = opened((rows, size))
    keep[...] = jnp.where(place >= open_at, 1.0, 0.0)
    carry[...] = jnp.where(seg < base, 1.0, 0.0)
    place, seg = opened((rows, rows))
    source = lax.broadcasted_iota(jnp.int32, (rows, rows), 1) + base
    allowed[...] = jnp.where((source <= place) & (source >= seg), 1.0, 0.0)
    even_joins = jnp.where(open_middle < middle - rows, 1.0, 0.0)
    odd_joins = jnp.where(open_end < middle, 1.0, 0.0)

    def columns(h):
        return pl.ds(pl.multiple_of(h * size, size), size)

    def lifted(ref, h):
        x = ref[:, columns(h)].astype(f32)
        return x / (1.0 + jnp.exp(-x))

    def fresh_state(h):
        kept = lifted(k_ref, h) * keep[...]
        return jnp.dot(kept.T.astype(bf16), v_ref[:, columns(h)], preferred_element_type=f32)

    half = local // 2
    bundle = half // 2
    mine_at, other_at = odd * half, (1 - odd) * half

    def some(g):
        return pl.ds(g * bundle, bundle)

    def my_some(g):
        return pl.ds(mine_at + g * bundle, bundle)

    def to_peer(g):
        return remote(give.at[some(g)], peer.at[some(g)], b_s.at[g], b_r.at[g], beside, mine)

    def chain(g):
        to = lax.rem(me + 2, n)
        return remote(after.at[some(g)], before.at[some(g)], c_s.at[g], c_r.at[g], to, mine)

    def to_state(g):
        return remote(lend.at[some(g)], state.at[my_some(g)], d_s.at[g], d_r.at[g], beside, mine)

    for g in range(2):

        @pl.loop(g * bundle, (g + 1) * bundle)
        def _(i):
            give[i] = fresh_state(other_at + i).astype(bf16)

        to_peer(g).start()

    for k in range(2):
        to_beside(k).start()

    @pl.loop(0, half)
    def _(i):
        fresh[i] = fresh_state(mine_at + i)

    @pl.when(pair == 0)
    def _():
        before[...] = jnp.zeros_like(before)

    def turn():
        @pl.loop(0, 2)
        def _(g):
            to_peer(g).wait_recv()

            @pl.when(pair > 0)
            def _():
                chain(g).wait_recv()

            held, theirs = fresh[some(g)], peer[some(g)].astype(f32)
            past = before[some(g)].astype(f32)
            between = jnp.where(odd == 0, held, theirs) + even_joins * past

            @pl.when(pair < n // 2 - 1)
            def _():
                total = jnp.where(odd == 0, theirs, held) + odd_joins * between
                after[some(g)] = total.astype(bf16)
                chain(g).start()

            lend[some(g)] = jnp.where(odd == 0, between, past).astype(bf16)
            to_state(g).start()
            state[my_some(g)] = jnp.where(odd == 0, past, between).astype(bf16)

    def inside(h):
        scores = lax.dot_general(
            lifted(q_ref, h).astype(bf16),
            lifted(k_ref, h).astype(bf16),
            (((1,), (1,)), ((), ())),
            preferred_element_type=f32,
        )
        attn[:, columns(h)] = jnp.dot(
            (scores * allowed[...]).astype(bf16), v_ref[:, columns(h)], preferred_element_type=f32
        )

    services = pieces * (slots // 2 - 1)
    many = -(-local // 3)

    def serve(j):
        q, k = lax.div(j, pieces) + 1, lax.rem(j, pieces)
        to_far(q, k).wait_recv()
        pass_far(q, k).start()

        @pl.when(j + AHEAD < services)
        def _():
            to_far(lax.div(j + AHEAD, pieces) + 1, lax.rem(j + AHEAD, pieces)).start()

        @pl.when(j < pieces - 2)
        def _():
            to_beside(j + 2).start()

    moment = jnp.minimum(pair, services - 3)

    def insides(j):
        @pl.loop(j * many, (j + 1) * many)
        def _(h):
            @pl.when(h < local)
            def _():
                inside(h)

    def finish(h):
        outside = jnp.dot(lifted(q_ref, h).astype(bf16), state[h], preferred_element_type=f32)
        full = attn[:, columns(h)] + outside * carry[...]
        mean_square = jnp.mean(full * full, axis=1, keepdims=True)
        scaled = full * lax.rsqrt(mean_square + 1e-06) * gain_ref[:, columns(h)]
        at = pl.multiple_of(lax.rem(h, half) * size, size)
        headed[lax.div(h, half), :, pl.ds(at, size)] = scaled.astype(bf16)

    def exchange(p):
        return remote(headed.at[p], headed.at[2 + p], e_s.at[p], e_r.at[p], across, mine)

    def finish_all():
        for g in range(2):
            to_state(g).wait_recv()
        for p in range(2):

            @pl.loop(p * half, (p + 1) * half)
            def _(h):
                finish(h)

            exchange(p).start()

    @pl.loop(0, services - 2)
    def _(j):
        @pl.when(j == moment)
        def _():
            turn()

        insides(j)

        @pl.when(j == jnp.maximum(moment, 2))
        def _():
            finish_all()

        serve(j)

    def route():
        expert = lax.broadcasted_iota(jnp.int32, (n, rows), 0)
        first = ids_ref[0:1, :] == expert
        second = ids_ref[1:2, :] == expert
        raw = route_ref[...].astype(f32)
        shares = raw / (raw[0:1, :] + raw[1:2, :])
        weight = jnp.where(first, shares[0:1, :], 0.0) + jnp.where(second, shares[1:2, :], 0.0)
        named = first | second
        earlier = (
            lax.broadcasted_iota(jnp.int32, (rows, rows), 0)
            < lax.broadcasted_iota(jnp.int32, (rows, rows), 1)
        ).astype(f32)
        count = jnp.dot(
            jnp.where(named, 1.0, 0.0).astype(bf16), earlier.astype(bf16), preferred_element_type=f32
        )
        rank = jnp.where(named, count, -1.0)
        for e in range(n):
            rank_row[e] = jnp.broadcast_to(rank[e : e + 1, :], (8, rows))
        rank_col[...] = rank.T
        weight_col[...] = weight.T

    def mask_of(s):
        return 4 * lax.div(s, 2) + lax.rem(s, 2)

    def block_of(s):
        return flip(me, mask_of(s), n)

    def owner_of(s):
        head = lax.div(block_of(s), group)
        return lax.div(head, 2), lax.rem(head, 2)

    def to_core(s, c, u):
        at = s * strips + c
        return remote(
            mixed.at[u, at],
            beside_core.at[u, at],
            k_s.at[u, at],
            k_r.at[u, at],
            me,
            chip * 2 + 1 - core,
        )

    def to_owner(s, c, u, to, rel):
        at = s * strips + c
        return remote(
            mixed.at[u, at], parts.at[u, at, rel], r_s.at[u, at], r_r.at[u, at, rel], me, to
        )

    def project(s, some_strips, u):
        deep = wall.shape[2] // 2
        value = 0.0
        for p in range(2):
            block = [wall[s, c, p * deep : (p + 1) * deep] for c in some_strips]
            value += jnp.dot(
                headed[2 * u + p], jnp.concatenate(block, axis=1), preferred_element_type=f32
            )
        for i, c in enumerate(some_strips):
            tile = value[:, i * width : (i + 1) * width]
            acc[u, s * strips + c] = tile
            mixed[u, s * strips + c] = tile.astype(bf16)

    def send(s, some_strips, u):
        @pl.when(owner_of(s)[1] != core)
        def _():
            for c in some_strips:
                to_core(s, c, u).start()

    def presum(s, some_strips, u):
        owner_chip, owner_core = owner_of(s)

        @pl.when(owner_core == core)
        def _():
            for c in some_strips:
                at = s * strips + c
                to_core(s, c, u).wait_recv()
                value = acc[u, at] + beside_core[u, at].astype(f32)
                acc[u, at] = value
                mixed[u, at] = value.astype(bf16)

            @pl.when(owner_chip != chip)
            def _():
                rel = lax.rem(chip - owner_chip + chips, chips)
                for c in some_strips:
                    to_owner(s, c, u, owner_chip * 2 + core, rel).start()

    def work(low, high, step, first, last, u):
        some_strips = list(range(first, last))
        if not some_strips:
            return
        count = (high - low) // step
        for body in (project, send, presum):

            @pl.loop(0, count, unroll=count <= 4)
            def _(i):
                body(low + i * step, some_strips, u)

    def passed(k):
        @pl.loop(1, slots // 2)
        def _(q):
            pass_far(q, k).wait_recv()

    for k in range(pieces):
        to_beside(k).wait_recv()
    work(0, 2, 1, 0, strips, 0)
    work(2, slots, 2, 0, strips - 1, 0)
    route()
    serve(services - 2)
    for k in range(pieces - 2):
        passed(k)
    work(3, slots + 1, 2, 0, strips - 1, 0)
    serve(services - 1)
    for p in range(2):
        exchange(p).wait_recv()
    work(0, slots, 1, 0, strips - 1, 1)
    work(2, slots, 2, strips - 1, strips, 1)
    work(0, 2, 1, strips - 1, strips, 1)
    passed(pieces - 2)
    passed(pieces - 1)
    work(3, slots + 1, 2, strips - 1, strips, 1)
    work(2, slots, 1, strips - 1, strips, 0)

    def summed(s, c, u):
        value = acc[u, s * strips + c]
        for rel in range(1, chips):
            to_owner(s, c, u, mine, rel).wait_recv()
            value = value + parts[u, s * strips + c, rel].astype(f32)
        return value

    def cell(ref, b, c):
        if flat:
            return ref.at[:, pl.ds(pl.multiple_of(b * col + c * width, 128), width)]
        return ref.at[b]

    def hand_over(s, c):
        at = s * strips + c
        return remote(sum_out.at[at], sum_in.at[at], o_s.at[at], o_r.at[at], across, mine)

    def settle(block, c, value):
        b = block - group * mine
        total = value + cell(res_ref, b, c)[...].astype(f32)
        cell(hidden_ref, b, c)[...] = total
        squared[...] += total * total

    squared[...] = jnp.zeros_like(squared)

    def owned(first, last, body, seat_of=None):
        @pl.loop(0, slots)
        def _(s):
            block = block_of(s) if seat_of is None else flip(seat_of, mask_of(s), n)

            @pl.when(lax.div(block, group) == mine)
            def _():
                @pl.loop(first, last)
                def _(c):
                    body(block, s, c)

    def reduce_other(block, s, c):
        sum_out[s * strips + c] = summed(s, c, 1).astype(bf16)
        hand_over(s, c).start()

    def reduce_own(block, s, c):
        settle(block, c, summed(s, c, 0))

    def take(block, s, c):
        hand_over(s, c).wait_recv()
        settle(block, c, sum_in[s * strips + c].astype(f32))

    owned(0, strips - 1, reduce_other)
    owned(0, strips - 1, reduce_own)
    owned(strips - 1, strips, reduce_other)
    owned(strips - 1, strips, reduce_own)
    owned(0, strips, take, across)

    sq_own[...] = lax.dot_general(
        jnp.ones((8, width), f32),
        squared[...],
        (((1,), (1,)), ((), ())),
        precision=highest,
        preferred_element_type=f32,
    )

    def spread(j, to, slot):
        return remote(sq_own, sq_all.at[slot], q_s.at[j], q_r.at[j], me, to)

    for j in range(1, heads):
        spread(j, lax.rem(mine + j, heads), j).start()
    squares = sq_own[...]
    for j in range(1, heads):
        spread(j, mine, j).wait_recv()
        squares = squares + sq_all[j]
    scale = lax.rsqrt(squares / (col * n) + 1e-06).T[:, 0:1]
    if flat:
        normed_ref[...] = (hidden_ref[...] * scale * norm_ref[...][None, :]).astype(bf16)
    else:
        for p in range(group):
            normed_ref[p] = (hidden_ref[p] * scale * norm_ref[p]).astype(bf16)

    for j in range(1, heads):
        spread(j, mine, j).wait_send()
    for p in range(2):
        exchange(p).wait_send()
    for k in range(pieces):
        to_beside(k).wait_send()

    @pl.loop(0, services)
    def _(j):
        q, k = lax.div(j, pieces) + 1, lax.rem(j, pieces)
        to_far(q, k).wait_send()
        pass_far(q, k).wait_send()

    for g in range(2):
        to_peer(g).wait_send()
        to_state(g).wait_send()

    @pl.when(pair < n // 2 - 1)
    def _():
        for g in range(2):
            chain(g).wait_send()

    @pl.loop(0, slots)
    def _(s):
        owner_chip, owner_core = owner_of(s)
        relay = owner_core == core

        @pl.loop(0, strips)
        def _(c):
            @pl.when(jnp.logical_not(relay))
            def _():
                for u in range(2):
                    to_core(s, c, u).wait_send()

            @pl.when(relay & (owner_chip != chip))
            def _():
                for u in range(2):
                    to_owner(s, c, u, mine, 0).wait_send()

            @pl.when(relay & (owner_chip == chip))
            def _():
                hand_over(s, c).wait_send()


def attend(
    lengths, query, key, value, gain, weight, residual, norm_gain, ids, route, n, heads
):
    rows, feats = query.shape
    col, group, slots = weight.shape[1], n // heads, n // 2
    local, flat = feats // HEAD_DIM, col % 128 == 0
    strips = col // 128 if flat else 1
    width, depth = col // strips, weight.shape[0]
    dma = pltpu.SemaphoreType.DMA
    bf16, f32 = jnp.bfloat16, jnp.float32
    vmem = pl.BlockSpec(memory_space=pltpu.VMEM)
    if not flat:
        norm_gain = norm_gain.reshape(group, 1, col)
    shape = (rows, group * col) if flat else (group, rows, col)
    if not flat:
        residual = jnp.swapaxes(residual.reshape(rows, group, col), 0, 1)
    hidden, normed, *routing = pl.pallas_call(
        functools.partial(attend_kernel, n, heads, flat),
        out_shape=(
            jax.ShapeDtypeStruct(shape, f32),
            jax.ShapeDtypeStruct(shape, bf16),
            jax.ShapeDtypeStruct((n, 8, rows), f32),
            jax.ShapeDtypeStruct((rows, n), f32),
            jax.ShapeDtypeStruct((rows, n), f32),
        ),
        in_specs=[pl.BlockSpec(memory_space=pltpu.SMEM)]
        + [vmem] * 4
        + [pl.BlockSpec(memory_space=pl.ANY)]
        + [vmem] * 4,
        out_specs=(vmem,) * 5,
        scratch_shapes=[
            pltpu.VMEM((slots, strips, depth, width), bf16),
            pltpu.VMEM((rows, rows), f32),
            pltpu.VMEM((rows, HEAD_DIM), f32),
            pltpu.VMEM((rows, HEAD_DIM), f32),
            pltpu.VMEM((local // 2, HEAD_DIM, HEAD_DIM), f32),
        ]
        + [pltpu.VMEM((local // 2, HEAD_DIM, HEAD_DIM), bf16)] * 5
        + [
            pltpu.VMEM((local, HEAD_DIM, HEAD_DIM), bf16),
            pltpu.VMEM((rows, feats), f32),
            pltpu.VMEM((4, rows, feats // 2), bf16),
            pltpu.VMEM((2, slots * strips, rows, width), f32),
            pltpu.VMEM((2, slots * strips, rows, width), bf16),
            pltpu.VMEM((2, slots * strips, rows, width), bf16),
            pltpu.VMEM((2, slots * strips, heads // 2, rows, width), bf16),
            pltpu.VMEM((slots * strips, rows, width), bf16),
            pltpu.VMEM((slots * strips, rows, width), bf16),
            pltpu.VMEM((rows, width), f32),
            pltpu.VMEM((8, rows), f32),
            pltpu.VMEM((heads, 8, rows), f32),
            dma((strips,)),
        ]
        + [dma((2 * strips,))] * 2
        + [dma((slots // 2, 2 * strips))] * 4
        + [dma((2,))] * 8
        + [dma((2, slots * strips))] * 3
        + [
            dma((2, slots * strips, heads // 2)),
            dma((slots * strips,)),
            dma((slots * strips,)),
            dma((heads,)),
            dma((heads,)),
        ],
        compiler_params=pltpu.CompilerParams(
            collective_id=2, has_side_effects=True, vmem_limit_bytes=60 * 1024 * 1024
        ),
        name="attend",
    )(lengths, query, key, value, gain, weight, residual, norm_gain, ids, route)
    if not flat:
        hidden, normed = (jnp.swapaxes(a, 0, 1).reshape(rows, -1) for a in (hidden, normed))
    return hidden, normed, *routing


def on_device(
    query,
    key,
    value,
    episode_lengths,
    attn_gain,
    out_weight,
    residual,
    norm_gain,
    expert_ids,
    route_weights,
    gate_weight,
    up_weight,
    down_weight,
):
    n, heads = lax.axis_size("ctx"), lax.axis_size("head")
    tokens = attend(
        episode_lengths,
        query,
        key,
        value,
        attn_gain[None, :],
        out_weight,
        residual,
        norm_gain,
        expert_ids.T,
        route_weights.T,
        n,
        heads,
    )
    return experts(*tokens, gate_weight[0], up_weight[0], down_weight[0], n, heads)


def solution(mesh):
    placed = (
        P("ctx", "head"),
        P("ctx", "head"),
        P("ctx", "head"),
        P(),
        P("head"),
        P("head", "ctx"),
        P("ctx", "head"),
        P("head"),
        P("ctx", None),
        P("ctx", None),
        P("ctx", None, "head"),
        P("ctx", None, "head"),
        P("ctx", "head", None),
    )
    return jax.shard_map(
        on_device, mesh=mesh, in_specs=placed, out_specs=P("ctx", "head"), check_vma=False
    )
```
